32 devices in a mesh: dp: 4 (over z), ctx: 8 (over y, x, core).
Axes of the slice: x: 2, y: 2, z: 4, core: 2. Of those that a mesh axis runs over, the one named last changes fastest.
Arguments:
- tokens: bfloat16 [4096, 1152], P(('dp', 'ctx')), may hold values from -6 to 6
- in_gain: bfloat16 [1152], P('dp'), may hold values from 0.099609375 to 1.8984375
- query_weight: bfloat16 [1152, 1024], P('dp'), may hold values from -0.1875 to 0.1875
- key_weight: bfloat16 [1152, 256], P('dp'), may hold values from -0.1875 to 0.1875
- value_weight: bfloat16 [1152, 256], P('dp'), may hold values from -0.1875 to 0.1875
- query_gain: bfloat16 [256], P('dp'), may hold values from 0.099609375 to 1.8984375
- key_gain: bfloat16 [256], P('dp'), may hold values from 0.099609375 to 1.8984375
- out_weight: bfloat16 [1024, 1152], P('dp'), may hold values from -0.75 to 0.75
- attn_post_gain: bfloat16 [1152], P('dp'), may hold values from 0.099609375 to 1.8984375
- ffn_pre_gain: bfloat16 [1152], P('dp'), may hold values from 0.099609375 to 1.8984375
- gate_weight: bfloat16 [1152, 6912], P('dp', 'ctx'), may hold values from -0.1875 to 0.1875
- up_weight: bfloat16 [1152, 6912], P('dp', 'ctx'), may hold values from -0.1875 to 0.1875
- down_weight: bfloat16 [1152, 6912], P('dp', 'ctx'), may hold values from -0.078125 to 0.078125
- ffn_post_gain: bfloat16 [1152], P('dp'), may hold values from 0.099609375 to 1.8984375
- cotangent: bfloat16 [4096, 1152], P(('dp', 'ctx')), may hold values from -6 to 6
Outputs:
- block_out: bfloat16 [4096, 1152], P(('dp', 'ctx'))
- input_grad: float32 [4096, 1152], P(('dp', 'ctx'))
- in_gain_grad: float32 [1152], P('dp')
- query_weight_grad: float32 [1152, 1024], P('dp')
- key_weight_grad: float32 [1152, 256], P('dp')
- value_weight_grad: float32 [1152, 256], P('dp')
- query_gain_grad: float32 [256], P('dp')
- key_gain_grad: float32 [256], P('dp')
- out_weight_grad: float32 [1024, 1152], P('dp')
- attn_post_gain_grad: float32 [1152], P('dp')
- ffn_pre_gain_grad: float32 [1152], P('dp')
- gate_weight_grad: float32 [1152, 6912], P('dp', 'ctx')
- up_weight_grad: float32 [1152, 6912], P('dp', 'ctx')
- down_weight_grad: float32 [1152, 6912], P('dp', 'ctx')
- ffn_post_gain_grad: float32 [1152], P('dp')
The draws below stay inside these ranges and needn't reach their ends.
All inputs are finite; a program needn't handle non-finite values.
Results may differ from the reference program's by a relative error of at most 0.017.
Values may be sent and summed in bfloat16 or wider, within the bound.
A program may use at most 128 MiB of HBM per device.

```python
import math
import jax
import jax.numpy as jnp
from jax import lax

D = 1152
HEADS = 4
HEAD = 256
FF = 6912
QWIDTH = 1024
LENGTH = 1024
SEQS = 4
TOKENS = 4096


def steps_of(stream_key, extent, pieces, least, high):
    level, own = 1.0, jax.random.fold_in(stream_key, 6)
    for position, parts in pieces:
        draws = jnp.exp(jax.random.uniform(jax.random.fold_in(own, position), (parts,), jnp.float32, least / len(pieces), high / len(pieces)))
        level = level * jnp.repeat(draws, extent[position] // parts).reshape([-1 if axis == position else 1 for axis in range(len(extent))])
    return level


def normal_values(rng, extent, spread, bound, split=(), held_as=jnp.bfloat16):
    array = spread * jax.random.normal(rng, extent, jnp.float32)
    if split:
        array = array * steps_of(rng, extent, split, -0.22, 0.18)
    return jnp.clip(array, -bound, bound).astype(held_as)


def setup_inputs(seed: int = 0) -> dict:
    key_of = jax.random.split(jax.random.key(seed), 16)
    tokens = normal_values(key_of[0], (TOKENS, D), 1.0, 6.0, ((0, 32),))
    in_gain = jnp.clip(1.0 + 0.18 * jax.random.normal(key_of[1], (D,), jnp.float32), 0.099609375, 1.8984375).astype(jnp.bfloat16)
    query_weight = normal_values(key_of[2], (D, QWIDTH), D ** -0.5, 0.1875, ((0, 4),))
    key_weight = normal_values(key_of[3], (D, HEAD), D ** -0.5, 0.1875, ((0, 4),))
    value_weight = normal_values(key_of[4], (D, HEAD), D ** -0.5, 0.1875, ((0, 4),))
    query_gain = jnp.clip(1.0 + 0.18 * jax.random.normal(key_of[5], (HEAD,), jnp.float32), 0.099609375, 1.8984375).astype(jnp.bfloat16)
    key_gain = jnp.clip(1.0 + 0.18 * jax.random.normal(key_of[6], (HEAD,), jnp.float32), 0.099609375, 1.8984375).astype(jnp.bfloat16)
    out_weight = normal_values(key_of[7], (QWIDTH, D), (QWIDTH // 16) ** -0.5, 0.75, ((0, 4),))
    attn_post_gain = jnp.clip(1.0 + 0.18 * jax.random.normal(key_of[8], (D,), jnp.float32), 0.099609375, 1.8984375).astype(jnp.bfloat16)
    ffn_pre_gain = jnp.clip(1.0 + 0.18 * jax.random.normal(key_of[9], (D,), jnp.float32), 0.099609375, 1.8984375).astype(jnp.bfloat16)
    gate_weight = normal_values(key_of[10], (D, FF), D ** -0.5, 0.1875, ((0, 4), (1, 8)))
    up_weight = normal_values(key_of[11], (D, FF), D ** -0.5, 0.1875, ((0, 4), (1, 8)))
    down_weight = normal_values(key_of[12], (D, FF), FF ** -0.5, 0.078125, ((0, 4), (1, 8)))
    ffn_post_gain = jnp.clip(1.0 + 0.18 * jax.random.normal(key_of[13], (D,), jnp.float32), 0.099609375, 1.8984375).astype(jnp.bfloat16)
    cotangent = normal_values(key_of[14], (TOKENS, D), 1.0, 6.0, ((0, 32),))
    return dict(tokens=tokens, in_gain=in_gain, query_weight=query_weight, key_weight=key_weight, value_weight=value_weight, query_gain=query_gain, key_gain=key_gain, out_weight=out_weight, attn_post_gain=attn_post_gain, ffn_pre_gain=ffn_pre_gain, gate_weight=gate_weight, up_weight=up_weight, down_weight=down_weight, ffn_post_gain=ffn_post_gain, cotangent=cotangent)


EPS = 1e-06
GELU_C = math.sqrt(2.0 / math.pi)
NEG_FILL = -1e+30

def inverse_rms(values):
    return lax.rsqrt(lax.optimization_barrier(jnp.mean(values * values, axis=-1, keepdims=True)) + EPS)

def norm_back(values, scale_inv, gain, grad_out):
    weighted = grad_out * gain
    cubed = scale_inv * scale_inv * scale_inv
    return scale_inv * weighted - values * cubed * lax.optimization_barrier(jnp.mean(weighted * values, axis=-1, keepdims=True))

def gelu_pair(values):
    inner = GELU_C * (values + 0.044715 * values * values * values)
    tanh_val = jnp.tanh(inner)
    result = 0.5 * values * (1.0 + tanh_val)
    slope = 0.5 * (1.0 + tanh_val) + 0.5 * values * (1.0 - tanh_val * tanh_val) * GELU_C * (1.0 + 3.0 * 0.044715 * values * values)
    return (result, slope)

def rotate(values, cosine, sine):
    middle = values.shape[-1] // 2
    first = values[..., :middle]
    second = values[..., middle:]
    return jnp.concatenate([first * cosine - second * sine, second * cosine + first * sine], axis=-1)

def unrotate(grads, cosine, sine):
    middle = grads.shape[-1] // 2
    first = grads[..., :middle]
    second = grads[..., middle:]
    return jnp.concatenate([first * cosine + second * sine, second * cosine - first * sine], axis=-1)

def rope_tables(positions):
    middle = HEAD // 2
    freqs = jnp.exp(-(2.0 * jnp.arange(middle, dtype=jnp.float32) / HEAD) * math.log(1000000.0))
    angles = positions[:, None] * freqs[None, :]
    return (jnp.cos(angles), jnp.sin(angles))

def rounded(values):
    return lax.optimization_barrier(values.astype(jnp.bfloat16)).astype(jnp.float32)

def matmul(left, right):
    return jnp.dot(left, right, preferred_element_type=jnp.float32)

def matmul_tn(left, right):
    return lax.dot_general(left, right, (((0,), (0,)), ((), ())), preferred_element_type=jnp.float32)

def matmul_nt(left, right):
    return lax.dot_general(left, right, (((1,), (1,)), ((), ())), preferred_element_type=jnp.float32)

def reference(tokens, in_gain, query_weight, key_weight, value_weight, query_gain, key_gain, out_weight, attn_post_gain, ffn_pre_gain, gate_weight, up_weight, down_weight, ffn_post_gain, cotangent):
    positions = jnp.arange(LENGTH, dtype=jnp.float32)
    cosine, sine = rope_tables(positions)
    scaling = 1.0 / math.sqrt(HEAD)
    row_index = jnp.arange(LENGTH, dtype=jnp.int32)
    causal = (row_index[:, None] >= row_index[None, :])[None]
    gain_in = in_gain.astype(jnp.float32)
    gain_query = query_gain.astype(jnp.float32)
    gain_key = key_gain.astype(jnp.float32)
    gain_attn = attn_post_gain.astype(jnp.float32)
    gain_pre = ffn_pre_gain.astype(jnp.float32)
    gain_post = ffn_post_gain.astype(jnp.float32)

    def one_sequence(totals, inputs):
        seq_tokens, seq_cot = inputs
        inputs_f = seq_tokens.astype(jnp.float32)
        inv_one = inverse_rms(inputs_f)
        normed_one = (inputs_f * inv_one * gain_in).astype(jnp.bfloat16)
        queries = matmul(normed_one, query_weight).reshape(LENGTH, HEADS, HEAD)
        keys = matmul(normed_one, key_weight)
        values = matmul(normed_one, value_weight).astype(jnp.bfloat16)
        inv_query = inverse_rms(queries)
        inv_key = inverse_rms(keys)
        query_rot = (rotate(queries * inv_query * gain_query, cosine[:, None, :], sine[:, None, :]) * scaling).astype(jnp.bfloat16)
        key_rot = rotate(keys * inv_key * gain_key, cosine, sine).astype(jnp.bfloat16)
        scores = jnp.einsum('qhd,kd->hqk', query_rot.astype(jnp.float32), key_rot.astype(jnp.float32))
        scores = jnp.where(causal, scores, NEG_FILL)
        row_max = lax.optimization_barrier(jnp.max(scores, axis=-1, keepdims=True))
        weights = jnp.where(causal, jnp.exp(scores - row_max), 0.0)
        total = lax.optimization_barrier(jnp.sum(weights, axis=-1, keepdims=True))
        log_total = row_max + jnp.log(total)
        summed = jnp.einsum('hqk,kd->hqd', rounded(weights), values.astype(jnp.float32))
        attn_heads = jnp.transpose(summed / total, (1, 0, 2)).astype(jnp.bfloat16)
        attn_out = attn_heads.reshape(LENGTH, HEADS * HEAD)
        projected = matmul(attn_out, out_weight)
        inv_proj = inverse_rms(projected)
        residual = inputs_f + projected * inv_proj * gain_attn
        inv_two = inverse_rms(residual)
        normed_two = (residual * inv_two * gain_pre).astype(jnp.bfloat16)
        gate = matmul(normed_two, gate_weight)
        upper = matmul(normed_two, up_weight)
        gelu_val, gelu_der = gelu_pair(gate)
        hidden = (gelu_val * upper).astype(jnp.bfloat16)
        ffn_sum = matmul_nt(hidden, down_weight)
        inv_ffn = inverse_rms(ffn_sum)
        block_out = (residual + ffn_sum * inv_ffn * gain_post).astype(jnp.bfloat16)
        cot = seq_cot.astype(jnp.float32)
        grad_post = lax.optimization_barrier(jnp.sum(cot * ffn_sum * inv_ffn, axis=0))
        ffn_sum_grad = norm_back(ffn_sum, inv_ffn, gain_post, cot).astype(jnp.bfloat16)
        hidden_grad = matmul(ffn_sum_grad, down_weight)
        grad_down = matmul_tn(ffn_sum_grad, hidden)
        gate_grad = (hidden_grad * upper * gelu_der).astype(jnp.bfloat16)
        up_grad = (hidden_grad * gelu_val).astype(jnp.bfloat16)
        grad_gate = matmul_tn(normed_two, gate_grad)
        grad_up = matmul_tn(normed_two, up_grad)
        normed_two_grad = matmul_nt(gate_grad, gate_weight) + matmul_nt(up_grad, up_weight)
        grad_pre = lax.optimization_barrier(jnp.sum(normed_two_grad * residual * inv_two, axis=0))
        residual_grad = cot + norm_back(residual, inv_two, gain_pre, normed_two_grad)
        grad_attn = lax.optimization_barrier(jnp.sum(residual_grad * projected * inv_proj, axis=0))
        projected_grad = norm_back(projected, inv_proj, gain_attn, residual_grad).astype(jnp.bfloat16)
        grad_out = matmul_tn(attn_out, projected_grad)
        attn_out_grad = matmul_nt(projected_grad, out_weight).astype(jnp.bfloat16).reshape(LENGTH, HEADS, HEAD)
        delta = lax.optimization_barrier(jnp.sum(attn_out_grad.astype(jnp.float32) * attn_heads.astype(jnp.float32), axis=-1))
        delta = jnp.transpose(delta, (1, 0))[:, :, None]
        probs = jnp.where(causal, jnp.exp(scores - log_total), 0.0)
        prob_grad = jnp.einsum('qhd,kd->hqk', attn_out_grad.astype(jnp.float32), values.astype(jnp.float32))
        score_grad = rounded(probs * (prob_grad - delta))
        values_grad = jnp.einsum('hqk,qhd->kd', rounded(probs), attn_out_grad.astype(jnp.float32))
        key_rot_grad = jnp.einsum('hqk,qhd->kd', score_grad, query_rot.astype(jnp.float32))
        query_rot_grad = jnp.einsum('hqk,kd->qhd', score_grad, key_rot.astype(jnp.float32))
        query_normed_grad = unrotate(query_rot_grad * scaling, cosine[:, None, :], sine[:, None, :])
        grad_qgain = lax.optimization_barrier(jnp.sum(query_normed_grad * queries * inv_query, axis=(0, 1)))
        query_grad = norm_back(queries, inv_query, gain_query, query_normed_grad).reshape(LENGTH, HEADS * HEAD).astype(jnp.bfloat16)
        key_normed_grad = unrotate(key_rot_grad, cosine, sine)
        grad_kgain = lax.optimization_barrier(jnp.sum(key_normed_grad * keys * inv_key, axis=0))
        key_grad = norm_back(keys, inv_key, gain_key, key_normed_grad).astype(jnp.bfloat16)
        value_grad = values_grad.astype(jnp.bfloat16)
        grad_query = matmul_tn(normed_one, query_grad)
        grad_key = matmul_tn(normed_one, key_grad)
        grad_value = matmul_tn(normed_one, value_grad)
        normed_one_grad = matmul_nt(query_grad, query_weight) + matmul_nt(key_grad, key_weight) + matmul_nt(value_grad, value_weight)
        grad_in = lax.optimization_barrier(jnp.sum(normed_one_grad * inputs_f * inv_one, axis=0))
        input_grad = residual_grad + norm_back(inputs_f, inv_one, gain_in, normed_one_grad)
        updates = (grad_in, grad_query, grad_key, grad_value, grad_qgain, grad_kgain, grad_out, grad_attn, grad_pre, grad_gate, grad_up, grad_down, grad_post)
        new_totals = tuple((old + new for old, new in zip(totals, updates)))
        return (new_totals, (block_out, input_grad))
    shapes = (in_gain, query_weight, key_weight, value_weight, query_gain, key_gain, out_weight, attn_post_gain, ffn_pre_gain, gate_weight, up_weight, down_weight, ffn_post_gain)
    initial = tuple((jnp.zeros(item.shape, jnp.float32) for item in shapes))
    seq_inputs = (tokens.reshape(SEQS, LENGTH, D), cotangent.reshape(SEQS, LENGTH, D))
    totals, (outputs, input_grads) = lax.scan(one_sequence, initial, seq_inputs)
    return (outputs.reshape(TOKENS, D), input_grads.reshape(TOKENS, D), totals[0], totals[1], totals[2], totals[3], totals[4], totals[5], totals[6], totals[7], totals[8], totals[9], totals[10], totals[11], totals[12])
```

```python
import functools
import math

import jax
import jax.numpy as jnp
from jax import lax
from jax.experimental import pallas as pl
from jax.experimental.pallas import tpu as pltpu
from jax.sharding import PartitionSpec as P

HEADS = 4
HEAD = 256


EPS = 1e-06
GELU_C = math.sqrt(2.0 / math.pi)
NEG_FILL = -1e30


def inverse_rms(values):
    return lax.rsqrt(jnp.mean(values * values, axis=-1, keepdims=True) + EPS)


def norm_back(values, scale_inv, gain, grad_out):
    weighted = grad_out * gain
    cubed = scale_inv * scale_inv * scale_inv
    return scale_inv * weighted - values * cubed * jnp.mean(
        weighted * values, axis=-1, keepdims=True
    )


def gelu_pair(values):
    inner = GELU_C * (values + 0.044715 * values * values * values)
    tanh_val = jnp.tanh(inner)
    result = 0.5 * values * (1.0 + tanh_val)
    slope = 0.5 * (1.0 + tanh_val) + 0.5 * values * (1.0 - tanh_val * tanh_val) * GELU_C * (
        1.0 + 3.0 * 0.044715 * values * values
    )
    return (result, slope)


def rotate(values, cosine, sine):
    middle = values.shape[-1] // 2
    first = values[..., :middle]
    second = values[..., middle:]
    return jnp.concatenate(
        [first * cosine - second * sine, second * cosine + first * sine], axis=-1
    )


def unrotate(grads, cosine, sine):
    middle = grads.shape[-1] // 2
    first = grads[..., :middle]
    second = grads[..., middle:]
    return jnp.concatenate(
        [first * cosine + second * sine, second * cosine - first * sine], axis=-1
    )


def rope_tables(positions):
    middle = HEAD // 2
    freqs = jnp.exp(-(2.0 * jnp.arange(middle, dtype=jnp.float32) / HEAD) * math.log(1000000.0))
    angles = positions[:, None] * freqs[None, :]
    return (jnp.cos(angles), jnp.sin(angles))


def matmul(left, right):
    return jnp.dot(left, right, preferred_element_type=jnp.float32)


def matmul_tn(left, right):
    return lax.dot_general(
        left, right, (((0,), (0,)), ((), ())), preferred_element_type=jnp.float32
    )


def matmul_nt(left, right):
    return lax.dot_general(
        left, right, (((1,), (1,)), ((), ())), preferred_element_type=jnp.float32
    )


MESH = pl.DeviceIdType.MESH


def swap_kernel(size, axis, kinds, *refs):
    count = len(kinds)
    ins, outs, kept = refs[:count], refs[count : 2 * count], refs[2 * count : 3 * count]
    send, recv, local = refs[3 * count :]
    me = lax.axis_index(axis)
    own = []
    for item, kind in enumerate(kinds):
        source = ins[item].at[me] if kind == "swap" else ins[item]
        own.append(pltpu.make_async_copy(source, kept[item], local.at[item, 0]))
        own[-1].start()
    barrier = pltpu.get_barrier_semaphore()
    for step in range(1, size):
        peer = lax.rem(me + step, size)
        pl.semaphore_signal(barrier, inc=1, device_id={axis: peer}, device_id_type=MESH)
    pl.semaphore_wait(barrier, size - 1)
    copies = []
    for item, kind in enumerate(kinds):
        for step in range(1, size):
            peer = lax.rem(me + step, size)
            source = ins[item].at[peer] if kind == "swap" else ins[item]
            copy = pltpu.make_async_remote_copy(
                src_ref=source,
                dst_ref=outs[item].at[me],
                send_sem=send.at[item, step - 1],
                recv_sem=recv.at[item, step - 1],
                device_id={axis: peer},
                device_id_type=MESH,
            )
            copy.start()
            copies.append(copy)
    for item in range(count):
        own[item].wait()
        copy = pltpu.make_async_copy(kept[item], outs[item].at[me], local.at[item, 1])
        copy.start()
        copies.append(copy)
    for copy in copies:
        copy.wait()


def chunks_of(rows):
    for parts in (4, 3, 2):
        if rows % (16 * parts) == 0:
            return parts
    return 1


def pair_gather_kernel(size, axis, kinds, *refs):
    count = len(kinds)
    ins, outs, kept = refs[:count], refs[count : 2 * count], refs[2 * count : 3 * count]
    send, recv, pass_send, pass_recv, local = refs[3 * count :]
    me = lax.axis_index(axis)
    twin = me + 1 - 2 * lax.rem(me, 2)
    half = size // 2
    own = []
    for item in range(count):
        own.append(pltpu.make_async_copy(ins[item], kept[item], local.at[item, 0]))
        own[-1].start()
    barrier = pltpu.get_barrier_semaphore()
    for step in range(1, half):
        peer = lax.rem(me + 2 * step, size)
        pl.semaphore_signal(barrier, inc=1, device_id={axis: peer}, device_id_type=MESH)
    pl.semaphore_signal(barrier, inc=1, device_id={axis: twin}, device_id_type=MESH)
    pl.semaphore_wait(barrier, half)
    pieces = []
    for item in range(count):
        rows = ins[item].shape[0]
        pieces += [
            (item, part, pl.ds(part * (rows // chunks_of(rows)), rows // chunks_of(rows)))
            for part in range(chunks_of(rows))
        ]
    across, last = [], []
    for item, part, span in pieces:
        for step in range(1, half):
            copy = pltpu.make_async_remote_copy(
                src_ref=ins[item].at[span],
                dst_ref=outs[item].at[me, span],
                send_sem=send.at[item, step, part],
                recv_sem=recv.at[item, step, part],
                device_id={axis: lax.rem(me + 2 * step, size)},
                device_id_type=MESH,
            )
            copy.start()
            across.append((copy, item, step, part, span))
    for item, part, span in pieces:
        copy = pltpu.make_async_remote_copy(
            src_ref=ins[item].at[span],
            dst_ref=outs[item].at[me, span],
            send_sem=pass_send.at[item, 0, part],
            recv_sem=pass_recv.at[item, 0, part],
            device_id={axis: twin},
            device_id_type=MESH,
        )
        copy.start()
        last.append(copy)
    for item in range(count):
        own[item].wait()
        copy = pltpu.make_async_copy(kept[item], outs[item].at[me], local.at[item, 1])
        copy.start()
        last.append(copy)
    for arrived, item, step, part, span in across:
        arrived.wait_recv()
        origin = lax.rem(me + size - 2 * step, size)
        copy = pltpu.make_async_remote_copy(
            src_ref=outs[item].at[origin, span],
            dst_ref=outs[item].at[origin, span],
            send_sem=pass_send.at[item, step, part],
            recv_sem=pass_recv.at[item, step, part],
            device_id={axis: twin},
            device_id_type=MESH,
        )
        copy.start()
        last.append(copy)
    for sent, *_ in across:
        sent.wait_send()
    for copy in last:
        copy.wait()


def exchange(arrays, kinds, axis, size, ident):
    count = len(arrays)
    pairs = all(kind == "gather" for kind in kinds) and axis == "ctx" and size % 2 == 0
    shapes = tuple(
        jax.ShapeDtypeStruct(x.shape if kind == "swap" else (size,) + x.shape, x.dtype)
        for x, kind in zip(arrays, kinds)
    )
    dma = pltpu.SemaphoreType.DMA
    if pairs:
        half = size // 2
        parts = max(chunks_of(x.shape[0]) for x in arrays)
        scratch = [dma((count, half, parts))] * 4
        body = pair_gather_kernel
    else:
        scratch = [dma((count, size - 1))] * 2
        body = swap_kernel
    moved = sum(x.size * x.dtype.itemsize for x in shapes)
    return pl.pallas_call(
        functools.partial(body, size, axis, tuple(kinds)),
        out_shape=shapes,
        in_specs=[pl.BlockSpec(memory_space=pl.ANY)] * count,
        out_specs=tuple(pl.BlockSpec(memory_space=pl.ANY) for _ in arrays),
        scratch_shapes=[pltpu.VMEM(x.shape[1:], x.dtype) for x in shapes]
        + scratch
        + [dma((count, 2))],
        compiler_params=pltpu.CompilerParams(collective_id=ident, has_side_effects=True),
        cost_estimate=pl.CostEstimate(flops=0, bytes_accessed=20 * moved, transcendentals=0),
        name=f"exchange_{ident}",
    )(*arrays)


def pieces_of(rows):
    parts = chunks_of(rows)
    return [pl.ds(part * (rows // parts), rows // parts) for part in range(parts)]


def remote(source, target, send, recv, axis, peer):
    copy = pltpu.make_async_remote_copy(
        src_ref=source,
        dst_ref=target,
        send_sem=send,
        recv_sem=recv,
        device_id={axis: peer},
        device_id_type=MESH,
    )
    copy.start()
    return copy


class Place:
    def __init__(self, axis, size):
        self.axis, self.size, self.half = axis, size, size // 2
        self.me = lax.axis_index(axis)
        self.core = lax.rem(self.me, 2)
        self.twin = self.me + 1 - 2 * self.core

    def across(self, step):
        return lax.rem(self.me + 2 * step, self.size)

    def behind(self, step):
        return lax.rem(self.me + self.size - 2 * step, self.size)

    def greet_pairs(self):
        barrier = pltpu.get_barrier_semaphore()
        for step in range(1, self.half):
            pl.semaphore_signal(
                barrier, inc=1, device_id={self.axis: self.across(step)}, device_id_type=MESH
            )
        pl.semaphore_signal(barrier, inc=1, device_id={self.axis: self.twin}, device_id_type=MESH)
        pl.semaphore_wait(barrier, self.half)

    def greet_all(self):
        barrier = pltpu.get_barrier_semaphore()
        for step in range(1, self.size):
            peer = lax.rem(self.me + step, self.size)
            pl.semaphore_signal(barrier, inc=1, device_id={self.axis: peer}, device_id_type=MESH)
        pl.semaphore_wait(barrier, self.size - 1)


def scatter_scratch(size, rows, width):
    half, parts, dma = size // 2, chunks_of(rows), pltpu.SemaphoreType.DMA
    block = lambda count: pltpu.VMEM((count, rows, width), jnp.bfloat16)
    return [block(half), block(half), block(half - 1), block(half - 1), dma((half,))] + [
        dma((half, parts))
    ] * 4


class Scatter:
    def __init__(self, place, part, scratch):
        self.place, self.part = place, part
        self.kept, self.twins, self.summed, self.landed = scratch[:4]
        self.local, self.twin_send, self.twin_recv, self.send, self.recv = scratch[4:]
        self.spans = pieces_of(self.kept.shape[1])

    def load(self):
        place = self.place
        self.loads = []
        for slot in range(place.half):
            copy = pltpu.make_async_copy(
                self.part.at[place.across(slot)], self.kept.at[slot], self.local.at[slot]
            )
            copy.start()
            self.loads.append(copy)

    def start(self):
        place = self.place
        self.twin_copies, self.copies = {}, {}
        slots = list(range(1, place.half)) + [0]
        for index, span in enumerate(self.spans):
            for slot in slots:
                self.twin_copies[slot, index] = remote(
                    self.part.at[place.across(slot) + 1 - 2 * place.core, span],
                    self.twins.at[slot, span],
                    self.twin_send.at[slot, index],
                    self.twin_recv.at[slot, index],
                    place.axis,
                    place.twin,
                )
        for copy in self.loads:
            copy.wait()
        for index, span in enumerate(self.spans):
            for slot in slots[:-1]:
                self.twin_copies[slot, index].wait_recv()
                self.summed[slot - 1, span] = (
                    self.kept[slot, span].astype(jnp.float32)
                    + self.twins[slot, span].astype(jnp.float32)
                ).astype(jnp.bfloat16)
                self.copies[slot, index] = remote(
                    self.summed.at[slot - 1, span],
                    self.landed.at[slot - 1, span],
                    self.send.at[slot, index],
                    self.recv.at[slot, index],
                    place.axis,
                    place.across(slot),
                )

    def total(self, index):
        span = self.spans[index]
        self.twin_copies[0, index].wait_recv()
        value = self.kept[0, span].astype(jnp.float32) + self.twins[0, span].astype(jnp.float32)
        for slot in range(1, self.place.half):
            self.copies[slot, index].wait_recv()
            value = value + self.landed[slot - 1, span].astype(jnp.float32)
        return value

    def finish(self):
        for copy in list(self.twin_copies.values()) + list(self.copies.values()):
            copy.wait_send()


def gather_scratch(size, rows):
    dma = pltpu.SemaphoreType.DMA
    return [dma((size // 2, chunks_of(rows)))] * 4 + [dma((chunks_of(rows),))]


class Gather:
    def __init__(self, place, source, target, scratch):
        self.place, self.source, self.target = place, source, target
        self.send, self.recv, self.pass_send, self.pass_recv, self.local = scratch
        self.spans = pieces_of(source.shape[0])
        self.across, self.last = [], []

    def start(self, index):
        place, span = self.place, self.spans[index]
        for step in range(1, place.half):
            copy = remote(
                self.source.at[span],
                self.target.at[place.me, span],
                self.send.at[step, index],
                self.recv.at[step, index],
                place.axis,
                place.across(step),
            )
            self.across.append((copy, step, index))
        self.last.append(
            remote(
                self.source.at[span],
                self.target.at[place.me, span],
                self.pass_send.at[0, index],
                self.pass_recv.at[0, index],
                place.axis,
                place.twin,
            )
        )
        copy = pltpu.make_async_copy(
            self.source.at[span], self.target.at[place.me, span], self.local.at[index]
        )
        copy.start()
        self.last.append(copy)

    def relay(self):
        place = self.place
        for copy, step, index in self.across:
            copy.wait_recv()
            block = self.target.at[place.behind(step), self.spans[index]]
            self.last.append(
                remote(
                    block,
                    block,
                    self.pass_send.at[step, index],
                    self.pass_recv.at[step, index],
                    place.axis,
                    place.twin,
                )
            )

    def finish(self):
        for copy, *_ in self.across:
            copy.wait_send()
        for copy in self.last:
            copy.wait()


def ffn_turn_kernel(axis, size, part, residual, cot, gain, block_out, gain_grad, gathered, grad, *scratch):
    place = Place(axis, size)
    scatter = Scatter(place, part, scratch[:9])
    gather = Gather(place, grad, gathered, scratch[9:])
    scatter.load()
    place.greet_pairs()
    scatter.start()
    gain_row = gain[...]
    for index, span in enumerate(scatter.spans):
        ffn_sum = scatter.total(index)
        inverse = inverse_rms(ffn_sum)
        incoming = cot[span].astype(jnp.float32)
        grad[span] = norm_back(ffn_sum, inverse, gain_row, incoming).astype(jnp.bfloat16)
        gather.start(index)
        scaled = ffn_sum * inverse
        block_out[span] = (residual[span] + scaled * gain_row).astype(jnp.bfloat16)
        share = jnp.sum(incoming * scaled, axis=0, keepdims=True)
        gain_grad[...] = share if index == 0 else gain_grad[...] + share
    gather.relay()
    scatter.finish()
    gather.finish()


def ffn_turn(part, residual, cotangent, gain, axis, size, ident):
    rows, width = residual.shape
    whole = pl.BlockSpec(memory_space=pltpu.VMEM)
    away = pl.BlockSpec(memory_space=pl.ANY)
    return pl.pallas_call(
        functools.partial(ffn_turn_kernel, axis, size),
        out_shape=(
            jax.ShapeDtypeStruct((rows, width), jnp.bfloat16),
            jax.ShapeDtypeStruct((1, width), jnp.float32),
            jax.ShapeDtypeStruct((size, rows, width), jnp.bfloat16),
        ),
        in_specs=[away, whole, whole, whole],
        out_specs=(whole, whole, away),
        scratch_shapes=[pltpu.VMEM((rows, width), jnp.bfloat16)]
        + scatter_scratch(size, rows, width)
        + gather_scratch(size, rows),
        compiler_params=pltpu.CompilerParams(collective_id=ident, has_side_effects=True),
        cost_estimate=pl.CostEstimate(
            flops=0, bytes_accessed=20 * part.size * 2, transcendentals=0
        ),
        name=f"ffn_turn_{ident}",
    )(part, residual, cotangent, gain)


def attn_back_kernel(
    axis,
    size,
    part,
    residual,
    cot,
    projected,
    tokens,
    gains,
    head_gains,
    out_hbm,
    query_hbm,
    pair_hbm,
    attn_out,
    query_rot,
    key_hbm,
    value_hbm,
    queries,
    keys,
    cosine,
    sine,
    post_grad,
    input_grad,
    query_cols,
    pair_cols,
    proj_cols,
    all_gains,
    out_w,
    query_w,
    pair_w,
    key_all,
    value_all,
    res_grad,
    proj_grad,
    stacked_p,
    stacked_s,
    stacked_g,
    stacked_q,
    pair_part,
    query_grad,
    query_send,
    pair_send,
    proj_send,
    gain_send,
    local,
    send,
    recv,
    *scratch,
):
    rows, width = residual.shape
    total_keys = key_all.shape[0]
    bf16, f32 = jnp.bfloat16, jnp.float32
    scaling = 1.0 / math.sqrt(HEAD)
    place = Place(axis, size)
    me = place.me
    two = Scatter(place, part, scratch[:9])
    pairs = Scatter(place, pair_part, scratch[9:])
    two.load()
    loads = []
    for source, target in (
        (out_hbm, out_w),
        (key_hbm, key_all),
        (value_hbm, value_all),
        (query_hbm, query_w),
        (pair_hbm, pair_w),
    ):
        copy = pltpu.make_async_copy(source, target, local.at[len(loads)])
        copy.start()
        loads.append(copy)
    place.greet_all()
    two.start()
    swaps = []

    def swap(item, source, target):
        for step in range(1, size):
            peer = lax.rem(me + step, size)
            swaps.append(
                remote(
                    source.at[peer],
                    target.at[me],
                    send.at[item, step - 1],
                    recv.at[item, step - 1],
                    axis,
                    peer,
                )
            )
        copy = pltpu.make_async_copy(source.at[me], target.at[me], local.at[len(loads) + item])
        copy.start()
        swaps.append(copy)

    gain_in, gain_attn, gain_pre = gains[0:1], gains[1:2], gains[2:3]
    gain_query, gain_key = head_gains[0:1], head_gains[1:2]
    gain_send[...] = jnp.zeros_like(gain_send)
    gain_send[3:4] = post_grad[...]
    proj_width = width // size
    for index, span in enumerate(two.spans):
        two_grad = two.total(index)
        kept = residual[span]
        inv_two = inverse_rms(kept)
        back = cot[span].astype(f32) + norm_back(kept, inv_two, gain_pre, two_grad)
        res_grad[span] = back
        ahead = projected[span]
        inv_proj = inverse_rms(ahead)
        proj_back = norm_back(ahead, inv_proj, gain_attn, back)
        proj_grad[span] = proj_back.astype(bf16)
        for peer in range(size):
            proj_send[peer, span] = proj_back[:, peer * proj_width : (peer + 1) * proj_width].astype(
                bf16
            )
        gain_send[2:3] += jnp.sum(two_grad * kept * inv_two, axis=0, keepdims=True)
        gain_send[1:2] += jnp.sum(back * ahead * inv_proj, axis=0, keepdims=True)
    swap(0, proj_send, proj_cols)
    loads[0].wait()
    attn_grad = matmul_nt(proj_grad[...], out_w[...]).astype(bf16)
    loads[1].wait()
    loads[2].wait()
    query_pos = me * rows + lax.broadcasted_iota(jnp.int32, (rows, total_keys), 0)
    allowed = query_pos >= lax.broadcasted_iota(jnp.int32, (rows, total_keys), 1)
    for head in range(HEADS):
        lanes = slice(head * HEAD, (head + 1) * HEAD)
        level = pl.ds(head * rows, rows)
        query = query_rot[:, lanes]
        incoming = attn_grad[:, lanes]
        scores = jnp.where(allowed, matmul_nt(query, key_all[...]), NEG_FILL)
        weights = jnp.where(
            allowed, jnp.exp(scores - jnp.max(scores, axis=-1, keepdims=True)), 0.0
        )
        probs = weights / jnp.sum(weights, axis=-1, keepdims=True)
        delta = jnp.sum(
            incoming.astype(f32) * attn_out[:, lanes].astype(f32), axis=-1, keepdims=True
        )
        prob_grad = matmul_nt(incoming, value_all[...])
        stacked_s[level] = (probs * (prob_grad - delta)).astype(bf16)
        stacked_p[level] = probs.astype(bf16)
        stacked_g[level] = incoming
        stacked_q[level] = query
    values_part = matmul_tn(stacked_p[...], stacked_g[...]).astype(bf16)
    keys_part = matmul_tn(stacked_s[...], stacked_q[...]).astype(bf16)
    for peer in range(size):
        block = slice(peer * rows, (peer + 1) * rows)
        pair_part[peer, :, :HEAD] = keys_part[block]
        pair_part[peer, :, HEAD:] = values_part[block]
    pairs.load()
    pairs.start()
    query_width = HEADS * HEAD // size
    gain_share = jnp.zeros((1, HEAD), f32)
    for head in range(HEADS):
        lanes = slice(head * HEAD, (head + 1) * HEAD)
        level = pl.ds(head * rows, rows)
        normed_grad = unrotate(
            matmul(stacked_s[level], key_all[...]) * scaling, cosine[...], sine[...]
        )
        value = queries[:, lanes]
        inverse = inverse_rms(value)
        gain_share = gain_share + jnp.sum(normed_grad * value * inverse, axis=0, keepdims=True)
        query_grad[:, lanes] = norm_back(value, inverse, gain_query, normed_grad).astype(bf16)
    for peer in range(size):
        query_send[peer] = query_grad[:, peer * query_width : (peer + 1) * query_width]
    swap(1, query_send, query_cols)
    gain_send[4:5, :HEAD] = gain_share
    loads[3].wait()
    input_grad[...] = matmul_nt(query_grad[...], query_w[...])
    loads[4].wait()
    pair_width = 2 * HEAD // size
    key_share = jnp.zeros((1, HEAD), f32)
    for index, span in enumerate(pairs.spans):
        pair_total = pairs.total(index)
        normed_grad = unrotate(pair_total[:, :HEAD], cosine[span], sine[span])
        value = keys[span]
        inverse = inverse_rms(value)
        key_share = key_share + jnp.sum(normed_grad * value * inverse, axis=0, keepdims=True)
        both = jnp.concatenate(
            [norm_back(value, inverse, gain_key, normed_grad), pair_total[:, HEAD:]], axis=1
        )
        for peer in range(size):
            pair_send[peer, span] = both[:, peer * pair_width : (peer + 1) * pair_width].astype(bf16)
        one_grad = input_grad[span] + matmul_nt(both.astype(bf16), pair_w[...])
        inputs = tokens[span].astype(f32)
        inv_one = inverse_rms(inputs)
        gain_send[0:1] += jnp.sum(one_grad * inputs * inv_one, axis=0, keepdims=True)
        input_grad[span] = res_grad[span] + norm_back(inputs, inv_one, gain_in, one_grad)
    gain_send[5:6, :HEAD] = key_share
    swap(2, pair_send, pair_cols)
    for step in range(1, size):
        peer = lax.rem(me + step, size)
        swaps.append(
            remote(
                gain_send,
                all_gains.at[me],
                send.at[3, step - 1],
                recv.at[3, step - 1],
                axis,
                peer,
            )
        )
    copy = pltpu.make_async_copy(gain_send, all_gains.at[me], local.at[len(loads) + 3])
    copy.start()
    swaps.append(copy)
    two.finish()
    pairs.finish()
    for copy in swaps:
        copy.wait()


def attn_back(
    part,
    residual,
    cotangent,
    projected,
    tokens,
    gains,
    head_gains,
    out_full,
    query_full,
    pair_full,
    attn_out,
    query_rot,
    key_all,
    value_all,
    queries,
    keys,
    cosine,
    sine,
    post_grad,
    axis,
    size,
    ident,
):
    rows, width = residual.shape
    bf16, f32 = jnp.bfloat16, jnp.float32
    whole = pl.BlockSpec(memory_space=pltpu.VMEM)
    away = pl.BlockSpec(memory_space=pl.ANY)
    qwidth, total_keys = query_full.shape[1], key_all.shape[0]
    query_cols = (size, rows, qwidth // size)
    pair_cols = (size, rows, 2 * HEAD // size)
    proj_cols = (size, rows, width // size)
    dma = pltpu.SemaphoreType.DMA
    return pl.pallas_call(
        functools.partial(attn_back_kernel, axis, size),
        out_shape=(
            jax.ShapeDtypeStruct((rows, width), f32),
            jax.ShapeDtypeStruct(query_cols, bf16),
            jax.ShapeDtypeStruct(pair_cols, bf16),
            jax.ShapeDtypeStruct(proj_cols, bf16),
            jax.ShapeDtypeStruct((size, 8, width), f32),
        ),
        in_specs=[away]
        + [whole] * 6
        + [away] * 3
        + [whole] * 2
        + [away] * 2
        + [whole] * 5,
        out_specs=(whole, away, away, away, away),
        scratch_shapes=[
            pltpu.VMEM(out_full.shape, bf16),
            pltpu.VMEM(query_full.shape, bf16),
            pltpu.VMEM(pair_full.shape, bf16),
            pltpu.VMEM(key_all.shape, bf16),
            pltpu.VMEM(value_all.shape, bf16),
            pltpu.VMEM((rows, width), f32),
            pltpu.VMEM((rows, width), bf16),
            pltpu.VMEM((HEADS * rows, total_keys), bf16),
            pltpu.VMEM((HEADS * rows, total_keys), bf16),
            pltpu.VMEM((HEADS * rows, HEAD), bf16),
            pltpu.VMEM((HEADS * rows, HEAD), bf16),
            pltpu.VMEM((size, rows, 2 * HEAD), bf16),
            pltpu.VMEM((rows, qwidth), bf16),
            pltpu.VMEM(query_cols, bf16),
            pltpu.VMEM(pair_cols, bf16),
            pltpu.VMEM(proj_cols, bf16),
            pltpu.VMEM((8, width), f32),
            dma((9,)),
            dma((4, size - 1)),
            dma((4, size - 1)),
        ]
        + scatter_scratch(size, rows, width)
        + scatter_scratch(size, rows, 2 * HEAD),
        compiler_params=pltpu.CompilerParams(collective_id=ident, has_side_effects=True),
        cost_estimate=pl.CostEstimate(
            flops=0, bytes_accessed=30 * part.size * 2, transcendentals=0
        ),
        name=f"attn_back_{ident}",
    )(
        part,
        residual,
        cotangent,
        projected,
        tokens,
        gains,
        head_gains,
        out_full,
        query_full,
        pair_full,
        attn_out,
        query_rot,
        key_all,
        value_all,
        queries,
        keys,
        cosine,
        sine,
        post_grad,
    )


def by_columns(array, parts):
    rows, columns = array.shape
    return jnp.transpose(array.reshape(rows, parts, columns // parts), (1, 0, 2))


def from_columns(array):
    parts, rows, columns = array.shape
    return jnp.transpose(array, (1, 0, 2)).reshape(rows, parts * columns)


def sum_blocks(array):
    return jnp.sum(array.astype(jnp.float32), axis=0)


def on_device(
    dp,
    ctx,
    tokens,
    in_gain,
    query_weight,
    key_weight,
    value_weight,
    query_gain,
    key_gain,
    out_weight,
    attn_post_gain,
    ffn_pre_gain,
    gate_weight,
    up_weight,
    down_weight,
    ffn_post_gain,
    cotangent,
):
    rows, width = tokens.shape
    bf16 = jnp.bfloat16
    scaling = 1.0 / math.sqrt(HEAD)
    ctx_index = lax.axis_index("ctx")
    query_pos = ctx_index * rows + jnp.arange(rows, dtype=jnp.int32)
    cosine, sine = rope_tables(query_pos.astype(jnp.float32))

    qwidth = query_weight.shape[1]
    kwidth = key_weight.shape[1]
    out_columns = out_weight.shape[1] // ctx
    query_columns = qwidth // ctx
    pair = jnp.concatenate([key_weight, value_weight], axis=1)
    pair_rows = pair.shape[0] // ctx
    out_rows = out_weight.shape[0] // ctx
    query_slice = lax.dynamic_slice_in_dim(query_weight, ctx_index * query_columns, query_columns, 1)
    pair_slice = lax.dynamic_slice_in_dim(pair, ctx_index * pair_rows, pair_rows, 0)
    out_slice = lax.dynamic_slice_in_dim(out_weight, ctx_index * out_rows, out_rows, 0)
    gains = (in_gain, query_gain, key_gain, attn_post_gain, ffn_pre_gain, ffn_post_gain)
    cuts = [0]
    for gain in gains:
        cuts.append(cuts[-1] + gain.shape[0])
    packed_gains = jnp.concatenate([gain.astype(jnp.float32) for gain in gains])[None]
    query_dp, pair_dp, out_dp, gains_dp = exchange(
        (query_slice, pair_slice, out_slice, packed_gains), ("gather",) * 4, "dp", dp, 0
    )
    gate_full, up_full, down_full = (
        lax.all_gather(gate_weight, "dp", axis=0, tiled=True),
        lax.all_gather(up_weight, "dp", axis=0, tiled=True),
        lax.all_gather(down_weight, "dp", axis=0, tiled=True),
    )
    gains_dp = gains_dp[:, 0]
    gain_in, gain_query, gain_key, gain_attn, gain_pre, gain_post = (
        gains_dp[:, low:high].reshape(-1) for low, high in zip(cuts[:-1], cuts[1:])
    )
    query_all, pair_all, out_all, tokens_all = exchange(
        (query_dp.reshape(-1, query_columns), pair_dp, out_dp, tokens),
        ("gather",) * 4,
        "ctx",
        ctx,
        1,
    )
    query_full = from_columns(query_all)
    pair_full = jnp.transpose(pair_all, (1, 0, 2, 3)).reshape(-1, 2 * kwidth)
    key_full = pair_full[:, :kwidth]
    value_full = pair_full[:, kwidth:]
    out_full = jnp.transpose(out_all, (1, 0, 2, 3)).reshape(-1, out_weight.shape[1])

    inputs_f = tokens.astype(jnp.float32)
    inv_one = inverse_rms(inputs_f)
    normed_one = (inputs_f * inv_one * gain_in).astype(bf16)
    all_f = tokens_all.reshape(-1, width).astype(jnp.float32)
    normed_all = (all_f * inverse_rms(all_f) * gain_in).astype(bf16)
    key_pos = jnp.arange(all_f.shape[0], dtype=jnp.int32)
    cosine_all, sine_all = rope_tables(key_pos.astype(jnp.float32))
    queries = matmul(normed_one, query_full).reshape(rows, HEADS, HEAD)
    keys = matmul(normed_one, key_full)
    keys_every = matmul(normed_all, key_full)
    value_all = matmul(normed_all, value_full).astype(bf16)
    inv_query = inverse_rms(queries)
    inv_key = inverse_rms(keys)
    query_rot = (
        rotate(queries * inv_query * gain_query, cosine[:, None, :], sine[:, None, :]) * scaling
    ).astype(bf16)
    key_all = rotate(
        keys_every * inverse_rms(keys_every) * gain_key, cosine_all, sine_all
    ).astype(bf16)
    allowed = (query_pos[:, None] >= key_pos[None, :])[None]
    scores = jnp.einsum("qhd,kd->hqk", query_rot, key_all, preferred_element_type=jnp.float32)
    scores = jnp.where(allowed, scores, NEG_FILL)
    row_max = jnp.max(scores, axis=-1, keepdims=True)
    weights = jnp.where(allowed, jnp.exp(scores - row_max), 0.0)
    total = jnp.sum(weights, axis=-1, keepdims=True)
    accum = jnp.einsum(
        "hqk,kd->hqd", weights.astype(bf16), value_all, preferred_element_type=jnp.float32
    )
    attn_heads = jnp.transpose(accum / total, (1, 0, 2)).astype(bf16)
    attn_out = attn_heads.reshape(rows, HEADS * HEAD)
    projected = matmul(attn_out, out_full)
    inv_proj = inverse_rms(projected)
    residual = inputs_f + projected * inv_proj * gain_attn
    inv_two = inverse_rms(residual)
    normed_two = (residual * inv_two * gain_pre).astype(bf16)

    rows_all, attn_all = exchange((normed_two, attn_out), ("gather",) * 2, "ctx", ctx, 2)
    attn_all = attn_all.reshape(-1, attn_out.shape[1])
    rows_all = rows_all.reshape(-1, width)
    gate = matmul(rows_all, gate_full)
    upper = matmul(rows_all, up_full)
    gelu_val, gelu_der = gelu_pair(gate)
    hidden = (gelu_val * upper).astype(bf16)
    ffn_part = matmul_nt(hidden, down_full).astype(bf16).reshape(ctx, rows, width)
    block_out, grad_post, grad_all = ffn_turn(
        ffn_part, residual, cotangent, gain_post[None], "ctx", ctx, 3
    )
    grad_all = grad_all.reshape(-1, width)
    down_part, grad_all = lax.optimization_barrier(
        (matmul_tn(grad_all, hidden).astype(bf16), grad_all)
    )
    down_shard = lax.psum_scatter(down_part, "dp", scatter_dimension=0, tiled=True)
    down_shard = down_shard.astype(jnp.float32)
    hidden_grad = matmul(grad_all, down_full)
    gate_grad = (hidden_grad * upper * gelu_der).astype(bf16)
    up_grad = (hidden_grad * gelu_val).astype(bf16)
    two_part, gate_part, up_part = lax.optimization_barrier(
        (
            (matmul_nt(gate_grad, gate_full) + matmul_nt(up_grad, up_full)).astype(bf16),
            matmul_tn(rows_all, gate_grad).astype(bf16),
            matmul_tn(rows_all, up_grad).astype(bf16),
        )
    )
    gate_shard = lax.psum_scatter(gate_part, "dp", scatter_dimension=0, tiled=True)
    gate_shard = gate_shard.astype(jnp.float32)
    up_shard = lax.psum_scatter(up_part, "dp", scatter_dimension=0, tiled=True)
    up_shard = up_shard.astype(jnp.float32)
    input_grad, query_cols, pair_cols, proj_cols, all_gains = attn_back(
        two_part.reshape(ctx, rows, width),
        residual,
        cotangent,
        projected,
        tokens,
        jnp.stack([gain_in, gain_attn, gain_pre]),
        jnp.stack([gain_query, gain_key]),
        out_full,
        query_full,
        pair_full,
        attn_out,
        query_rot.reshape(rows, HEADS * HEAD),
        key_all,
        value_all,
        queries.reshape(rows, HEADS * HEAD),
        keys,
        cosine,
        sine,
        grad_post,
        "ctx",
        ctx,
        5,
    )
    gain_sums = jnp.sum(all_gains, axis=0)
    gain_grads = (
        gain_sums[0],
        gain_sums[4, :HEAD],
        gain_sums[5, :HEAD],
        gain_sums[1],
        gain_sums[2],
        gain_sums[3],
    )
    packed = jnp.concatenate([grad.reshape(dp, -1) for grad in gain_grads], axis=1)
    query_w = matmul_tn(normed_all, query_cols.reshape(-1, query_columns)).astype(bf16)
    pair_w = matmul_tn(normed_all, pair_cols.reshape(normed_all.shape[0], -1)).astype(bf16)
    out_w = matmul_tn(attn_all, proj_cols.reshape(-1, out_columns)).astype(bf16)
    query_w, pair_w, out_w, gain_parts = exchange(
        (
            query_w.reshape(dp, -1, query_columns),
            pair_w.reshape(dp, -1, pair_w.shape[1]),
            out_w.reshape(dp, -1, out_columns),
            packed[:, None],
        ),
        ("swap",) * 4,
        "dp",
        dp,
        8,
    )
    query_w, pair_w, out_w = exchange(
        (sum_blocks(query_w).astype(bf16), sum_blocks(pair_w).astype(bf16), sum_blocks(out_w).astype(bf16)),
        ("gather",) * 3,
        "ctx",
        ctx,
        9,
    )
    query_w = from_columns(query_w).astype(jnp.float32)
    pair_w = from_columns(pair_w).astype(jnp.float32)
    out_w = from_columns(out_w).astype(jnp.float32)
    gain_done = sum_blocks(gain_parts).reshape(-1)
    share = [gain_done[low:high] for low, high in zip(cuts[:-1], cuts[1:])]
    return (
        block_out,
        input_grad,
        share[0],
        query_w,
        pair_w[:, :kwidth],
        pair_w[:, kwidth:],
        share[1],
        share[2],
        out_w,
        share[3],
        share[4],
        gate_shard,
        up_shard,
        down_shard,
        share[5],
    )


def solution(mesh):
    return jax.shard_map(
        functools.partial(on_device, mesh.shape["dp"], mesh.shape["ctx"]),
        mesh=mesh,
        in_specs=(
            P(("dp", "ctx"), None),
            P("dp"),
            P("dp", None),
            P("dp", None),
            P("dp", None),
            P("dp"),
            P("dp"),
            P("dp", None),
            P("dp"),
            P("dp"),
            P("dp", "ctx"),
            P("dp", "ctx"),
            P("dp", "ctx"),
            P("dp"),
            P(("dp", "ctx"), None),
        ),
        out_specs=(
            P(("dp", "ctx"), None),
            P(("dp", "ctx"), None),
            P("dp"),
            P("dp", None),
            P("dp", None),
            P("dp", None),
            P("dp"),
            P("dp"),
            P("dp", None),
            P("dp"),
            P("dp"),
            P("dp", "ctx"),
            P("dp", "ctx"),
            P("dp", "ctx"),
            P("dp"),
        ),
        check_vma=False,
    )
```

```python
import functools
import math

import jax
import jax.numpy as jnp
from jax import lax
from jax.experimental import pallas as pl
from jax.experimental.layout import Layout, with_layout_constraint
from jax.experimental.pallas import tpu as pltpu
from jax.sharding import PartitionSpec as P

HEADS = 4
HEAD = 256


EPS = 1e-06
GELU_C = math.sqrt(2.0 / math.pi)
NEG_FILL = -1e30


def inverse_rms(values):
    return lax.rsqrt(jnp.mean(values * values, axis=-1, keepdims=True) + EPS)


def norm_back(values, scale_inv, gain, grad_out):
    weighted = grad_out * gain
    cubed = scale_inv * scale_inv * scale_inv
    return scale_inv * weighted - values * cubed * jnp.mean(
        weighted * values, axis=-1, keepdims=True
    )


def gelu_pair(values):
    inner = GELU_C * (values + 0.044715 * values * values * values)
    tanh_val = jnp.tanh(inner)
    result = 0.5 * values * (1.0 + tanh_val)
    slope = 0.5 * (1.0 + tanh_val) + 0.5 * values * (1.0 - tanh_val * tanh_val) * GELU_C * (
        1.0 + 3.0 * 0.044715 * values * values
    )
    return (result, slope)


def rotate(values, cosine, sine):
    middle = values.shape[-1] // 2
    first = values[..., :middle]
    second = values[..., middle:]
    return jnp.concatenate(
        [first * cosine - second * sine, second * cosine + first * sine], axis=-1
    )


def unrotate(grads, cosine, sine):
    middle = grads.shape[-1] // 2
    first = grads[..., :middle]
    second = grads[..., middle:]
    return jnp.concatenate(
        [first * cosine + second * sine, second * cosine - first * sine], axis=-1
    )


def rope_tables(positions):
    middle = HEAD // 2
    freqs = jnp.exp(-(2.0 * jnp.arange(middle, dtype=jnp.float32) / HEAD) * math.log(1000000.0))
    angles = positions[:, None] * freqs[None, :]
    return (jnp.cos(angles), jnp.sin(angles))


def matmul(left, right):
    return jnp.dot(left, right, preferred_element_type=jnp.float32)


def matmul_tn(left, right):
    return lax.dot_general(
        left, right, (((0,), (0,)), ((), ())), preferred_element_type=jnp.float32
    )


def matmul_nt(left, right):
    return lax.dot_general(
        left, right, (((1,), (1,)), ((), ())), preferred_element_type=jnp.float32
    )


MESH = pl.DeviceIdType.MESH


def swap_kernel(size, axis, kinds, *refs):
    count = len(kinds)
    ins, outs, kept = refs[:count], refs[count : 2 * count], refs[2 * count : 3 * count]
    send, recv, local = refs[3 * count :]
    me = lax.axis_index(axis)
    own = []
    for item, kind in enumerate(kinds):
        source = ins[item].at[me] if kind == "swap" else ins[item]
        own.append(pltpu.make_async_copy(source, kept[item], local.at[item, 0]))
        own[-1].start()
    barrier = pltpu.get_barrier_semaphore()
    for step in range(1, size):
        peer = lax.rem(me + step, size)
        pl.semaphore_signal(barrier, inc=1, device_id={axis: peer}, device_id_type=MESH)
    pl.semaphore_wait(barrier, size - 1)
    copies = []
    for item, kind in enumerate(kinds):
        for step in range(1, size):
            peer = lax.rem(me + step, size)
            source = ins[item].at[peer] if kind == "swap" else ins[item]
            copy = pltpu.make_async_remote_copy(
                src_ref=source,
                dst_ref=outs[item].at[me],
                send_sem=send.at[item, step - 1],
                recv_sem=recv.at[item, step - 1],
                device_id={axis: peer},
                device_id_type=MESH,
            )
            copy.start()
            copies.append(copy)
    for item in range(count):
        own[item].wait()
        copy = pltpu.make_async_copy(kept[item], outs[item].at[me], local.at[item, 1])
        copy.start()
        copies.append(copy)
    for copy in copies:
        copy.wait()


def chunks_of(rows):
    for parts in (4, 3, 2):
        if rows % (16 * parts) == 0:
            return parts
    return 1


def pair_gather_kernel(size, axis, kinds, *refs):
    count = len(kinds)
    ins, outs, kept = refs[:count], refs[count : 2 * count], refs[2 * count : 3 * count]
    send, recv, pass_send, pass_recv, local = refs[3 * count :]
    me = lax.axis_index(axis)
    twin = me + 1 - 2 * lax.rem(me, 2)
    half = size // 2
    own = []
    for item in range(count):
        own.append(pltpu.make_async_copy(ins[item], kept[item], local.at[item, 0]))
        own[-1].start()
    barrier = pltpu.get_barrier_semaphore()
    for step in range(1, half):
        peer = lax.rem(me + 2 * step, size)
        pl.semaphore_signal(barrier, inc=1, device_id={axis: peer}, device_id_type=MESH)
    pl.semaphore_signal(barrier, inc=1, device_id={axis: twin}, device_id_type=MESH)
    pl.semaphore_wait(barrier, half)
    pieces = []
    for item in range(count):
        rows = ins[item].shape[0]
        pieces += [
            (item, part, pl.ds(part * (rows // chunks_of(rows)), rows // chunks_of(rows)))
            for part in range(chunks_of(rows))
        ]
    across, last = [], []
    for item, part, span in pieces:
        for step in range(1, half):
            copy = pltpu.make_async_remote_copy(
                src_ref=ins[item].at[span],
                dst_ref=outs[item].at[me, span],
                send_sem=send.at[item, step, part],
                recv_sem=recv.at[item, step, part],
                device_id={axis: lax.rem(me + 2 * step, size)},
                device_id_type=MESH,
            )
            copy.start()
            across.append((copy, item, step, part, span))
    for item, part, span in pieces:
        copy = pltpu.make_async_remote_copy(
            src_ref=ins[item].at[span],
            dst_ref=outs[item].at[me, span],
            send_sem=pass_send.at[item, 0, part],
            recv_sem=pass_recv.at[item, 0, part],
            device_id={axis: twin},
            device_id_type=MESH,
        )
        copy.start()
        last.append(copy)
    for item in range(count):
        own[item].wait()
        copy = pltpu.make_async_copy(kept[item], outs[item].at[me], local.at[item, 1])
        copy.start()
        last.append(copy)
    for arrived, item, step, part, span in across:
        arrived.wait_recv()
        origin = lax.rem(me + size - 2 * step, size)
        copy = pltpu.make_async_remote_copy(
            src_ref=outs[item].at[origin, span],
            dst_ref=outs[item].at[origin, span],
            send_sem=pass_send.at[item, step, part],
            recv_sem=pass_recv.at[item, step, part],
            device_id={axis: twin},
            device_id_type=MESH,
        )
        copy.start()
        last.append(copy)
    for sent, *_ in across:
        sent.wait_send()
    for copy in last:
        copy.wait()


def exchange(arrays, kinds, axis, size, ident):
    count = len(arrays)
    pairs = all(kind == "gather" for kind in kinds) and axis == "ctx" and size % 2 == 0
    shapes = tuple(
        jax.ShapeDtypeStruct(x.shape if kind == "swap" else (size,) + x.shape, x.dtype)
        for x, kind in zip(arrays, kinds)
    )
    dma = pltpu.SemaphoreType.DMA
    if pairs:
        half = size // 2
        parts = max(chunks_of(x.shape[0]) for x in arrays)
        scratch = [dma((count, half, parts))] * 4
        body = pair_gather_kernel
    else:
        scratch = [dma((count, size - 1))] * 2
        body = swap_kernel
    moved = sum(x.size * x.dtype.itemsize for x in shapes)
    return pl.pallas_call(
        functools.partial(body, size, axis, tuple(kinds)),
        out_shape=shapes,
        in_specs=[pl.BlockSpec(memory_space=pl.ANY)] * count,
        out_specs=tuple(pl.BlockSpec(memory_space=pl.ANY) for _ in arrays),
        scratch_shapes=[pltpu.VMEM(x.shape[1:], x.dtype) for x in shapes]
        + scratch
        + [dma((count, 2))],
        compiler_params=pltpu.CompilerParams(collective_id=ident, has_side_effects=True),
        cost_estimate=pl.CostEstimate(flops=0, bytes_accessed=20 * moved, transcendentals=0),
        name=f"exchange_{ident}",
    )(*arrays)


def pieces_of(rows):
    parts = chunks_of(rows)
    return [pl.ds(part * (rows // parts), rows // parts) for part in range(parts)]


def remote(source, target, send, recv, axis, peer):
    copy = pltpu.make_async_remote_copy(
        src_ref=source,
        dst_ref=target,
        send_sem=send,
        recv_sem=recv,
        device_id={axis: peer},
        device_id_type=MESH,
    )
    copy.start()
    return copy


class Place:
    def __init__(self, axis, size):
        self.axis, self.size, self.half = axis, size, size // 2
        self.me = lax.axis_index(axis)
        self.core = lax.rem(self.me, 2)
        self.twin = self.me + 1 - 2 * self.core

    def across(self, step):
        return lax.rem(self.me + 2 * step, self.size)

    def behind(self, step):
        return lax.rem(self.me + self.size - 2 * step, self.size)

    def greet_pairs(self):
        barrier = pltpu.get_barrier_semaphore()
        for step in range(1, self.half):
            pl.semaphore_signal(
                barrier, inc=1, device_id={self.axis: self.across(step)}, device_id_type=MESH
            )
        pl.semaphore_signal(barrier, inc=1, device_id={self.axis: self.twin}, device_id_type=MESH)
        pl.semaphore_wait(barrier, self.half)

    def greet_all(self):
        barrier = pltpu.get_barrier_semaphore()
        for step in range(1, self.size):
            peer = lax.rem(self.me + step, self.size)
            pl.semaphore_signal(barrier, inc=1, device_id={self.axis: peer}, device_id_type=MESH)
        pl.semaphore_wait(barrier, self.size - 1)


def scatter_scratch(size, rows, width):
    half, parts, dma = size // 2, chunks_of(rows), pltpu.SemaphoreType.DMA
    block = lambda count: pltpu.VMEM((count, rows, width), jnp.bfloat16)
    return [block(half), block(half), block(half - 1), block(half - 1), dma((half,))] + [
        dma((half, parts))
    ] * 4


class Scatter:
    def __init__(self, place, part, scratch):
        self.place, self.part = place, part
        self.kept, self.twins, self.summed, self.landed = scratch[:4]
        self.local, self.twin_send, self.twin_recv, self.send, self.recv = scratch[4:]
        self.spans = pieces_of(self.kept.shape[1])

    def load(self):
        place = self.place
        self.loads = []
        for slot in range(place.half):
            copy = pltpu.make_async_copy(
                self.part.at[place.across(slot)], self.kept.at[slot], self.local.at[slot]
            )
            copy.start()
            self.loads.append(copy)

    def start(self):
        place = self.place
        self.twin_copies, self.copies = {}, {}
        slots = list(range(1, place.half)) + [0]
        for index, span in enumerate(self.spans):
            for slot in slots:
                self.twin_copies[slot, index] = remote(
                    self.part.at[place.across(slot) + 1 - 2 * place.core, span],
                    self.twins.at[slot, span],
                    self.twin_send.at[slot, index],
                    self.twin_recv.at[slot, index],
                    place.axis,
                    place.twin,
                )
        for copy in self.loads:
            copy.wait()
        for index, span in enumerate(self.spans):
            for slot in slots[:-1]:
                self.twin_copies[slot, index].wait_recv()
                self.summed[slot - 1, span] = (
                    self.kept[slot, span].astype(jnp.float32)
                    + self.twins[slot, span].astype(jnp.float32)
                ).astype(jnp.bfloat16)
                self.copies[slot, index] = remote(
                    self.summed.at[slot - 1, span],
                    self.landed.at[slot - 1, span],
                    self.send.at[slot, index],
                    self.recv.at[slot, index],
                    place.axis,
                    place.across(slot),
                )

    def total(self, index):
        span = self.spans[index]
        self.twin_copies[0, index].wait_recv()
        value = self.kept[0, span].astype(jnp.float32) + self.twins[0, span].astype(jnp.float32)
        for slot in range(1, self.place.half):
            self.copies[slot, index].wait_recv()
            value = value + self.landed[slot - 1, span].astype(jnp.float32)
        return value

    def finish(self):
        for copy in list(self.twin_copies.values()) + list(self.copies.values()):
            copy.wait_send()


def gather_scratch(size, rows):
    dma = pltpu.SemaphoreType.DMA
    return [dma((size // 2, chunks_of(rows)))] * 4 + [dma((chunks_of(rows),))]


class Gather:
    def __init__(self, place, source, target, scratch):
        self.place, self.source, self.target = place, source, target
        self.send, self.recv, self.pass_send, self.pass_recv, self.local = scratch
        self.spans = pieces_of(source.shape[0])
        self.across, self.last = [], []

    def start(self, index):
        place, span = self.place, self.spans[index]
        for step in range(1, place.half):
            copy = remote(
                self.source.at[span],
                self.target.at[place.me, span],
                self.send.at[step, index],
                self.recv.at[step, index],
                place.axis,
                place.across(step),
            )
            self.across.append((copy, step, index))
        self.last.append(
            remote(
                self.source.at[span],
                self.target.at[place.me, span],
                self.pass_send.at[0, index],
                self.pass_recv.at[0, index],
                place.axis,
                place.twin,
            )
        )
        copy = pltpu.make_async_copy(
            self.source.at[span], self.target.at[place.me, span], self.local.at[index]
        )
        copy.start()
        self.last.append(copy)

    def relay(self):
        place = self.place
        for copy, step, index in self.across:
            copy.wait_recv()
            block = self.target.at[place.behind(step), self.spans[index]]
            self.last.append(
                remote(
                    block,
                    block,
                    self.pass_send.at[step, index],
                    self.pass_recv.at[step, index],
                    place.axis,
                    place.twin,
                )
            )

    def finish(self):
        for copy, *_ in self.across:
            copy.wait_send()
        for copy in self.last:
            copy.wait()


def ffn_turn_kernel(axis, size, part, residual, cot, gain, block_out, gain_grad, gathered, grad, *scratch):
    place = Place(axis, size)
    scatter = Scatter(place, part, scratch[:9])
    gather = Gather(place, grad, gathered, scratch[9:])
    scatter.load()
    place.greet_pairs()
    scatter.start()
    gain_row = gain[...]
    for index, span in enumerate(scatter.spans):
        ffn_sum = scatter.total(index)
        inverse = inverse_rms(ffn_sum)
        incoming = cot[span].astype(jnp.float32)
        grad[span] = norm_back(ffn_sum, inverse, gain_row, incoming).astype(jnp.bfloat16)
        gather.start(index)
        scaled = ffn_sum * inverse
        block_out[span] = (residual[span] + scaled * gain_row).astype(jnp.bfloat16)
        share = jnp.sum(incoming * scaled, axis=0, keepdims=True)
        gain_grad[...] = share if index == 0 else gain_grad[...] + share
    gather.relay()
    scatter.finish()
    gather.finish()


def ffn_turn(part, residual, cotangent, gain, axis, size, ident):
    rows, width = residual.shape
    whole = pl.BlockSpec(memory_space=pltpu.VMEM)
    away = pl.BlockSpec(memory_space=pl.ANY)
    return pl.pallas_call(
        functools.partial(ffn_turn_kernel, axis, size),
        out_shape=(
            jax.ShapeDtypeStruct((rows, width), jnp.bfloat16),
            jax.ShapeDtypeStruct((1, width), jnp.float32),
            jax.ShapeDtypeStruct((size, rows, width), jnp.bfloat16),
        ),
        in_specs=[away, whole, whole, whole],
        out_specs=(whole, whole, away),
        scratch_shapes=[pltpu.VMEM((rows, width), jnp.bfloat16)]
        + scatter_scratch(size, rows, width)
        + gather_scratch(size, rows),
        compiler_params=pltpu.CompilerParams(collective_id=ident, has_side_effects=True),
        cost_estimate=pl.CostEstimate(
            flops=0, bytes_accessed=20 * part.size * 2, transcendentals=0
        ),
        name=f"ffn_turn_{ident}",
    )(part, residual, cotangent, gain)


def attn_back_kernel(
    axis,
    size,
    part,
    residual,
    cot,
    projected,
    tokens,
    gains,
    out_hbm,
    query_hbm,
    pair_hbm,
    attn_out,
    query_rot,
    key_hbm,
    value_hbm,
    queries,
    keys,
    cosine,
    sine,
    post_grad,
    input_grad,
    query_cols,
    pair_cols,
    proj_cols,
    all_gains,
    out_w,
    query_w,
    pair_w,
    key_all,
    value_all,
    res_grad,
    proj_grad,
    stacked_p,
    stacked_s,
    stacked_g,
    stacked_q,
    pair_part,
    query_grad,
    query_send,
    pair_send,
    proj_send,
    gain_send,
    local,
    send,
    recv,
    *scratch,
):
    rows, width = residual.shape
    total_keys = key_all.shape[0]
    bf16, f32 = jnp.bfloat16, jnp.float32
    scaling = 1.0 / math.sqrt(HEAD)
    place = Place(axis, size)
    me = place.me
    two = Scatter(place, part, scratch[:9])
    pairs = Scatter(place, pair_part, scratch[9:])
    two.load()
    loads = []
    for source, target in (
        (out_hbm, out_w),
        (key_hbm, key_all),
        (value_hbm, value_all),
        (query_hbm, query_w),
        (pair_hbm, pair_w),
    ):
        copy = pltpu.make_async_copy(source, target, local.at[len(loads)])
        copy.start()
        loads.append(copy)
    place.greet_all()
    two.start()
    swaps = []

    def swap(item, source, target):
        for step in range(1, size):
            peer = lax.rem(me + step, size)
            swaps.append(
                remote(
                    source.at[peer],
                    target.at[me],
                    send.at[item, step - 1],
                    recv.at[item, step - 1],
                    axis,
                    peer,
                )
            )
        copy = pltpu.make_async_copy(source.at[me], target.at[me], local.at[len(loads) + item])
        copy.start()
        swaps.append(copy)

    gain_in, gain_attn, gain_pre = gains[0:1], gains[1:2], gains[2:3]
    gain_query, gain_key = gains[4:5, :HEAD], gains[4:5, HEAD : 2 * HEAD]
    here = pl.ds(pl.multiple_of(me * rows, rows), rows)
    cos_here, sin_here = cosine[here], sine[here]
    gain_send[...] = jnp.zeros_like(gain_send)
    gain_send[3:4] = post_grad[...]
    proj_width = width // size
    for index, span in enumerate(two.spans):
        two_grad = two.total(index)
        kept = residual[span]
        inv_two = inverse_rms(kept)
        back = cot[span].astype(f32) + norm_back(kept, inv_two, gain_pre, two_grad)
        res_grad[span] = back
        ahead = projected[span]
        inv_proj = inverse_rms(ahead)
        proj_back = norm_back(ahead, inv_proj, gain_attn, back)
        proj_grad[span] = proj_back.astype(bf16)
        for peer in range(size):
            proj_send[peer, span] = proj_back[:, peer * proj_width : (peer + 1) * proj_width].astype(
                bf16
            )
        gain_send[2:3] += jnp.sum(two_grad * kept * inv_two, axis=0, keepdims=True)
        gain_send[1:2] += jnp.sum(back * ahead * inv_proj, axis=0, keepdims=True)
    swap(0, proj_send, proj_cols)
    loads[0].wait()
    attn_grad = matmul_nt(proj_grad[...], out_w[...]).astype(bf16)
    loads[1].wait()
    loads[2].wait()
    query_pos = me * rows + lax.broadcasted_iota(jnp.int32, (rows, total_keys), 0)
    allowed = query_pos >= lax.broadcasted_iota(jnp.int32, (rows, total_keys), 1)
    for head in range(HEADS):
        lanes = slice(head * HEAD, (head + 1) * HEAD)
        level = pl.ds(head * rows, rows)
        query = query_rot[:, lanes]
        incoming = attn_grad[:, lanes]
        scores = jnp.where(allowed, matmul_nt(query, key_all[...]), NEG_FILL)
        weights = jnp.where(
            allowed, jnp.exp(scores - jnp.max(scores, axis=-1, keepdims=True)), 0.0
        )
        probs = weights / jnp.sum(weights, axis=-1, keepdims=True)
        delta = jnp.sum(
            incoming.astype(f32) * attn_out[:, lanes].astype(f32), axis=-1, keepdims=True
        )
        prob_grad = matmul_nt(incoming, value_all[...])
        stacked_s[level] = (probs * (prob_grad - delta)).astype(bf16)
        stacked_p[level] = probs.astype(bf16)
        stacked_g[level] = incoming
        stacked_q[level] = query
    values_part = matmul_tn(stacked_p[...], stacked_g[...]).astype(bf16)
    keys_part = matmul_tn(stacked_s[...], stacked_q[...]).astype(bf16)
    for peer in range(size):
        block = slice(peer * rows, (peer + 1) * rows)
        pair_part[peer, :, :HEAD] = keys_part[block]
        pair_part[peer, :, HEAD:] = values_part[block]
    pairs.load()
    pairs.start()
    query_width = HEADS * HEAD // size
    gain_share = jnp.zeros((1, HEAD), f32)
    for head in range(HEADS):
        lanes = slice(head * HEAD, (head + 1) * HEAD)
        level = pl.ds(head * rows, rows)
        normed_grad = unrotate(
            matmul(stacked_s[level], key_all[...]) * scaling, cos_here, sin_here
        )
        value = queries[:, lanes]
        inverse = inverse_rms(value)
        gain_share = gain_share + jnp.sum(normed_grad * value * inverse, axis=0, keepdims=True)
        query_grad[:, lanes] = norm_back(value, inverse, gain_query, normed_grad).astype(bf16)
    for peer in range(size):
        query_send[peer] = query_grad[:, peer * query_width : (peer + 1) * query_width]
    swap(1, query_send, query_cols)
    gain_send[4:5, :HEAD] = gain_share
    loads[3].wait()
    input_grad[...] = matmul_nt(query_grad[...], query_w[...])
    loads[4].wait()
    pair_width = 2 * HEAD // size
    key_share = jnp.zeros((1, HEAD), f32)
    for index, span in enumerate(pairs.spans):
        pair_total = pairs.total(index)
        near = slice(span.start, span.start + span.size)
        normed_grad = unrotate(pair_total[:, :HEAD], cos_here[near], sin_here[near])
        value = keys[span]
        inverse = inverse_rms(value)
        key_share = key_share + jnp.sum(normed_grad * value * inverse, axis=0, keepdims=True)
        both = jnp.concatenate(
            [norm_back(value, inverse, gain_key, normed_grad), pair_total[:, HEAD:]], axis=1
        )
        for peer in range(size):
            pair_send[peer, span] = both[:, peer * pair_width : (peer + 1) * pair_width].astype(bf16)
        one_grad = input_grad[span] + matmul_nt(both.astype(bf16), pair_w[...])
        inputs = tokens[span].astype(f32)
        inv_one = inverse_rms(inputs)
        gain_send[0:1] += jnp.sum(one_grad * inputs * inv_one, axis=0, keepdims=True)
        input_grad[span] = res_grad[span] + norm_back(inputs, inv_one, gain_in, one_grad)
    gain_send[5:6, :HEAD] = key_share
    swap(2, pair_send, pair_cols)
    for step in range(1, size):
        peer = lax.rem(me + step, size)
        swaps.append(
            remote(
                gain_send,
                all_gains.at[me],
                send.at[3, step - 1],
                recv.at[3, step - 1],
                axis,
                peer,
            )
        )
    copy = pltpu.make_async_copy(gain_send, all_gains.at[me], local.at[len(loads) + 3])
    copy.start()
    swaps.append(copy)
    two.finish()
    pairs.finish()
    for copy in swaps:
        copy.wait()


def attn_back(
    part,
    residual,
    cotangent,
    projected,
    tokens,
    gains,
    out_full,
    query_full,
    pair_full,
    attn_out,
    query_rot,
    key_all,
    value_all,
    queries,
    keys,
    cosine,
    sine,
    post_grad,
    axis,
    size,
    ident,
):
    rows, width = residual.shape
    bf16, f32 = jnp.bfloat16, jnp.float32
    whole = pl.BlockSpec(memory_space=pltpu.VMEM)
    away = pl.BlockSpec(memory_space=pl.ANY)
    qwidth, total_keys = query_full.shape[1], key_all.shape[0]
    query_cols = (size, rows, qwidth // size)
    pair_cols = (size, rows, 2 * HEAD // size)
    proj_cols = (size, rows, width // size)
    dma = pltpu.SemaphoreType.DMA
    return pl.pallas_call(
        functools.partial(attn_back_kernel, axis, size),
        out_shape=(
            jax.ShapeDtypeStruct((rows, width), f32),
            jax.ShapeDtypeStruct(query_cols, bf16),
            jax.ShapeDtypeStruct(pair_cols, bf16),
            jax.ShapeDtypeStruct(proj_cols, bf16),
            jax.ShapeDtypeStruct((size, 8, width), f32),
        ),
        in_specs=[away]
        + [whole] * 5
        + [away] * 3
        + [whole] * 2
        + [away] * 2
        + [whole] * 5,
        out_specs=(whole, away, away, away, away),
        scratch_shapes=[
            pltpu.VMEM(out_full.shape, bf16),
            pltpu.VMEM(query_full.shape, bf16),
            pltpu.VMEM(pair_full.shape, bf16),
            pltpu.VMEM(key_all.shape, bf16),
            pltpu.VMEM(value_all.shape, bf16),
            pltpu.VMEM((rows, width), f32),
            pltpu.VMEM((rows, width), bf16),
            pltpu.VMEM((HEADS * rows, total_keys), bf16),
            pltpu.VMEM((HEADS * rows, total_keys), bf16),
            pltpu.VMEM((HEADS * rows, HEAD), bf16),
            pltpu.VMEM((HEADS * rows, HEAD), bf16),
            pltpu.VMEM((size, rows, 2 * HEAD), bf16),
            pltpu.VMEM((rows, qwidth), bf16),
            pltpu.VMEM(query_cols, bf16),
            pltpu.VMEM(pair_cols, bf16),
            pltpu.VMEM(proj_cols, bf16),
            pltpu.VMEM((8, width), f32),
            dma((9,)),
            dma((4, size - 1)),
            dma((4, size - 1)),
        ]
        + scatter_scratch(size, rows, width)
        + scatter_scratch(size, rows, 2 * HEAD),
        compiler_params=pltpu.CompilerParams(collective_id=ident, has_side_effects=True),
        cost_estimate=pl.CostEstimate(
            flops=0, bytes_accessed=30 * part.size * 2, transcendentals=0
        ),
        name=f"attn_back_{ident}",
    )(
        part,
        residual,
        cotangent,
        projected,
        tokens,
        gains,
        out_full,
        query_full,
        pair_full,
        attn_out,
        query_rot,
        key_all,
        value_all,
        queries,
        keys,
        cosine,
        sine,
        post_grad,
    )


def attn_front_kernel(
    dp,
    ctx,
    tokens,
    query_in,
    pair_in,
    out_in,
    gains_in,
    cosine,
    sine,
    residual,
    projected,
    queries,
    keys,
    query_rot,
    attn_out,
    key_all,
    value_all,
    gains,
    normed_hbm,
    query_hbm,
    pair_hbm,
    out_hbm,
    rows_all,
    attn_all,
    tokens_all,
    normed_all,
    query_w,
    pair_w,
    out_w,
    keys_all,
    gains_all,
    normed_two,
    local,
    far_send,
    far_recv,
    near_send,
    near_recv,
    pass_send,
    pass_recv,
    *scratch,
):
    rows, width = tokens.shape
    total_keys = key_all.shape[0]
    bf16, f32 = jnp.bfloat16, jnp.float32
    scaling = 1.0 / math.sqrt(HEAD)
    place = Place("ctx", ctx)
    me, row = place.me, lax.axis_index("dp")
    shard = query_in.shape[0]
    query_width = query_w.shape[1] // ctx
    pair_depth, pair_width = pair_in.shape
    out_shard = out_in.shape[0]
    out_depth = out_shard // ctx

    def query_region(source, base, origin):
        return source.at[
            pl.ds(pl.multiple_of(base * shard, 16), shard),
            pl.ds(pl.multiple_of(origin * query_width, 128), query_width),
        ]

    def pair_region(base, origin):
        start = base * shard + lax.rem(origin, 2) * pair_depth
        return pair_w.at[
            pl.ds(pl.multiple_of(start, 16), pair_depth),
            pl.ds(pl.multiple_of((origin // 2) * pair_width, 128), pair_width),
        ]

    def out_region(source, base, origin):
        start = base * out_shard + origin * out_depth
        return source.at[pl.ds(pl.multiple_of(start, 16), out_depth)]

    regions = (
        pair_region,
        functools.partial(query_region, query_w),
        functools.partial(out_region, out_w),
    )
    sources = (pair_in, query_region(query_in, 0, me), out_region(out_in, 0, me))
    pending = []

    def stay(source, target, index):
        copy = pltpu.make_async_copy(source, target, local.at[index])
        copy.start()
        return copy

    own = [stay(sources[item], regions[item](row, me), item) for item in range(3)]
    own.append(stay(gains_in, gains_all.at[row], 3))
    barrier = pltpu.get_barrier_semaphore()
    for step in range(1, place.half):
        pl.semaphore_signal(
            barrier, inc=1, device_id={"ctx": place.across(step)}, device_id_type=MESH
        )
    pl.semaphore_signal(barrier, inc=1, device_id={"ctx": place.twin}, device_id_type=MESH)
    for step in range(1, dp):
        pl.semaphore_signal(
            barrier, inc=1, device_id={"dp": lax.rem(row + step, dp)}, device_id_type=MESH
        )
    pl.semaphore_wait(barrier, place.half + dp - 1)

    far, near = {}, {}
    for item in (3, 0, 1, 2):
        for step in range(1, dp):
            far[item, step] = remote(
                gains_in if item == 3 else sources[item],
                gains_all.at[row] if item == 3 else regions[item](row, me),
                far_send.at[item, step - 1],
                far_recv.at[item, step - 1],
                "dp",
                lax.rem(row + step, dp),
            )
    token_gather = Gather(place, tokens, tokens_all, scratch[:5])
    row_gather = Gather(place, normed_two, rows_all, scratch[5:10])
    attn_gather = Gather(place, attn_out, attn_all, scratch[10:15])
    for index in range(len(token_gather.spans)):
        token_gather.start(index)

    def spread(item, lag):
        base = lax.rem(row + dp - lag, dp)
        if lag:
            far[item, lag].wait_recv()
        source = regions[item](base, me) if lag else sources[item]
        target = regions[item](base, me)
        for step in range(1, place.half):
            near[item, lag, step] = remote(
                source,
                target,
                near_send.at[item, lag, step],
                near_recv.at[item, lag, step],
                "ctx",
                place.across(step),
            )
        pending.append(
            remote(
                source,
                target,
                pass_send.at[item, lag, 0],
                pass_recv.at[item, lag, 0],
                "ctx",
                place.twin,
            )
        )
        item_passes[item].append(pending[-1])

    def relay(item):
        for lag in range(dp):
            base = lax.rem(row + dp - lag, dp)
            for step in range(1, place.half):
                near[item, lag, step].wait_recv()
                block = regions[item](base, place.behind(step))
                pending.append(
                    remote(
                        block,
                        block,
                        pass_send.at[item, lag, step],
                        pass_recv.at[item, lag, step],
                        "ctx",
                        place.twin,
                    )
                )
                item_passes[item].append(pending[-1])

    def complete(item):
        for copy in item_passes[item]:
            copy.wait_recv()
        own[item].wait()

    item_passes = ([], [], [])
    for item in range(3):
        spread(item, 0)
    token_gather.relay()
    for lag in range(1, dp):
        spread(0, lag)
    for step in range(1, dp):
        far[3, step].wait_recv()
    own[3].wait()
    total = gains_all[0]
    for step in range(1, dp):
        total = total + gains_all[step]
    gains[...] = total
    token_gather.finish()

    def normalize(block, carry):
        value = tokens_all[block].astype(f32)
        normed_all[block] = (value * inverse_rms(value) * gains[0:1]).astype(bf16)
        return carry

    lax.fori_loop(0, ctx, normalize, 0)
    saves = [stay(normed_all, normed_hbm, 4)]
    for lag in range(1, dp):
        spread(1, lag)
    relay(0)
    for lag in range(1, dp):
        spread(2, lag)
    complete(0)
    saves.append(stay(pair_w, pair_hbm, 5))

    def project(block, carry):
        both = matmul(normed_all[block], pair_w[...])
        value = both[:, :HEAD]
        turn = pl.ds(pl.multiple_of(block * rows, rows), rows)
        keys_all[block] = value
        key_all[turn] = rotate(
            value * inverse_rms(value) * gains[4:5, HEAD : 2 * HEAD], cosine[turn], sine[turn]
        ).astype(bf16)
        value_all[turn] = both[:, HEAD:].astype(bf16)
        return carry

    lax.fori_loop(0, ctx, project, 0)
    keys[...] = keys_all[me]
    relay(1)
    complete(1)
    saves.append(stay(query_w, query_hbm, 6))
    queries[...] = matmul(normed_all[me], query_w[...])
    here = pl.ds(pl.multiple_of(me * rows, rows), rows)
    cos_here, sin_here = cosine[here], sine[here]
    query_pos = me * rows + lax.broadcasted_iota(jnp.int32, (rows, total_keys), 0)
    allowed = query_pos >= lax.broadcasted_iota(jnp.int32, (rows, total_keys), 1)
    for head in range(HEADS):
        lanes = slice(head * HEAD, (head + 1) * HEAD)
        value = queries[:, lanes]
        query = (
            rotate(value * inverse_rms(value) * gains[4:5, :HEAD], cos_here, sin_here) * scaling
        ).astype(bf16)
        query_rot[:, lanes] = query
        scores = jnp.where(allowed, matmul_nt(query, key_all[...]), NEG_FILL)
        weights = jnp.where(
            allowed, jnp.exp(scores - jnp.max(scores, axis=-1, keepdims=True)), 0.0
        )
        attn_out[:, lanes] = (
            matmul(weights.astype(bf16), value_all[...]) / jnp.sum(weights, axis=-1, keepdims=True)
        ).astype(bf16)
    relay(2)
    complete(2)
    saves.append(stay(out_w, out_hbm, 7))
    projected[...] = matmul(attn_out[...], out_w[...])
    for index, span in enumerate(row_gather.spans):
        ahead = projected[span]
        kept = tokens[span].astype(f32) + ahead * inverse_rms(ahead) * gains[1:2]
        residual[span] = kept
        normed_two[span] = (kept * inverse_rms(kept) * gains[2:3]).astype(bf16)
        row_gather.start(index)
    for index in range(len(attn_gather.spans)):
        attn_gather.start(index)
    row_gather.relay()
    attn_gather.relay()
    row_gather.finish()
    attn_gather.finish()
    for copy in list(far.values()) + list(near.values()) + pending:
        copy.wait_send()
    for copy in saves:
        copy.wait()


def attn_front(tokens, query_weight, pair, out_weight, gain_rows, cosine, sine, dp, ctx, ident):
    rows, width = tokens.shape
    shard, qwidth = query_weight.shape
    half = ctx // 2
    pair_depth, pair_width = shard // 2, pair.shape[1] // half
    index = lax.axis_index("ctx")
    pair_slice = lax.dynamic_slice(
        pair, (lax.rem(index, 2) * pair_depth, index // 2 * pair_width), (pair_depth, pair_width)
    )
    bf16, f32 = jnp.bfloat16, jnp.float32
    whole = pl.BlockSpec(memory_space=pltpu.VMEM)
    away = pl.BlockSpec(memory_space=pl.ANY)
    dma = pltpu.SemaphoreType.DMA
    vmem, shape = pltpu.VMEM, jax.ShapeDtypeStruct
    query_full, pair_full = (dp * shard, qwidth), (dp * shard, pair.shape[1])
    out_full = (dp * out_weight.shape[0], width)
    return pl.pallas_call(
        functools.partial(attn_front_kernel, dp, ctx),
        out_shape=(
            shape((rows, width), f32),
            shape((rows, width), f32),
            shape((rows, qwidth), f32),
            shape((rows, HEAD), f32),
            shape((rows, qwidth), bf16),
            shape((rows, qwidth), bf16),
            shape((ctx * rows, HEAD), bf16),
            shape((ctx * rows, HEAD), bf16),
            shape((8, width), f32),
            shape((ctx, rows, width), bf16),
            shape(query_full, bf16),
            shape(pair_full, bf16),
            shape(out_full, bf16),
            shape((ctx, rows, width), bf16),
            shape((ctx, rows, qwidth), bf16),
        ),
        in_specs=[whole, away, whole, away, whole, whole, whole],
        out_specs=(whole,) * 9 + (away,) * 6,
        scratch_shapes=[
            vmem((ctx, rows, width), bf16),
            vmem((ctx, rows, width), bf16),
            vmem(query_full, bf16),
            vmem(pair_full, bf16),
            vmem(out_full, bf16),
            vmem((ctx, rows, HEAD), f32),
            vmem((dp, 8, width), f32),
            vmem((rows, width), bf16),
            dma((8,)),
            dma((4, dp - 1)),
            dma((4, dp - 1)),
        ]
        + [dma((3, dp, half))] * 4
        + gather_scratch(ctx, rows) * 3,
        compiler_params=pltpu.CompilerParams(collective_id=ident, has_side_effects=True),
        cost_estimate=pl.CostEstimate(
            flops=0, bytes_accessed=100 * ctx * rows * width, transcendentals=0
        ),
        name=f"attn_front_{ident}",
    )(tokens, query_weight, pair_slice, out_weight, gain_rows, cosine, sine)


def fits_front(shard, qwidth, pair_width, out_shard, ctx):
    return (
        ctx % 2 == 0
        and qwidth % (128 * ctx) == 0
        and pair_width % (64 * ctx) == 0
        and shard % 32 == 0
        and out_shard % (16 * ctx) == 0
    )


def gain_block(gains, width):
    gain_in, gain_query, gain_key, gain_attn, gain_pre, gain_post = gains
    heads = jnp.concatenate([gain_query, gain_key])
    heads = jnp.pad(heads, (0, width - heads.shape[0]))
    stacked = jnp.stack([gain_in, gain_attn, gain_pre, gain_post, heads])
    return jnp.pad(stacked, ((0, 3), (0, 0)))


def spread_gain(gain, dp):
    place = jnp.arange(dp * gain.shape[0], dtype=jnp.int32) // gain.shape[0]
    tiled = jnp.tile(gain.astype(jnp.float32), dp)
    return jnp.where(place == lax.axis_index("dp"), tiled, 0.0)


def by_rows(array):
    return with_layout_constraint(array, Layout(major_to_minor=(0, 1)))


def by_columns(array, parts):
    rows, columns = array.shape
    return jnp.transpose(array.reshape(rows, parts, columns // parts), (1, 0, 2))


def from_columns(array):
    parts, rows, columns = array.shape
    return jnp.transpose(array, (1, 0, 2)).reshape(rows, parts * columns)


def sum_blocks(array):
    return jnp.sum(array.astype(jnp.float32), axis=0)


def plain_front(
    tokens, query_weight, pair, out_weight, raw_gains, cuts, cosine_all, sine_all, dp, ctx
):
    rows, width = tokens.shape
    bf16 = jnp.bfloat16
    scaling = 1.0 / math.sqrt(HEAD)
    ctx_index = lax.axis_index("ctx")
    query_pos = ctx_index * rows + jnp.arange(rows, dtype=jnp.int32)
    cosine = lax.dynamic_slice_in_dim(cosine_all, ctx_index * rows, rows, 0)
    sine = lax.dynamic_slice_in_dim(sine_all, ctx_index * rows, rows, 0)
    kwidth = pair.shape[1] // 2
    query_columns = query_weight.shape[1] // ctx
    pair_rows = pair.shape[0] // ctx
    out_rows = out_weight.shape[0] // ctx
    query_slice = lax.dynamic_slice_in_dim(query_weight, ctx_index * query_columns, query_columns, 1)
    pair_slice = lax.dynamic_slice_in_dim(pair, ctx_index * pair_rows, pair_rows, 0)
    out_slice = lax.dynamic_slice_in_dim(out_weight, ctx_index * out_rows, out_rows, 0)
    packed_gains = jnp.concatenate([gain.astype(jnp.float32) for gain in raw_gains])[None]
    query_dp, pair_dp, out_dp, gains_dp = exchange(
        (query_slice, pair_slice, out_slice, packed_gains), ("gather",) * 4, "dp", dp, 0
    )
    gains_dp = gains_dp[:, 0]
    gain_in, gain_query, gain_key, gain_attn, gain_pre, gain_post = (
        gains_dp[:, low:high].reshape(-1) for low, high in zip(cuts[:-1], cuts[1:])
    )
    query_all, pair_all, out_all, tokens_all = exchange(
        (query_dp.reshape(-1, query_columns), pair_dp, out_dp, tokens),
        ("gather",) * 4,
        "ctx",
        ctx,
        1,
    )
    query_full = from_columns(query_all)
    pair_full = jnp.transpose(pair_all, (1, 0, 2, 3)).reshape(-1, 2 * kwidth)
    key_full = pair_full[:, :kwidth]
    value_full = pair_full[:, kwidth:]
    out_full = jnp.transpose(out_all, (1, 0, 2, 3)).reshape(-1, out_weight.shape[1])

    inputs_f = tokens.astype(jnp.float32)
    inv_one = inverse_rms(inputs_f)
    normed_one = (inputs_f * inv_one * gain_in).astype(bf16)
    all_f = tokens_all.reshape(-1, width).astype(jnp.float32)
    normed_all = (all_f * inverse_rms(all_f) * gain_in).astype(bf16)
    key_pos = jnp.arange(all_f.shape[0], dtype=jnp.int32)
    queries = matmul(normed_one, query_full).reshape(rows, HEADS, HEAD)
    keys = matmul(normed_one, key_full)
    keys_every = matmul(normed_all, key_full)
    value_all = matmul(normed_all, value_full).astype(bf16)
    inv_query = inverse_rms(queries)
    inv_key = inverse_rms(keys)
    query_rot = (
        rotate(queries * inv_query * gain_query, cosine[:, None, :], sine[:, None, :]) * scaling
    ).astype(bf16)
    key_all = rotate(
        keys_every * inverse_rms(keys_every) * gain_key, cosine_all, sine_all
    ).astype(bf16)
    allowed = (query_pos[:, None] >= key_pos[None, :])[None]
    scores = jnp.einsum("qhd,kd->hqk", query_rot, key_all, preferred_element_type=jnp.float32)
    scores = jnp.where(allowed, scores, NEG_FILL)
    row_max = jnp.max(scores, axis=-1, keepdims=True)
    weights = jnp.where(allowed, jnp.exp(scores - row_max), 0.0)
    total = jnp.sum(weights, axis=-1, keepdims=True)
    accum = jnp.einsum(
        "hqk,kd->hqd", weights.astype(bf16), value_all, preferred_element_type=jnp.float32
    )
    attn_heads = jnp.transpose(accum / total, (1, 0, 2)).astype(bf16)
    attn_out = attn_heads.reshape(rows, HEADS * HEAD)
    projected = matmul(attn_out, out_full)
    inv_proj = inverse_rms(projected)
    residual = inputs_f + projected * inv_proj * gain_attn
    inv_two = inverse_rms(residual)
    normed_two = (residual * inv_two * gain_pre).astype(bf16)

    rows_all, attn_all = exchange((normed_two, attn_out), ("gather",) * 2, "ctx", ctx, 2)
    gains = gain_block(
        [gain_in, gain_query, gain_key, gain_attn, gain_pre, gains_dp[:, cuts[-2] :].reshape(-1)], width
    )
    return (
        residual,
        projected,
        queries.reshape(rows, HEADS * HEAD),
        keys,
        query_rot.reshape(rows, HEADS * HEAD),
        attn_out,
        key_all,
        value_all,
        gains,
        normed_all,
        query_full,
        pair_full,
        out_full,
        rows_all,
        attn_all,
    )


def on_device(
    dp,
    ctx,
    tokens,
    in_gain,
    query_weight,
    key_weight,
    value_weight,
    query_gain,
    key_gain,
    out_weight,
    attn_post_gain,
    ffn_pre_gain,
    gate_weight,
    up_weight,
    down_weight,
    ffn_post_gain,
    cotangent,
):
    rows, width = tokens.shape
    bf16 = jnp.bfloat16
    qwidth = query_weight.shape[1]
    kwidth = key_weight.shape[1]
    out_columns = out_weight.shape[1] // ctx
    query_columns = qwidth // ctx
    pair = jnp.concatenate([key_weight, value_weight], axis=1)
    raw_gains = (in_gain, query_gain, key_gain, attn_post_gain, ffn_pre_gain, ffn_post_gain)
    cuts = [0]
    for gain in raw_gains:
        cuts.append(cuts[-1] + gain.shape[0])
    key_pos = jnp.arange(ctx * rows, dtype=jnp.int32)
    cosine_all, sine_all = rope_tables(key_pos.astype(jnp.float32))
    gate_full, up_full, down_full = (
        lax.all_gather(gate_weight, "dp", axis=0, tiled=True),
        lax.all_gather(up_weight, "dp", axis=0, tiled=True),
        lax.all_gather(down_weight, "dp", axis=0, tiled=True),
    )
    if fits_front(query_weight.shape[0], qwidth, 2 * kwidth, out_weight.shape[0], ctx):
        gain_rows = gain_block([spread_gain(gain, dp) for gain in raw_gains], width)
        (
            residual,
            projected,
            queries,
            keys,
            query_rot,
            attn_out,
            key_all,
            value_all,
            gains,
            normed_all,
            query_full,
            pair_full,
            out_full,
            rows_all,
            attn_all,
        ) = attn_front(
            tokens, query_weight, pair, out_weight, gain_rows, cosine_all, sine_all, dp, ctx, 10
        )
    else:
        (
            residual,
            projected,
            queries,
            keys,
            query_rot,
            attn_out,
            key_all,
            value_all,
            gains,
            normed_all,
            query_full,
            pair_full,
            out_full,
            rows_all,
            attn_all,
        ) = plain_front(
            tokens, query_weight, pair, out_weight, raw_gains, cuts, cosine_all, sine_all, dp, ctx
        )
    normed_all = normed_all.reshape(-1, width)
    attn_all = attn_all.reshape(-1, qwidth)
    rows_all = rows_all.reshape(-1, width)
    gate = matmul(rows_all, gate_full)
    upper = matmul(rows_all, up_full)
    gelu_val, gelu_der = gelu_pair(gate)
    hidden = (gelu_val * upper).astype(bf16)
    ffn_part = matmul_nt(hidden, down_full).astype(bf16).reshape(ctx, rows, width)
    block_out, grad_post, grad_all = ffn_turn(
        ffn_part, residual, cotangent, gains[3:4], "ctx", ctx, 3
    )
    grad_all = grad_all.reshape(-1, width)
    down_part, grad_all = lax.optimization_barrier(
        (by_rows(matmul_tn(grad_all, hidden).astype(bf16)), grad_all)
    )
    down_shard = lax.psum_scatter(down_part, "dp", scatter_dimension=0, tiled=True)
    down_shard = down_shard.astype(jnp.float32)
    hidden_grad = matmul(grad_all, down_full)
    gate_grad = (hidden_grad * upper * gelu_der).astype(bf16)
    up_grad = (hidden_grad * gelu_val).astype(bf16)
    gate_part = by_rows(matmul_tn(rows_all, gate_grad).astype(bf16))
    up_part = by_rows(matmul_tn(rows_all, up_grad).astype(bf16))
    gate_shard = lax.psum_scatter(gate_part, "dp", scatter_dimension=0, tiled=True)
    gate_shard = gate_shard.astype(jnp.float32)
    up_shard = lax.psum_scatter(up_part, "dp", scatter_dimension=0, tiled=True)
    up_shard = up_shard.astype(jnp.float32)
    two_part = (matmul_nt(gate_grad, gate_full) + matmul_nt(up_grad, up_full)).astype(bf16)
    input_grad, query_cols, pair_cols, proj_cols, all_gains = attn_back(
        two_part.reshape(ctx, rows, width),
        residual,
        cotangent,
        projected,
        tokens,
        gains,
        out_full,
        query_full,
        pair_full,
        attn_out,
        query_rot,
        key_all,
        value_all,
        queries,
        keys,
        cosine_all,
        sine_all,
        grad_post,
        "ctx",
        ctx,
        5,
    )
    gain_sums = jnp.sum(all_gains, axis=0)
    gain_grads = (
        gain_sums[0],
        gain_sums[4, :HEAD],
        gain_sums[5, :HEAD],
        gain_sums[1],
        gain_sums[2],
        gain_sums[3],
    )
    packed = jnp.concatenate([grad.reshape(dp, -1) for grad in gain_grads], axis=1)
    query_w = matmul_tn(normed_all, query_cols.reshape(-1, query_columns)).astype(bf16)
    pair_w = matmul_tn(normed_all, pair_cols.reshape(normed_all.shape[0], -1)).astype(bf16)
    out_w = matmul_tn(attn_all, proj_cols.reshape(-1, out_columns)).astype(bf16)
    query_w, pair_w, out_w, gain_parts = exchange(
        (
            query_w.reshape(dp, -1, query_columns),
            pair_w.reshape(dp, -1, pair_w.shape[1]),
            out_w.reshape(dp, -1, out_columns),
            packed[:, None],
        ),
        ("swap",) * 4,
        "dp",
        dp,
        8,
    )
    query_w, pair_w, out_w = exchange(
        (sum_blocks(query_w).astype(bf16), sum_blocks(pair_w).astype(bf16), sum_blocks(out_w).astype(bf16)),
        ("gather",) * 3,
        "ctx",
        ctx,
        9,
    )
    query_w = from_columns(query_w).astype(jnp.float32)
    pair_w = from_columns(pair_w).astype(jnp.float32)
    out_w = from_columns(out_w).astype(jnp.float32)
    gain_done = sum_blocks(gain_parts).reshape(-1)
    share = [gain_done[low:high] for low, high in zip(cuts[:-1], cuts[1:])]
    return (
        block_out,
        input_grad,
        share[0],
        query_w,
        pair_w[:, :kwidth],
        pair_w[:, kwidth:],
        share[1],
        share[2],
        out_w,
        share[3],
        share[4],
        gate_shard,
        up_shard,
        down_shard,
        share[5],
    )


def solution(mesh):
    return jax.shard_map(
        functools.partial(on_device, mesh.shape["dp"], mesh.shape["ctx"]),
        mesh=mesh,
        in_specs=(
            P(("dp", "ctx"), None),
            P("dp"),
            P("dp", None),
            P("dp", None),
            P("dp", None),
            P("dp"),
            P("dp"),
            P("dp", None),
            P("dp"),
            P("dp"),
            P("dp", "ctx"),
            P("dp", "ctx"),
            P("dp", "ctx"),
            P("dp"),
            P(("dp", "ctx"), None),
        ),
        out_specs=(
            P(("dp", "ctx"), None),
            P(("dp", "ctx"), None),
            P("dp"),
            P("dp", None),
            P("dp", None),
            P("dp", None),
            P("dp"),
            P("dp"),
            P("dp", None),
            P("dp"),
            P("dp"),
            P("dp", "ctx"),
            P("dp", "ctx"),
            P("dp", "ctx"),
            P("dp"),
        ),
        check_vma=False,
    )
```

```python
import functools
import math

import jax
import jax.numpy as jnp
from jax import lax
from jax.experimental import pallas as pl
from jax.experimental.layout import Layout, with_layout_constraint
from jax.experimental.pallas import tpu as pltpu
from jax.sharding import PartitionSpec as P

HEADS = 4
HEAD = 256


EPS = 1e-06
GELU_C = math.sqrt(2.0 / math.pi)
NEG_FILL = -1e30


def inverse_rms(values):
    return lax.rsqrt(jnp.mean(values * values, axis=-1, keepdims=True) + EPS)


def norm_back(values, scale_inv, gain, grad_out):
    weighted = grad_out * gain
    cubed = scale_inv * scale_inv * scale_inv
    return scale_inv * weighted - values * cubed * jnp.mean(
        weighted * values, axis=-1, keepdims=True
    )


def gelu_pair(values):
    inner = GELU_C * (values + 0.044715 * values * values * values)
    tanh_val = jnp.tanh(inner)
    result = 0.5 * values * (1.0 + tanh_val)
    slope = 0.5 * (1.0 + tanh_val) + 0.5 * values * (1.0 - tanh_val * tanh_val) * GELU_C * (
        1.0 + 3.0 * 0.044715 * values * values
    )
    return (result, slope)


def rotate(values, cosine, sine):
    middle = values.shape[-1] // 2
    first = values[..., :middle]
    second = values[..., middle:]
    return jnp.concatenate(
        [first * cosine - second * sine, second * cosine + first * sine], axis=-1
    )


def unrotate(grads, cosine, sine):
    middle = grads.shape[-1] // 2
    first = grads[..., :middle]
    second = grads[..., middle:]
    return jnp.concatenate(
        [first * cosine + second * sine, second * cosine - first * sine], axis=-1
    )


def rope_tables(positions):
    middle = HEAD // 2
    freqs = jnp.exp(-(2.0 * jnp.arange(middle, dtype=jnp.float32) / HEAD) * math.log(1000000.0))
    angles = positions[:, None] * freqs[None, :]
    return (jnp.cos(angles), jnp.sin(angles))


def matmul(left, right):
    return jnp.dot(left, right, preferred_element_type=jnp.float32)


def matmul_tn(left, right):
    return lax.dot_general(
        left, right, (((0,), (0,)), ((), ())), preferred_element_type=jnp.float32
    )


def matmul_nt(left, right):
    return lax.dot_general(
        left, right, (((1,), (1,)), ((), ())), preferred_element_type=jnp.float32
    )


MESH = pl.DeviceIdType.MESH


def swap_kernel(size, axis, kinds, *refs):
    count = len(kinds)
    ins, outs, kept = refs[:count], refs[count : 2 * count], refs[2 * count : 3 * count]
    send, recv, local = refs[3 * count :]
    me = lax.axis_index(axis)
    own = []
    for item, kind in enumerate(kinds):
        source = ins[item].at[me] if kind == "swap" else ins[item]
        own.append(pltpu.make_async_copy(source, kept[item], local.at[item, 0]))
        own[-1].start()
    barrier = pltpu.get_barrier_semaphore()
    for step in range(1, size):
        peer = lax.rem(me + step, size)
        pl.semaphore_signal(barrier, inc=1, device_id={axis: peer}, device_id_type=MESH)
    pl.semaphore_wait(barrier, size - 1)
    copies = []
    for item, kind in enumerate(kinds):
        for step in range(1, size):
            peer = lax.rem(me + step, size)
            source = ins[item].at[peer] if kind == "swap" else ins[item]
            copy = pltpu.make_async_remote_copy(
                src_ref=source,
                dst_ref=outs[item].at[me],
                send_sem=send.at[item, step - 1],
                recv_sem=recv.at[item, step - 1],
                device_id={axis: peer},
                device_id_type=MESH,
            )
            copy.start()
            copies.append(copy)
    for item in range(count):
        own[item].wait()
        copy = pltpu.make_async_copy(kept[item], outs[item].at[me], local.at[item, 1])
        copy.start()
        copies.append(copy)
    for copy in copies:
        copy.wait()


def chunks_of(rows):
    for parts in (4, 3, 2):
        if rows % (16 * parts) == 0:
            return parts
    return 1


def pair_gather_kernel(size, axis, kinds, *refs):
    count = len(kinds)
    ins, outs, kept = refs[:count], refs[count : 2 * count], refs[2 * count : 3 * count]
    send, recv, pass_send, pass_recv, local = refs[3 * count :]
    me = lax.axis_index(axis)
    twin = me + 1 - 2 * lax.rem(me, 2)
    half = size // 2
    own = []
    for item in range(count):
        own.append(pltpu.make_async_copy(ins[item], kept[item], local.at[item, 0]))
        own[-1].start()
    barrier = pltpu.get_barrier_semaphore()
    for step in range(1, half):
        peer = lax.rem(me + 2 * step, size)
        pl.semaphore_signal(barrier, inc=1, device_id={axis: peer}, device_id_type=MESH)
    pl.semaphore_signal(barrier, inc=1, device_id={axis: twin}, device_id_type=MESH)
    pl.semaphore_wait(barrier, half)
    pieces = []
    for item in range(count):
        rows = ins[item].shape[0]
        pieces += [
            (item, part, pl.ds(part * (rows // chunks_of(rows)), rows // chunks_of(rows)))
            for part in range(chunks_of(rows))
        ]
    across, last = [], []
    for item, part, span in pieces:
        for step in range(1, half):
            copy = pltpu.make_async_remote_copy(
                src_ref=ins[item].at[span],
                dst_ref=outs[item].at[me, span],
                send_sem=send.at[item, step, part],
                recv_sem=recv.at[item, step, part],
                device_id={axis: lax.rem(me + 2 * step, size)},
                device_id_type=MESH,
            )
            copy.start()
            across.append((copy, item, step, part, span))
    for item, part, span in pieces:
        copy = pltpu.make_async_remote_copy(
            src_ref=ins[item].at[span],
            dst_ref=outs[item].at[me, span],
            send_sem=pass_send.at[item, 0, part],
            recv_sem=pass_recv.at[item, 0, part],
            device_id={axis: twin},
            device_id_type=MESH,
        )
        copy.start()
        last.append(copy)
    for item in range(count):
        own[item].wait()
        copy = pltpu.make_async_copy(kept[item], outs[item].at[me], local.at[item, 1])
        copy.start()
        last.append(copy)
    for arrived, item, step, part, span in across:
        arrived.wait_recv()
        origin = lax.rem(me + size - 2 * step, size)
        copy = pltpu.make_async_remote_copy(
            src_ref=outs[item].at[origin, span],
            dst_ref=outs[item].at[origin, span],
            send_sem=pass_send.at[item, step, part],
            recv_sem=pass_recv.at[item, step, part],
            device_id={axis: twin},
            device_id_type=MESH,
        )
        copy.start()
        last.append(copy)
    for sent, *_ in across:
        sent.wait_send()
    for copy in last:
        copy.wait()


def exchange(arrays, kinds, axis, size, ident):
    count = len(arrays)
    pairs = all(kind == "gather" for kind in kinds) and axis == "ctx" and size % 2 == 0
    shapes = tuple(
        jax.ShapeDtypeStruct(x.shape if kind == "swap" else (size,) + x.shape, x.dtype)
        for x, kind in zip(arrays, kinds)
    )
    dma = pltpu.SemaphoreType.DMA
    if pairs:
        half = size // 2
        parts = max(chunks_of(x.shape[0]) for x in arrays)
        scratch = [dma((count, half, parts))] * 4
        body = pair_gather_kernel
    else:
        scratch = [dma((count, size - 1))] * 2
        body = swap_kernel
    moved = sum(x.size * x.dtype.itemsize for x in shapes)
    return pl.pallas_call(
        functools.partial(body, size, axis, tuple(kinds)),
        out_shape=shapes,
        in_specs=[pl.BlockSpec(memory_space=pl.ANY)] * count,
        out_specs=tuple(pl.BlockSpec(memory_space=pl.ANY) for _ in arrays),
        scratch_shapes=[pltpu.VMEM(x.shape[1:], x.dtype) for x in shapes]
        + scratch
        + [dma((count, 2))],
        compiler_params=pltpu.CompilerParams(collective_id=ident, has_side_effects=True),
        cost_estimate=pl.CostEstimate(flops=0, bytes_accessed=20 * moved, transcendentals=0),
        name=f"exchange_{ident}",
    )(*arrays)


def pieces_of(rows):
    parts = chunks_of(rows)
    return [pl.ds(part * (rows // parts), rows // parts) for part in range(parts)]


def remote(source, target, send, recv, axis, peer):
    copy = pltpu.make_async_remote_copy(
        src_ref=source,
        dst_ref=target,
        send_sem=send,
        recv_sem=recv,
        device_id={axis: peer},
        device_id_type=MESH,
    )
    copy.start()
    return copy


class Place:
    def __init__(self, axis, size):
        self.axis, self.size, self.half = axis, size, size // 2
        self.me = lax.axis_index(axis)
        self.core = lax.rem(self.me, 2)
        self.twin = self.me + 1 - 2 * self.core

    def across(self, step):
        return lax.rem(self.me + 2 * step, self.size)

    def behind(self, step):
        return lax.rem(self.me + self.size - 2 * step, self.size)

    def greet_pairs(self):
        barrier = pltpu.get_barrier_semaphore()
        for step in range(1, self.half):
            pl.semaphore_signal(
                barrier, inc=1, device_id={self.axis: self.across(step)}, device_id_type=MESH
            )
        pl.semaphore_signal(barrier, inc=1, device_id={self.axis: self.twin}, device_id_type=MESH)
        pl.semaphore_wait(barrier, self.half)

    def greet_all(self):
        barrier = pltpu.get_barrier_semaphore()
        for step in range(1, self.size):
            peer = lax.rem(self.me + step, self.size)
            pl.semaphore_signal(barrier, inc=1, device_id={self.axis: peer}, device_id_type=MESH)
        pl.semaphore_wait(barrier, self.size - 1)


def scatter_scratch(size, rows, width):
    half, parts, dma = size // 2, chunks_of(rows), pltpu.SemaphoreType.DMA
    block = lambda count: pltpu.VMEM((count, rows, width), jnp.bfloat16)
    return [block(half), block(half), block(half - 1), block(half - 1), dma((half,))] + [
        dma((half, parts))
    ] * 4


class Scatter:
    def __init__(self, place, part, scratch):
        self.place, self.part = place, part
        self.kept, self.twins, self.summed, self.landed = scratch[:4]
        self.local, self.twin_send, self.twin_recv, self.send, self.recv = scratch[4:]
        self.spans = pieces_of(self.kept.shape[1])

    def load(self):
        place = self.place
        self.loads = []
        for slot in range(place.half):
            copy = pltpu.make_async_copy(
                self.part.at[place.across(slot)], self.kept.at[slot], self.local.at[slot]
            )
            copy.start()
            self.loads.append(copy)

    def start(self):
        place = self.place
        self.twin_copies, self.copies = {}, {}
        slots = list(range(1, place.half)) + [0]
        for index, span in enumerate(self.spans):
            for slot in slots:
                self.twin_copies[slot, index] = remote(
                    self.part.at[place.across(slot) + 1 - 2 * place.core, span],
                    self.twins.at[slot, span],
                    self.twin_send.at[slot, index],
                    self.twin_recv.at[slot, index],
                    place.axis,
                    place.twin,
                )
        for copy in self.loads:
            copy.wait()
        for index, span in enumerate(self.spans):
            for slot in slots[:-1]:
                self.twin_copies[slot, index].wait_recv()
                self.summed[slot - 1, span] = (
                    self.kept[slot, span].astype(jnp.float32)
                    + self.twins[slot, span].astype(jnp.float32)
                ).astype(jnp.bfloat16)
                self.copies[slot, index] = remote(
                    self.summed.at[slot - 1, span],
                    self.landed.at[slot - 1, span],
                    self.send.at[slot, index],
                    self.recv.at[slot, index],
                    place.axis,
                    place.across(slot),
                )

    def total(self, index):
        span = self.spans[index]
        self.twin_copies[0, index].wait_recv()
        value = self.kept[0, span].astype(jnp.float32) + self.twins[0, span].astype(jnp.float32)
        for slot in range(1, self.place.half):
            self.copies[slot, index].wait_recv()
            value = value + self.landed[slot - 1, span].astype(jnp.float32)
        return value

    def finish(self):
        for copy in list(self.twin_copies.values()) + list(self.copies.values()):
            copy.wait_send()


def gather_scratch(size, rows):
    dma = pltpu.SemaphoreType.DMA
    return [dma((size // 2, chunks_of(rows)))] * 4 + [dma((chunks_of(rows),))]


class Gather:
    def __init__(self, place, source, target, scratch):
        self.place, self.source, self.target = place, source, target
        self.send, self.recv, self.pass_send, self.pass_recv, self.local = scratch
        self.spans = pieces_of(source.shape[0])
        self.across, self.last = [], []

    def start(self, index):
        place, span = self.place, self.spans[index]
        for step in range(1, place.half):
            copy = remote(
                self.source.at[span],
                self.target.at[place.me, span],
                self.send.at[step, index],
                self.recv.at[step, index],
                place.axis,
                place.across(step),
            )
            self.across.append((copy, step, index))
        self.last.append(
            remote(
                self.source.at[span],
                self.target.at[place.me, span],
                self.pass_send.at[0, index],
                self.pass_recv.at[0, index],
                place.axis,
                place.twin,
            )
        )
        copy = pltpu.make_async_copy(
            self.source.at[span], self.target.at[place.me, span], self.local.at[index]
        )
        copy.start()
        self.last.append(copy)

    def relay(self):
        place = self.place
        for copy, step, index in self.across:
            copy.wait_recv()
            block = self.target.at[place.behind(step), self.spans[index]]
            self.last.append(
                remote(
                    block,
                    block,
                    self.pass_send.at[step, index],
                    self.pass_recv.at[step, index],
                    place.axis,
                    place.twin,
                )
            )

    def finish(self):
        for copy, *_ in self.across:
            copy.wait_send()
        for copy in self.last:
            copy.wait()


def ffn_turn_kernel(axis, size, part, residual, cot, gain, block_out, gain_grad, gathered, grad, *scratch):
    place = Place(axis, size)
    scatter = Scatter(place, part, scratch[:9])
    gather = Gather(place, grad, gathered, scratch[9:])
    scatter.load()
    place.greet_pairs()
    scatter.start()
    gain_row = gain[...]
    for index, span in enumerate(scatter.spans):
        ffn_sum = scatter.total(index)
        inverse = inverse_rms(ffn_sum)
        incoming = cot[span].astype(jnp.float32)
        grad[span] = norm_back(ffn_sum, inverse, gain_row, incoming).astype(jnp.bfloat16)
        gather.start(index)
        scaled = ffn_sum * inverse
        block_out[span] = (residual[span] + scaled * gain_row).astype(jnp.bfloat16)
        share = jnp.sum(incoming * scaled, axis=0, keepdims=True)
        gain_grad[...] = share if index == 0 else gain_grad[...] + share
    gather.relay()
    scatter.finish()
    gather.finish()


def ffn_turn(part, residual, cotangent, gain, axis, size, ident):
    rows, width = residual.shape
    whole = pl.BlockSpec(memory_space=pltpu.VMEM)
    away = pl.BlockSpec(memory_space=pl.ANY)
    return pl.pallas_call(
        functools.partial(ffn_turn_kernel, axis, size),
        out_shape=(
            jax.ShapeDtypeStruct((rows, width), jnp.bfloat16),
            jax.ShapeDtypeStruct((1, width), jnp.float32),
            jax.ShapeDtypeStruct((size, rows, width), jnp.bfloat16),
        ),
        in_specs=[away, whole, whole, whole],
        out_specs=(whole, whole, away),
        scratch_shapes=[pltpu.VMEM((rows, width), jnp.bfloat16)]
        + scatter_scratch(size, rows, width)
        + gather_scratch(size, rows),
        compiler_params=pltpu.CompilerParams(collective_id=ident, has_side_effects=True),
        cost_estimate=pl.CostEstimate(
            flops=0, bytes_accessed=20 * part.size * 2, transcendentals=0
        ),
        name=f"ffn_turn_{ident}",
    )(part, residual, cotangent, gain)


def attn_back_kernel(
    axis,
    size,
    part,
    residual,
    cot,
    projected,
    tokens,
    gains,
    out_hbm,
    query_hbm,
    pair_hbm,
    attn_out,
    query_rot,
    key_hbm,
    value_hbm,
    queries,
    keys,
    cosine,
    sine,
    post_grad,
    input_grad,
    query_cols,
    pair_cols,
    proj_cols,
    all_gains,
    out_w,
    query_w,
    pair_w,
    key_all,
    value_all,
    res_grad,
    proj_grad,
    stacked_p,
    stacked_s,
    stacked_g,
    stacked_q,
    pair_part,
    query_grad,
    query_send,
    pair_send,
    proj_send,
    gain_send,
    local,
    send,
    recv,
    *scratch,
):
    rows, width = residual.shape
    total_keys = key_all.shape[0]
    bf16, f32 = jnp.bfloat16, jnp.float32
    scaling = 1.0 / math.sqrt(HEAD)
    place = Place(axis, size)
    me = place.me
    two = Scatter(place, part, scratch[:9])
    pairs = Scatter(place, pair_part, scratch[9:])
    two.load()
    loads = []
    for source, target in (
        (out_hbm, out_w),
        (key_hbm, key_all),
        (value_hbm, value_all),
        (query_hbm, query_w),
        (pair_hbm, pair_w),
    ):
        copy = pltpu.make_async_copy(source, target, local.at[len(loads)])
        copy.start()
        loads.append(copy)
    place.greet_all()
    two.start()
    swaps = []

    def swap(item, source, target):
        for step in range(1, size):
            peer = lax.rem(me + step, size)
            swaps.append(
                remote(
                    source.at[peer],
                    target.at[me],
                    send.at[item, step - 1],
                    recv.at[item, step - 1],
                    axis,
                    peer,
                )
            )
        copy = pltpu.make_async_copy(source.at[me], target.at[me], local.at[len(loads) + item])
        copy.start()
        swaps.append(copy)

    gain_in, gain_attn, gain_pre = gains[0:1], gains[1:2], gains[2:3]
    gain_query, gain_key = gains[4:5, :HEAD], gains[4:5, HEAD : 2 * HEAD]
    here = pl.ds(pl.multiple_of(me * rows, rows), rows)
    cos_here, sin_here = cosine[here], sine[here]
    gain_send[...] = jnp.zeros_like(gain_send)
    gain_send[3:4] = post_grad[...]
    proj_width = width // size
    for index, span in enumerate(two.spans):
        two_grad = two.total(index)
        kept = residual[span]
        inv_two = inverse_rms(kept)
        back = cot[span].astype(f32) + norm_back(kept, inv_two, gain_pre, two_grad)
        res_grad[span] = back
        ahead = projected[span]
        inv_proj = inverse_rms(ahead)
        proj_back = norm_back(ahead, inv_proj, gain_attn, back)
        proj_grad[span] = proj_back.astype(bf16)
        for peer in range(size):
            proj_send[peer, span] = proj_back[:, peer * proj_width : (peer + 1) * proj_width].astype(
                bf16
            )
        gain_send[2:3] += jnp.sum(two_grad * kept * inv_two, axis=0, keepdims=True)
        gain_send[1:2] += jnp.sum(back * ahead * inv_proj, axis=0, keepdims=True)
    swap(0, proj_send, proj_cols)
    loads[0].wait()
    query_grad[...] = matmul_nt(proj_grad[...], out_w[...]).astype(bf16)
    loads[1].wait()
    loads[2].wait()

    def probabilities(head, carry):
        lanes = pl.ds(pl.multiple_of(head * HEAD, HEAD), HEAD)
        level = pl.ds(pl.multiple_of(head * rows, rows), rows)
        query_pos = me * rows + lax.broadcasted_iota(jnp.int32, (rows, total_keys), 0)
        allowed = query_pos >= lax.broadcasted_iota(jnp.int32, (rows, total_keys), 1)
        query = query_rot[:, lanes]
        incoming = query_grad[:, lanes]
        scores = jnp.where(allowed, matmul_nt(query, key_all[...]), NEG_FILL)
        weights = jnp.where(
            allowed, jnp.exp(scores - jnp.max(scores, axis=-1, keepdims=True)), 0.0
        )
        probs = weights / jnp.sum(weights, axis=-1, keepdims=True)
        delta = jnp.sum(
            incoming.astype(f32) * attn_out[:, lanes].astype(f32), axis=-1, keepdims=True
        )
        prob_grad = matmul_nt(incoming, value_all[...])
        stacked_s[level] = (probs * (prob_grad - delta)).astype(bf16)
        stacked_p[level] = probs.astype(bf16)
        stacked_g[level] = incoming
        stacked_q[level] = query
        return carry

    lax.fori_loop(0, HEADS, probabilities, 0)
    values_part = matmul_tn(stacked_p[...], stacked_g[...]).astype(bf16)
    keys_part = matmul_tn(stacked_s[...], stacked_q[...]).astype(bf16)
    for peer in range(size):
        block = slice(peer * rows, (peer + 1) * rows)
        pair_part[peer, :, :HEAD] = keys_part[block]
        pair_part[peer, :, HEAD:] = values_part[block]
    pairs.load()
    pairs.start()
    query_width = HEADS * HEAD // size

    def query_back(head, share):
        lanes = pl.ds(pl.multiple_of(head * HEAD, HEAD), HEAD)
        level = pl.ds(pl.multiple_of(head * rows, rows), rows)
        normed_grad = unrotate(
            matmul(stacked_s[level], key_all[...]) * scaling, cosine[here], sine[here]
        )
        value = queries[:, lanes]
        inverse = inverse_rms(value)
        query_grad[:, lanes] = norm_back(value, inverse, gain_query, normed_grad).astype(bf16)
        return share + jnp.sum(normed_grad * value * inverse, axis=0, keepdims=True)

    gain_share = lax.fori_loop(0, HEADS, query_back, jnp.zeros((1, HEAD), f32))
    for peer in range(size):
        query_send[peer] = query_grad[:, peer * query_width : (peer + 1) * query_width]
    swap(1, query_send, query_cols)
    gain_send[4:5, :HEAD] = gain_share
    loads[3].wait()
    input_grad[...] = matmul_nt(query_grad[...], query_w[...])
    loads[4].wait()
    pair_width = 2 * HEAD // size
    key_share = jnp.zeros((1, HEAD), f32)
    for index, span in enumerate(pairs.spans):
        pair_total = pairs.total(index)
        near = slice(span.start, span.start + span.size)
        normed_grad = unrotate(pair_total[:, :HEAD], cos_here[near], sin_here[near])
        value = keys[span]
        inverse = inverse_rms(value)
        key_share = key_share + jnp.sum(normed_grad * value * inverse, axis=0, keepdims=True)
        both = jnp.concatenate(
            [norm_back(value, inverse, gain_key, normed_grad), pair_total[:, HEAD:]], axis=1
        )
        for peer in range(size):
            pair_send[peer, span] = both[:, peer * pair_width : (peer + 1) * pair_width].astype(bf16)
        one_grad = input_grad[span] + matmul_nt(both.astype(bf16), pair_w[...])
        inputs = tokens[span].astype(f32)
        inv_one = inverse_rms(inputs)
        gain_send[0:1] += jnp.sum(one_grad * inputs * inv_one, axis=0, keepdims=True)
        input_grad[span] = res_grad[span] + norm_back(inputs, inv_one, gain_in, one_grad)
    gain_send[5:6, :HEAD] = key_share
    swap(2, pair_send, pair_cols)
    for step in range(1, size):
        peer = lax.rem(me + step, size)
        swaps.append(
            remote(
                gain_send,
                all_gains.at[me],
                send.at[3, step - 1],
                recv.at[3, step - 1],
                axis,
                peer,
            )
        )
    copy = pltpu.make_async_copy(gain_send, all_gains.at[me], local.at[len(loads) + 3])
    copy.start()
    swaps.append(copy)
    two.finish()
    pairs.finish()
    for copy in swaps:
        copy.wait()


def attn_back(
    part,
    residual,
    cotangent,
    projected,
    tokens,
    gains,
    out_full,
    query_full,
    pair_full,
    attn_out,
    query_rot,
    key_all,
    value_all,
    queries,
    keys,
    cosine,
    sine,
    post_grad,
    axis,
    size,
    ident,
):
    rows, width = residual.shape
    bf16, f32 = jnp.bfloat16, jnp.float32
    whole = pl.BlockSpec(memory_space=pltpu.VMEM)
    away = pl.BlockSpec(memory_space=pl.ANY)
    qwidth, total_keys = query_full.shape[1], key_all.shape[0]
    query_cols = (size, rows, qwidth // size)
    pair_cols = (size, rows, 2 * HEAD // size)
    proj_cols = (size, rows, width // size)
    dma = pltpu.SemaphoreType.DMA
    return pl.pallas_call(
        functools.partial(attn_back_kernel, axis, size),
        out_shape=(
            jax.ShapeDtypeStruct((rows, width), f32),
            jax.ShapeDtypeStruct(query_cols, bf16),
            jax.ShapeDtypeStruct(pair_cols, bf16),
            jax.ShapeDtypeStruct(proj_cols, bf16),
            jax.ShapeDtypeStruct((size, 8, width), f32),
        ),
        in_specs=[away]
        + [whole] * 5
        + [away] * 3
        + [whole] * 2
        + [away] * 2
        + [whole] * 5,
        out_specs=(whole, away, away, away, away),
        scratch_shapes=[
            pltpu.VMEM(out_full.shape, bf16),
            pltpu.VMEM(query_full.shape, bf16),
            pltpu.VMEM(pair_full.shape, bf16),
            pltpu.VMEM(key_all.shape, bf16),
            pltpu.VMEM(value_all.shape, bf16),
            pltpu.VMEM((rows, width), f32),
            pltpu.VMEM((rows, width), bf16),
            pltpu.VMEM((HEADS * rows, total_keys), bf16),
            pltpu.VMEM((HEADS * rows, total_keys), bf16),
            pltpu.VMEM((HEADS * rows, HEAD), bf16),
            pltpu.VMEM((HEADS * rows, HEAD), bf16),
            pltpu.VMEM((size, rows, 2 * HEAD), bf16),
            pltpu.VMEM((rows, qwidth), bf16),
            pltpu.VMEM(query_cols, bf16),
            pltpu.VMEM(pair_cols, bf16),
            pltpu.VMEM(proj_cols, bf16),
            pltpu.VMEM((8, width), f32),
            dma((9,)),
            dma((4, size - 1)),
            dma((4, size - 1)),
        ]
        + scatter_scratch(size, rows, width)
        + scatter_scratch(size, rows, 2 * HEAD),
        compiler_params=pltpu.CompilerParams(collective_id=ident, has_side_effects=True),
        cost_estimate=pl.CostEstimate(
            flops=0, bytes_accessed=30 * part.size * 2, transcendentals=0
        ),
        name=f"attn_back_{ident}",
    )(
        part,
        residual,
        cotangent,
        projected,
        tokens,
        gains,
        out_full,
        query_full,
        pair_full,
        attn_out,
        query_rot,
        key_all,
        value_all,
        queries,
        keys,
        cosine,
        sine,
        post_grad,
    )


def attn_front_kernel(
    dp,
    ctx,
    tokens,
    query_in,
    pair_in,
    out_in,
    gains_in,
    cosine,
    sine,
    residual,
    projected,
    queries,
    keys,
    query_rot,
    attn_out,
    key_all,
    value_all,
    gains,
    normed_hbm,
    query_hbm,
    pair_hbm,
    out_hbm,
    rows_all,
    attn_all,
    tokens_all,
    normed_all,
    query_w,
    pair_w,
    out_w,
    keys_all,
    gains_all,
    normed_two,
    local,
    far_send,
    far_recv,
    near_send,
    near_recv,
    pass_send,
    pass_recv,
    *scratch,
):
    rows, width = tokens.shape
    total_keys = key_all.shape[0]
    bf16, f32 = jnp.bfloat16, jnp.float32
    scaling = 1.0 / math.sqrt(HEAD)
    place = Place("ctx", ctx)
    me, row = place.me, lax.axis_index("dp")
    shard = query_in.shape[0]
    query_width = query_w.shape[1] // ctx
    pair_depth, pair_width = pair_in.shape
    out_shard = out_in.shape[0]
    out_depth = out_shard // ctx

    def query_region(source, base, origin):
        return source.at[
            pl.ds(pl.multiple_of(base * shard, 16), shard),
            pl.ds(pl.multiple_of(origin * query_width, 128), query_width),
        ]

    def pair_region(base, origin):
        start = base * shard + lax.rem(origin, 2) * pair_depth
        return pair_w.at[
            pl.ds(pl.multiple_of(start, 16), pair_depth),
            pl.ds(pl.multiple_of((origin // 2) * pair_width, 128), pair_width),
        ]

    def out_region(source, base, origin):
        start = base * out_shard + origin * out_depth
        return source.at[pl.ds(pl.multiple_of(start, 16), out_depth)]

    regions = (
        pair_region,
        functools.partial(query_region, query_w),
        functools.partial(out_region, out_w),
    )
    sources = (pair_in, query_region(query_in, 0, me), out_region(out_in, 0, me))
    pending = []

    def stay(source, target, index):
        copy = pltpu.make_async_copy(source, target, local.at[index])
        copy.start()
        return copy

    own = [stay(sources[item], regions[item](row, me), item) for item in range(3)]
    own.append(stay(gains_in, gains_all.at[row], 3))
    barrier = pltpu.get_barrier_semaphore()
    for step in range(1, place.half):
        pl.semaphore_signal(
            barrier, inc=1, device_id={"ctx": place.across(step)}, device_id_type=MESH
        )
    pl.semaphore_signal(barrier, inc=1, device_id={"ctx": place.twin}, device_id_type=MESH)
    for step in range(1, dp):
        pl.semaphore_signal(
            barrier, inc=1, device_id={"dp": lax.rem(row + step, dp)}, device_id_type=MESH
        )
    pl.semaphore_wait(barrier, place.half + dp - 1)

    far, near = {}, {}
    for item in (3, 0, 1, 2):
        for step in range(1, dp):
            far[item, step] = remote(
                gains_in if item == 3 else sources[item],
                gains_all.at[row] if item == 3 else regions[item](row, me),
                far_send.at[item, step - 1],
                far_recv.at[item, step - 1],
                "dp",
                lax.rem(row + step, dp),
            )
    token_gather = Gather(place, tokens, tokens_all, scratch[:5])
    row_gather = Gather(place, normed_two, rows_all, scratch[5:10])
    attn_gather = Gather(place, attn_out, attn_all, scratch[10:15])
    for index in range(len(token_gather.spans)):
        token_gather.start(index)

    def spread(item, lag):
        base = lax.rem(row + dp - lag, dp)
        if lag:
            far[item, lag].wait_recv()
        source = regions[item](base, me) if lag else sources[item]
        target = regions[item](base, me)
        for step in range(1, place.half):
            near[item, lag, step] = remote(
                source,
                target,
                near_send.at[item, lag, step],
                near_recv.at[item, lag, step],
                "ctx",
                place.across(step),
            )
        pending.append(
            remote(
                source,
                target,
                pass_send.at[item, lag, 0],
                pass_recv.at[item, lag, 0],
                "ctx",
                place.twin,
            )
        )
        item_passes[item].append(pending[-1])

    def relay(item):
        for lag in range(dp):
            base = lax.rem(row + dp - lag, dp)
            for step in range(1, place.half):
                near[item, lag, step].wait_recv()
                block = regions[item](base, place.behind(step))
                pending.append(
                    remote(
                        block,
                        block,
                        pass_send.at[item, lag, step],
                        pass_recv.at[item, lag, step],
                        "ctx",
                        place.twin,
                    )
                )
                item_passes[item].append(pending[-1])

    def complete(item):
        for copy in item_passes[item]:
            copy.wait_recv()
        own[item].wait()

    item_passes = ([], [], [])
    for item in range(3):
        spread(item, 0)
    token_gather.relay()
    for lag in range(1, dp):
        spread(0, lag)
    for step in range(1, dp):
        far[3, step].wait_recv()
    own[3].wait()
    total = gains_all[0]
    for step in range(1, dp):
        total = total + gains_all[step]
    gains[...] = total
    token_gather.finish()

    def normalize(block, carry):
        value = tokens_all[block].astype(f32)
        normed_all[block] = (value * inverse_rms(value) * gains[0:1]).astype(bf16)
        return carry

    lax.fori_loop(0, ctx, normalize, 0)
    saves = [stay(normed_all, normed_hbm, 4)]
    for lag in range(1, dp):
        spread(1, lag)
    relay(0)
    for lag in range(1, dp):
        spread(2, lag)
    complete(0)
    saves.append(stay(pair_w, pair_hbm, 5))

    def project(block, carry):
        both = matmul(normed_all[block], pair_w[...])
        value = both[:, :HEAD]
        turn = pl.ds(pl.multiple_of(block * rows, rows), rows)
        keys_all[block] = value
        key_all[turn] = rotate(
            value * inverse_rms(value) * gains[4:5, HEAD : 2 * HEAD], cosine[turn], sine[turn]
        ).astype(bf16)
        value_all[turn] = both[:, HEAD:].astype(bf16)
        return carry

    lax.fori_loop(0, ctx, project, 0)
    keys[...] = keys_all[me]
    relay(1)
    complete(1)
    saves.append(stay(query_w, query_hbm, 6))
    queries[...] = matmul(normed_all[me], query_w[...])
    here = pl.ds(pl.multiple_of(me * rows, rows), rows)

    def attend(head, carry):
        lanes = pl.ds(pl.multiple_of(head * HEAD, HEAD), HEAD)
        query_pos = me * rows + lax.broadcasted_iota(jnp.int32, (rows, total_keys), 0)
        allowed = query_pos >= lax.broadcasted_iota(jnp.int32, (rows, total_keys), 1)
        value = queries[:, lanes]
        query = (
            rotate(value * inverse_rms(value) * gains[4:5, :HEAD], cosine[here], sine[here])
            * scaling
        ).astype(bf16)
        query_rot[:, lanes] = query
        scores = jnp.where(allowed, matmul_nt(query, key_all[...]), NEG_FILL)
        weights = jnp.where(
            allowed, jnp.exp(scores - jnp.max(scores, axis=-1, keepdims=True)), 0.0
        )
        attn_out[:, lanes] = (
            matmul(weights.astype(bf16), value_all[...]) / jnp.sum(weights, axis=-1, keepdims=True)
        ).astype(bf16)
        return carry

    lax.fori_loop(0, HEADS, attend, 0)
    relay(2)
    complete(2)
    saves.append(stay(out_w, out_hbm, 7))
    projected[...] = matmul(attn_out[...], out_w[...])
    for index, span in enumerate(row_gather.spans):
        ahead = projected[span]
        kept = tokens[span].astype(f32) + ahead * inverse_rms(ahead) * gains[1:2]
        residual[span] = kept
        normed_two[span] = (kept * inverse_rms(kept) * gains[2:3]).astype(bf16)
        row_gather.start(index)
    for index in range(len(attn_gather.spans)):
        attn_gather.start(index)
    row_gather.relay()
    attn_gather.relay()
    row_gather.finish()
    attn_gather.finish()
    for copy in list(far.values()) + list(near.values()) + pending:
        copy.wait_send()
    for copy in saves:
        copy.wait()


def attn_front(tokens, query_weight, pair, out_weight, gain_rows, cosine, sine, dp, ctx, ident):
    rows, width = tokens.shape
    shard, qwidth = query_weight.shape
    half = ctx // 2
    pair_depth, pair_width = shard // 2, pair.shape[1] // half
    index = lax.axis_index("ctx")
    pair_slice = lax.dynamic_slice(
        pair, (lax.rem(index, 2) * pair_depth, index // 2 * pair_width), (pair_depth, pair_width)
    )
    bf16, f32 = jnp.bfloat16, jnp.float32
    whole = pl.BlockSpec(memory_space=pltpu.VMEM)
    away = pl.BlockSpec(memory_space=pl.ANY)
    dma = pltpu.SemaphoreType.DMA
    vmem, shape = pltpu.VMEM, jax.ShapeDtypeStruct
    query_full, pair_full = (dp * shard, qwidth), (dp * shard, pair.shape[1])
    out_full = (dp * out_weight.shape[0], width)
    return pl.pallas_call(
        functools.partial(attn_front_kernel, dp, ctx),
        out_shape=(
            shape((rows, width), f32),
            shape((rows, width), f32),
            shape((rows, qwidth), f32),
            shape((rows, HEAD), f32),
            shape((rows, qwidth), bf16),
            shape((rows, qwidth), bf16),
            shape((ctx * rows, HEAD), bf16),
            shape((ctx * rows, HEAD), bf16),
            shape((8, width), f32),
            shape((ctx, rows, width), bf16),
            shape(query_full, bf16),
            shape(pair_full, bf16),
            shape(out_full, bf16),
            shape((ctx, rows, width), bf16),
            shape((ctx, rows, qwidth), bf16),
        ),
        in_specs=[whole, away, whole, away, whole, whole, whole],
        out_specs=(whole,) * 9 + (away,) * 6,
        scratch_shapes=[
            vmem((ctx, rows, width), bf16),
            vmem((ctx, rows, width), bf16),
            vmem(query_full, bf16),
            vmem(pair_full, bf16),
            vmem(out_full, bf16),
            vmem((ctx, rows, HEAD), f32),
            vmem((dp, 8, width), f32),
            vmem((rows, width), bf16),
            dma((8,)),
            dma((4, dp - 1)),
            dma((4, dp - 1)),
        ]
        + [dma((3, dp, half))] * 4
        + gather_scratch(ctx, rows) * 3,
        compiler_params=pltpu.CompilerParams(collective_id=ident, has_side_effects=True),
        cost_estimate=pl.CostEstimate(
            flops=0, bytes_accessed=100 * ctx * rows * width, transcendentals=0
        ),
        name=f"attn_front_{ident}",
    )(tokens, query_weight, pair_slice, out_weight, gain_rows, cosine, sine)


def fits_front(shard, qwidth, pair_width, out_shard, ctx):
    return (
        ctx % 2 == 0
        and qwidth % (128 * ctx) == 0
        and pair_width % (64 * ctx) == 0
        and shard % 32 == 0
        and out_shard % (16 * ctx) == 0
    )


def gain_block(gains, width):
    gain_in, gain_query, gain_key, gain_attn, gain_pre, gain_post = gains
    heads = jnp.concatenate([gain_query, gain_key])
    heads = jnp.pad(heads, (0, width - heads.shape[0]))
    stacked = jnp.stack([gain_in, gain_attn, gain_pre, gain_post, heads])
    return jnp.pad(stacked, ((0, 3), (0, 0)))


def spread_gain(gain, dp):
    place = jnp.arange(dp * gain.shape[0], dtype=jnp.int32) // gain.shape[0]
    tiled = jnp.tile(gain.astype(jnp.float32), dp)
    return jnp.where(place == lax.axis_index("dp"), tiled, 0.0)


def by_rows(array):
    return with_layout_constraint(array, Layout(major_to_minor=(0, 1)))


def by_columns(array, parts):
    rows, columns = array.shape
    return jnp.transpose(array.reshape(rows, parts, columns // parts), (1, 0, 2))


def from_columns(array):
    parts, rows, columns = array.shape
    return jnp.transpose(array, (1, 0, 2)).reshape(rows, parts * columns)


def sum_blocks(array):
    return jnp.sum(array.astype(jnp.float32), axis=0)


def plain_front(
    tokens, query_weight, pair, out_weight, raw_gains, cuts, cosine_all, sine_all, dp, ctx
):
    rows, width = tokens.shape
    bf16 = jnp.bfloat16
    scaling = 1.0 / math.sqrt(HEAD)
    ctx_index = lax.axis_index("ctx")
    query_pos = ctx_index * rows + jnp.arange(rows, dtype=jnp.int32)
    cosine = lax.dynamic_slice_in_dim(cosine_all, ctx_index * rows, rows, 0)
    sine = lax.dynamic_slice_in_dim(sine_all, ctx_index * rows, rows, 0)
    kwidth = pair.shape[1] // 2
    query_columns = query_weight.shape[1] // ctx
    pair_rows = pair.shape[0] // ctx
    out_rows = out_weight.shape[0] // ctx
    query_slice = lax.dynamic_slice_in_dim(query_weight, ctx_index * query_columns, query_columns, 1)
    pair_slice = lax.dynamic_slice_in_dim(pair, ctx_index * pair_rows, pair_rows, 0)
    out_slice = lax.dynamic_slice_in_dim(out_weight, ctx_index * out_rows, out_rows, 0)
    packed_gains = jnp.concatenate([gain.astype(jnp.float32) for gain in raw_gains])[None]
    query_dp, pair_dp, out_dp, gains_dp = exchange(
        (query_slice, pair_slice, out_slice, packed_gains), ("gather",) * 4, "dp", dp, 0
    )
    gains_dp = gains_dp[:, 0]
    gain_in, gain_query, gain_key, gain_attn, gain_pre, gain_post = (
        gains_dp[:, low:high].reshape(-1) for low, high in zip(cuts[:-1], cuts[1:])
    )
    query_all, pair_all, out_all, tokens_all = exchange(
        (query_dp.reshape(-1, query_columns), pair_dp, out_dp, tokens),
        ("gather",) * 4,
        "ctx",
        ctx,
        1,
    )
    query_full = from_columns(query_all)
    pair_full = jnp.transpose(pair_all, (1, 0, 2, 3)).reshape(-1, 2 * kwidth)
    key_full = pair_full[:, :kwidth]
    value_full = pair_full[:, kwidth:]
    out_full = jnp.transpose(out_all, (1, 0, 2, 3)).reshape(-1, out_weight.shape[1])

    inputs_f = tokens.astype(jnp.float32)
    inv_one = inverse_rms(inputs_f)
    normed_one = (inputs_f * inv_one * gain_in).astype(bf16)
    all_f = tokens_all.reshape(-1, width).astype(jnp.float32)
    normed_all = (all_f * inverse_rms(all_f) * gain_in).astype(bf16)
    key_pos = jnp.arange(all_f.shape[0], dtype=jnp.int32)
    queries = matmul(normed_one, query_full).reshape(rows, HEADS, HEAD)
    keys = matmul(normed_one, key_full)
    keys_every = matmul(normed_all, key_full)
    value_all = matmul(normed_all, value_full).astype(bf16)
    inv_query = inverse_rms(queries)
    inv_key = inverse_rms(keys)
    query_rot = (
        rotate(queries * inv_query * gain_query, cosine[:, None, :], sine[:, None, :]) * scaling
    ).astype(bf16)
    key_all = rotate(
        keys_every * inverse_rms(keys_every) * gain_key, cosine_all, sine_all
    ).astype(bf16)
    allowed = (query_pos[:, None] >= key_pos[None, :])[None]
    scores = jnp.einsum("qhd,kd->hqk", query_rot, key_all, preferred_element_type=jnp.float32)
    scores = jnp.where(allowed, scores, NEG_FILL)
    row_max = jnp.max(scores, axis=-1, keepdims=True)
    weights = jnp.where(allowed, jnp.exp(scores - row_max), 0.0)
    total = jnp.sum(weights, axis=-1, keepdims=True)
    accum = jnp.einsum(
        "hqk,kd->hqd", weights.astype(bf16), value_all, preferred_element_type=jnp.float32
    )
    attn_heads = jnp.transpose(accum / total, (1, 0, 2)).astype(bf16)
    attn_out = attn_heads.reshape(rows, HEADS * HEAD)
    projected = matmul(attn_out, out_full)
    inv_proj = inverse_rms(projected)
    residual = inputs_f + projected * inv_proj * gain_attn
    inv_two = inverse_rms(residual)
    normed_two = (residual * inv_two * gain_pre).astype(bf16)

    rows_all, attn_all = exchange((normed_two, attn_out), ("gather",) * 2, "ctx", ctx, 2)
    gains = gain_block(
        [gain_in, gain_query, gain_key, gain_attn, gain_pre, gains_dp[:, cuts[-2] :].reshape(-1)], width
    )
    return (
        residual,
        projected,
        queries.reshape(rows, HEADS * HEAD),
        keys,
        query_rot.reshape(rows, HEADS * HEAD),
        attn_out,
        key_all,
        value_all,
        gains,
        normed_all,
        query_full,
        pair_full,
        out_full,
        rows_all,
        attn_all,
    )


def on_device(
    dp,
    ctx,
    tokens,
    in_gain,
    query_weight,
    key_weight,
    value_weight,
    query_gain,
    key_gain,
    out_weight,
    attn_post_gain,
    ffn_pre_gain,
    gate_weight,
    up_weight,
    down_weight,
    ffn_post_gain,
    cotangent,
):
    rows, width = tokens.shape
    bf16 = jnp.bfloat16
    qwidth = query_weight.shape[1]
    kwidth = key_weight.shape[1]
    out_columns = out_weight.shape[1] // ctx
    query_columns = qwidth // ctx
    pair = jnp.concatenate([key_weight, value_weight], axis=1)
    raw_gains = (in_gain, query_gain, key_gain, attn_post_gain, ffn_pre_gain, ffn_post_gain)
    cuts = [0]
    for gain in raw_gains:
        cuts.append(cuts[-1] + gain.shape[0])
    key_pos = jnp.arange(ctx * rows, dtype=jnp.int32)
    cosine_all, sine_all = rope_tables(key_pos.astype(jnp.float32))
    gate_full, up_full, down_full = (
        lax.all_gather(gate_weight, "dp", axis=0, tiled=True),
        lax.all_gather(up_weight, "dp", axis=0, tiled=True),
        lax.all_gather(down_weight, "dp", axis=0, tiled=True),
    )
    if fits_front(query_weight.shape[0], qwidth, 2 * kwidth, out_weight.shape[0], ctx):
        gain_rows = gain_block([spread_gain(gain, dp) for gain in raw_gains], width)
        (
            residual,
            projected,
            queries,
            keys,
            query_rot,
            attn_out,
            key_all,
            value_all,
            gains,
            normed_all,
            query_full,
            pair_full,
            out_full,
            rows_all,
            attn_all,
        ) = attn_front(
            tokens, query_weight, pair, out_weight, gain_rows, cosine_all, sine_all, dp, ctx, 10
        )
    else:
        (
            residual,
            projected,
            queries,
            keys,
            query_rot,
            attn_out,
            key_all,
            value_all,
            gains,
            normed_all,
            query_full,
            pair_full,
            out_full,
            rows_all,
            attn_all,
        ) = plain_front(
            tokens, query_weight, pair, out_weight, raw_gains, cuts, cosine_all, sine_all, dp, ctx
        )
    normed_all = normed_all.reshape(-1, width)
    attn_all = attn_all.reshape(-1, qwidth)
    rows_all = rows_all.reshape(-1, width)
    gate = matmul(rows_all, gate_full)
    upper = matmul(rows_all, up_full)
    gelu_val, gelu_der = gelu_pair(gate)
    hidden = (gelu_val * upper).astype(bf16)
    ffn_part = matmul_nt(hidden, down_full).astype(bf16).reshape(ctx, rows, width)
    block_out, grad_post, grad_all = ffn_turn(
        ffn_part, residual, cotangent, gains[3:4], "ctx", ctx, 3
    )
    grad_all = grad_all.reshape(-1, width)
    down_part, grad_all = lax.optimization_barrier(
        (by_rows(matmul_tn(grad_all, hidden).astype(bf16)), grad_all)
    )
    down_shard = lax.psum_scatter(down_part, "dp", scatter_dimension=0, tiled=True)
    down_shard = down_shard.astype(jnp.float32)
    hidden_grad = matmul(grad_all, down_full)
    gate_grad = (hidden_grad * upper * gelu_der).astype(bf16)
    up_grad = (hidden_grad * gelu_val).astype(bf16)
    gate_part = by_rows(matmul_tn(rows_all, gate_grad).astype(bf16))
    up_part = by_rows(matmul_tn(rows_all, up_grad).astype(bf16))
    gate_shard = lax.psum_scatter(gate_part, "dp", scatter_dimension=0, tiled=True)
    gate_shard = gate_shard.astype(jnp.float32)
    two_part = (matmul_nt(gate_grad, gate_full) + matmul_nt(up_grad, up_full)).astype(bf16)
    input_grad, query_cols, pair_cols, proj_cols, all_gains = attn_back(
        two_part.reshape(ctx, rows, width),
        residual,
        cotangent,
        projected,
        tokens,
        gains,
        out_full,
        query_full,
        pair_full,
        attn_out,
        query_rot,
        key_all,
        value_all,
        queries,
        keys,
        cosine_all,
        sine_all,
        grad_post,
        "ctx",
        ctx,
        5,
    )
    gain_sums = jnp.sum(all_gains, axis=0)
    gain_grads = (
        gain_sums[0],
        gain_sums[4, :HEAD],
        gain_sums[5, :HEAD],
        gain_sums[1],
        gain_sums[2],
        gain_sums[3],
    )
    packed = jnp.concatenate([grad.reshape(dp, -1) for grad in gain_grads], axis=1)
    query_w = matmul_tn(normed_all, query_cols.reshape(-1, query_columns)).astype(bf16)
    pair_w = matmul_tn(normed_all, pair_cols.reshape(normed_all.shape[0], -1)).astype(bf16)
    out_w = matmul_tn(attn_all, proj_cols.reshape(-1, out_columns)).astype(bf16)
    query_w, pair_w, out_w, gain_parts = exchange(
        (
            query_w.reshape(dp, -1, query_columns),
            pair_w.reshape(dp, -1, pair_w.shape[1]),
            out_w.reshape(dp, -1, out_columns),
            packed[:, None],
        ),
        ("swap",) * 4,
        "dp",
        dp,
        8,
    )
    up_part, query_w, pair_w, out_w = lax.optimization_barrier((up_part, query_w, pair_w, out_w))
    up_shard = lax.psum_scatter(up_part, "dp", scatter_dimension=0, tiled=True)
    up_shard = up_shard.astype(jnp.float32)
    query_w, pair_w, out_w = exchange(
        (sum_blocks(query_w).astype(bf16), sum_blocks(pair_w).astype(bf16), sum_blocks(out_w).astype(bf16)),
        ("gather",) * 3,
        "ctx",
        ctx,
        9,
    )
    query_w = from_columns(query_w).astype(jnp.float32)
    pair_w = from_columns(pair_w).astype(jnp.float32)
    out_w = from_columns(out_w).astype(jnp.float32)
    gain_done = sum_blocks(gain_parts).reshape(-1)
    share = [gain_done[low:high] for low, high in zip(cuts[:-1], cuts[1:])]
    return (
        block_out,
        input_grad,
        share[0],
        query_w,
        pair_w[:, :kwidth],
        pair_w[:, kwidth:],
        share[1],
        share[2],
        out_w,
        share[3],
        share[4],
        gate_shard,
        up_shard,
        down_shard,
        share[5],
    )


def solution(mesh):
    return jax.shard_map(
        functools.partial(on_device, mesh.shape["dp"], mesh.shape["ctx"]),
        mesh=mesh,
        in_specs=(
            P(("dp", "ctx"), None),
            P("dp"),
            P("dp", None),
            P("dp", None),
            P("dp", None),
            P("dp"),
            P("dp"),
            P("dp", None),
            P("dp"),
            P("dp"),
            P("dp", "ctx"),
            P("dp", "ctx"),
            P("dp", "ctx"),
            P("dp"),
            P(("dp", "ctx"), None),
        ),
        out_specs=(
            P(("dp", "ctx"), None),
            P(("dp", "ctx"), None),
            P("dp"),
            P("dp", None),
            P("dp", None),
            P("dp", None),
            P("dp"),
            P("dp"),
            P("dp", None),
            P("dp"),
            P("dp"),
            P("dp", "ctx"),
            P("dp", "ctx"),
            P("dp", "ctx"),
            P("dp"),
        ),
        check_vma=False,
    )
```

```python
import functools
import math

import jax
import jax.numpy as jnp
from jax import lax
from jax.experimental import pallas as pl
from jax.experimental.layout import Layout, with_layout_constraint
from jax.experimental.pallas import tpu as pltpu
from jax.sharding import PartitionSpec as P

HEADS = 4
HEAD = 256


EPS = 1e-06
GELU_C = math.sqrt(2.0 / math.pi)
NEG_FILL = -1e30


def inverse_rms(values):
    return lax.rsqrt(jnp.mean(values * values, axis=-1, keepdims=True) + EPS)


def norm_back(values, scale_inv, gain, grad_out):
    weighted = grad_out * gain
    cubed = scale_inv * scale_inv * scale_inv
    return scale_inv * weighted - values * cubed * jnp.mean(
        weighted * values, axis=-1, keepdims=True
    )


def gelu_pair(values):
    inner = GELU_C * (values + 0.044715 * values * values * values)
    tanh_val = jnp.tanh(inner)
    result = 0.5 * values * (1.0 + tanh_val)
    slope = 0.5 * (1.0 + tanh_val) + 0.5 * values * (1.0 - tanh_val * tanh_val) * GELU_C * (
        1.0 + 3.0 * 0.044715 * values * values
    )
    return (result, slope)


def rotate(values, cosine, sine):
    middle = values.shape[-1] // 2
    first = values[..., :middle]
    second = values[..., middle:]
    return jnp.concatenate(
        [first * cosine - second * sine, second * cosine + first * sine], axis=-1
    )


def unrotate(grads, cosine, sine):
    middle = grads.shape[-1] // 2
    first = grads[..., :middle]
    second = grads[..., middle:]
    return jnp.concatenate(
        [first * cosine + second * sine, second * cosine - first * sine], axis=-1
    )


def rope_tables(positions):
    middle = HEAD // 2
    freqs = jnp.exp(-(2.0 * jnp.arange(middle, dtype=jnp.float32) / HEAD) * math.log(1000000.0))
    angles = positions[:, None] * freqs[None, :]
    return (jnp.cos(angles), jnp.sin(angles))


def matmul(left, right):
    return jnp.dot(left, right, preferred_element_type=jnp.float32)


def matmul_tn(left, right):
    return lax.dot_general(
        left, right, (((0,), (0,)), ((), ())), preferred_element_type=jnp.float32
    )


def matmul_nt(left, right):
    return lax.dot_general(
        left, right, (((1,), (1,)), ((), ())), preferred_element_type=jnp.float32
    )


MESH = pl.DeviceIdType.MESH


def swap_kernel(size, axis, kinds, *refs):
    count = len(kinds)
    ins, outs, kept = refs[:count], refs[count : 2 * count], refs[2 * count : 3 * count]
    send, recv, local = refs[3 * count :]
    me = lax.axis_index(axis)
    own = []
    for item, kind in enumerate(kinds):
        source = ins[item].at[me] if kind == "swap" else ins[item]
        own.append(pltpu.make_async_copy(source, kept[item], local.at[item, 0]))
        own[-1].start()
    barrier = pltpu.get_barrier_semaphore()
    for step in range(1, size):
        peer = lax.rem(me + step, size)
        pl.semaphore_signal(barrier, inc=1, device_id={axis: peer}, device_id_type=MESH)
    pl.semaphore_wait(barrier, size - 1)
    copies = []
    for item, kind in enumerate(kinds):
        for step in range(1, size):
            peer = lax.rem(me + step, size)
            source = ins[item].at[peer] if kind == "swap" else ins[item]
            copy = pltpu.make_async_remote_copy(
                src_ref=source,
                dst_ref=outs[item].at[me],
                send_sem=send.at[item, step - 1],
                recv_sem=recv.at[item, step - 1],
                device_id={axis: peer},
                device_id_type=MESH,
            )
            copy.start()
            copies.append(copy)
    for item in range(count):
        own[item].wait()
        copy = pltpu.make_async_copy(kept[item], outs[item].at[me], local.at[item, 1])
        copy.start()
        copies.append(copy)
    for copy in copies:
        copy.wait()


def chunks_of(rows):
    for parts in (4, 3, 2):
        if rows % (16 * parts) == 0:
            return parts
    return 1


def pair_gather_kernel(size, axis, kinds, *refs):
    count = len(kinds)
    ins, outs, kept = refs[:count], refs[count : 2 * count], refs[2 * count : 3 * count]
    send, recv, pass_send, pass_recv, local = refs[3 * count :]
    me = lax.axis_index(axis)
    twin = me + 1 - 2 * lax.rem(me, 2)
    half = size // 2
    own = []
    for item in range(count):
        own.append(pltpu.make_async_copy(ins[item], kept[item], local.at[item, 0]))
        own[-1].start()
    barrier = pltpu.get_barrier_semaphore()
    for step in range(1, half):
        peer = lax.rem(me + 2 * step, size)
        pl.semaphore_signal(barrier, inc=1, device_id={axis: peer}, device_id_type=MESH)
    pl.semaphore_signal(barrier, inc=1, device_id={axis: twin}, device_id_type=MESH)
    pl.semaphore_wait(barrier, half)
    pieces = []
    for item in range(count):
        rows = ins[item].shape[0]
        pieces += [
            (item, part, pl.ds(part * (rows // chunks_of(rows)), rows // chunks_of(rows)))
            for part in range(chunks_of(rows))
        ]
    across, last = [], []
    for item, part, span in pieces:
        for step in range(1, half):
            copy = pltpu.make_async_remote_copy(
                src_ref=ins[item].at[span],
                dst_ref=outs[item].at[me, span],
                send_sem=send.at[item, step, part],
                recv_sem=recv.at[item, step, part],
                device_id={axis: lax.rem(me + 2 * step, size)},
                device_id_type=MESH,
            )
            copy.start()
            across.append((copy, item, step, part, span))
    for item, part, span in pieces:
        copy = pltpu.make_async_remote_copy(
            src_ref=ins[item].at[span],
            dst_ref=outs[item].at[me, span],
            send_sem=pass_send.at[item, 0, part],
            recv_sem=pass_recv.at[item, 0, part],
            device_id={axis: twin},
            device_id_type=MESH,
        )
        copy.start()
        last.append(copy)
    for item in range(count):
        own[item].wait()
        copy = pltpu.make_async_copy(kept[item], outs[item].at[me], local.at[item, 1])
        copy.start()
        last.append(copy)
    for arrived, item, step, part, span in across:
        arrived.wait_recv()
        origin = lax.rem(me + size - 2 * step, size)
        copy = pltpu.make_async_remote_copy(
            src_ref=outs[item].at[origin, span],
            dst_ref=outs[item].at[origin, span],
            send_sem=pass_send.at[item, step, part],
            recv_sem=pass_recv.at[item, step, part],
            device_id={axis: twin},
            device_id_type=MESH,
        )
        copy.start()
        last.append(copy)
    for sent, *_ in across:
        sent.wait_send()
    for copy in last:
        copy.wait()


def exchange(arrays, kinds, axis, size, ident):
    count = len(arrays)
    pairs = all(kind == "gather" for kind in kinds) and axis == "ctx" and size % 2 == 0
    shapes = tuple(
        jax.ShapeDtypeStruct(x.shape if kind == "swap" else (size,) + x.shape, x.dtype)
        for x, kind in zip(arrays, kinds)
    )
    dma = pltpu.SemaphoreType.DMA
    if pairs:
        half = size // 2
        parts = max(chunks_of(x.shape[0]) for x in arrays)
        scratch = [dma((count, half, parts))] * 4
        body = pair_gather_kernel
    else:
        scratch = [dma((count, size - 1))] * 2
        body = swap_kernel
    moved = sum(x.size * x.dtype.itemsize for x in shapes)
    return pl.pallas_call(
        functools.partial(body, size, axis, tuple(kinds)),
        out_shape=shapes,
        in_specs=[pl.BlockSpec(memory_space=pl.ANY)] * count,
        out_specs=tuple(pl.BlockSpec(memory_space=pl.ANY) for _ in arrays),
        scratch_shapes=[pltpu.VMEM(x.shape[1:], x.dtype) for x in shapes]
        + scratch
        + [dma((count, 2))],
        compiler_params=pltpu.CompilerParams(collective_id=ident, has_side_effects=True),
        cost_estimate=pl.CostEstimate(flops=0, bytes_accessed=20 * moved, transcendentals=0),
        name=f"exchange_{ident}",
    )(*arrays)


def pieces_of(rows):
    parts = chunks_of(rows)
    return [pl.ds(part * (rows // parts), rows // parts) for part in range(parts)]


def remote(source, target, send, recv, axis, peer):
    copy = pltpu.make_async_remote_copy(
        src_ref=source,
        dst_ref=target,
        send_sem=send,
        recv_sem=recv,
        device_id={axis: peer},
        device_id_type=MESH,
    )
    copy.start()
    return copy


class Place:
    def __init__(self, axis, size):
        self.axis, self.size, self.half = axis, size, size // 2
        self.me = lax.axis_index(axis)
        self.core = lax.rem(self.me, 2)
        self.twin = self.me + 1 - 2 * self.core

    def across(self, step):
        return lax.rem(self.me + 2 * step, self.size)

    def behind(self, step):
        return lax.rem(self.me + self.size - 2 * step, self.size)

    def greet_pairs(self):
        barrier = pltpu.get_barrier_semaphore()
        for step in range(1, self.half):
            pl.semaphore_signal(
                barrier, inc=1, device_id={self.axis: self.across(step)}, device_id_type=MESH
            )
        pl.semaphore_signal(barrier, inc=1, device_id={self.axis: self.twin}, device_id_type=MESH)
        pl.semaphore_wait(barrier, self.half)

    def greet_all(self):
        barrier = pltpu.get_barrier_semaphore()
        for step in range(1, self.size):
            peer = lax.rem(self.me + step, self.size)
            pl.semaphore_signal(barrier, inc=1, device_id={self.axis: peer}, device_id_type=MESH)
        pl.semaphore_wait(barrier, self.size - 1)


def scatter_scratch(size, rows, width):
    half, parts, dma = size // 2, chunks_of(rows), pltpu.SemaphoreType.DMA
    block = lambda count: pltpu.VMEM((count, rows, width), jnp.bfloat16)
    return [block(half), block(half), block(half - 1), block(half - 1), dma((half,))] + [
        dma((half, parts))
    ] * 4


class Scatter:
    def __init__(self, place, part, scratch):
        self.place, self.part = place, part
        self.kept, self.twins, self.summed, self.landed = scratch[:4]
        self.local, self.twin_send, self.twin_recv, self.send, self.recv = scratch[4:]
        self.spans = pieces_of(self.kept.shape[1])

    def load(self):
        place = self.place
        self.loads = []
        for slot in range(place.half):
            copy = pltpu.make_async_copy(
                self.part.at[place.across(slot)], self.kept.at[slot], self.local.at[slot]
            )
            copy.start()
            self.loads.append(copy)

    def start(self):
        place = self.place
        self.twin_copies, self.copies = {}, {}
        slots = list(range(1, place.half)) + [0]
        for index, span in enumerate(self.spans):
            for slot in slots:
                self.twin_copies[slot, index] = remote(
                    self.part.at[place.across(slot) + 1 - 2 * place.core, span],
                    self.twins.at[slot, span],
                    self.twin_send.at[slot, index],
                    self.twin_recv.at[slot, index],
                    place.axis,
                    place.twin,
                )
        for copy in self.loads:
            copy.wait()
        for index, span in enumerate(self.spans):
            for slot in slots[:-1]:
                self.twin_copies[slot, index].wait_recv()
                self.summed[slot - 1, span] = (
                    self.kept[slot, span].astype(jnp.float32)
                    + self.twins[slot, span].astype(jnp.float32)
                ).astype(jnp.bfloat16)
                self.copies[slot, index] = remote(
                    self.summed.at[slot - 1, span],
                    self.landed.at[slot - 1, span],
                    self.send.at[slot, index],
                    self.recv.at[slot, index],
                    place.axis,
                    place.across(slot),
                )

    def total(self, index):
        span = self.spans[index]
        self.twin_copies[0, index].wait_recv()
        value = self.kept[0, span].astype(jnp.float32) + self.twins[0, span].astype(jnp.float32)
        for slot in range(1, self.place.half):
            self.copies[slot, index].wait_recv()
            value = value + self.landed[slot - 1, span].astype(jnp.float32)
        return value

    def finish(self):
        for copy in list(self.twin_copies.values()) + list(self.copies.values()):
            copy.wait_send()


def gather_scratch(size, rows):
    dma = pltpu.SemaphoreType.DMA
    return [dma((size // 2, chunks_of(rows)))] * 4 + [dma((chunks_of(rows),))]


class Gather:
    def __init__(self, place, source, target, scratch):
        self.place, self.source, self.target = place, source, target
        self.send, self.recv, self.pass_send, self.pass_recv, self.local = scratch
        self.spans = pieces_of(source.shape[0])
        self.across, self.last = [], []

    def start(self, index):
        place, span = self.place, self.spans[index]
        for step in range(1, place.half):
            copy = remote(
                self.source.at[span],
                self.target.at[place.me, span],
                self.send.at[step, index],
                self.recv.at[step, index],
                place.axis,
                place.across(step),
            )
            self.across.append((copy, step, index))
        self.last.append(
            remote(
                self.source.at[span],
                self.target.at[place.me, span],
                self.pass_send.at[0, index],
                self.pass_recv.at[0, index],
                place.axis,
                place.twin,
            )
        )
        copy = pltpu.make_async_copy(
            self.source.at[span], self.target.at[place.me, span], self.local.at[index]
        )
        copy.start()
        self.last.append(copy)

    def relay(self):
        place = self.place
        for copy, step, index in self.across:
            copy.wait_recv()
            block = self.target.at[place.behind(step), self.spans[index]]
            self.last.append(
                remote(
                    block,
                    block,
                    self.pass_send.at[step, index],
                    self.pass_recv.at[step, index],
                    place.axis,
                    place.twin,
                )
            )

    def finish(self):
        for copy, *_ in self.across:
            copy.wait_send()
        for copy in self.last:
            copy.wait()


def ffn_turn_kernel(axis, size, part, residual, cot, gain, block_out, gain_grad, gathered, grad, *scratch):
    place = Place(axis, size)
    scatter = Scatter(place, part, scratch[:9])
    gather = Gather(place, grad, gathered, scratch[9:])
    scatter.load()
    place.greet_pairs()
    scatter.start()
    gain_row = gain[...]
    for index, span in enumerate(scatter.spans):
        ffn_sum = scatter.total(index)
        inverse = inverse_rms(ffn_sum)
        incoming = cot[span].astype(jnp.float32)
        grad[span] = norm_back(ffn_sum, inverse, gain_row, incoming).astype(jnp.bfloat16)
        gather.start(index)
        scaled = ffn_sum * inverse
        block_out[span] = (residual[span] + scaled * gain_row).astype(jnp.bfloat16)
        share = jnp.sum(incoming * scaled, axis=0, keepdims=True)
        gain_grad[...] = share if index == 0 else gain_grad[...] + share
    gather.relay()
    scatter.finish()
    gather.finish()


def ffn_turn(part, residual, cotangent, gain, axis, size, ident):
    rows, width = residual.shape
    whole = pl.BlockSpec(memory_space=pltpu.VMEM)
    away = pl.BlockSpec(memory_space=pl.ANY)
    return pl.pallas_call(
        functools.partial(ffn_turn_kernel, axis, size),
        out_shape=(
            jax.ShapeDtypeStruct((rows, width), jnp.bfloat16),
            jax.ShapeDtypeStruct((1, width), jnp.float32),
            jax.ShapeDtypeStruct((size, rows, width), jnp.bfloat16),
        ),
        in_specs=[away, whole, whole, whole],
        out_specs=(whole, whole, away),
        scratch_shapes=[pltpu.VMEM((rows, width), jnp.bfloat16)]
        + scatter_scratch(size, rows, width)
        + gather_scratch(size, rows),
        compiler_params=pltpu.CompilerParams(collective_id=ident, has_side_effects=True),
        cost_estimate=pl.CostEstimate(
            flops=0, bytes_accessed=20 * part.size * 2, transcendentals=0
        ),
        name=f"ffn_turn_{ident}",
    )(part, residual, cotangent, gain)


def attn_back_kernel(
    axis,
    size,
    part,
    residual,
    cot,
    projected,
    tokens,
    gains,
    out_hbm,
    query_hbm,
    pair_hbm,
    attn_out,
    query_rot,
    key_hbm,
    value_hbm,
    queries,
    keys,
    cosine,
    sine,
    post_grad,
    input_grad,
    query_cols,
    pair_cols,
    proj_cols,
    all_gains,
    out_w,
    query_w,
    pair_w,
    key_all,
    value_all,
    res_grad,
    proj_grad,
    stacked_p,
    stacked_s,
    stacked_g,
    stacked_q,
    pair_part,
    query_grad,
    query_send,
    pair_send,
    proj_send,
    gain_send,
    local,
    send,
    recv,
    *scratch,
):
    rows, width = residual.shape
    total_keys = key_all.shape[0]
    bf16, f32 = jnp.bfloat16, jnp.float32
    scaling = 1.0 / math.sqrt(HEAD)
    place = Place(axis, size)
    me = place.me
    two = Scatter(place, part, scratch[:9])
    pairs = Scatter(place, pair_part, scratch[9:])
    two.load()
    loads = []
    for source, target in (
        (out_hbm, out_w),
        (key_hbm, key_all),
        (value_hbm, value_all),
        (query_hbm, query_w),
        (pair_hbm, pair_w),
    ):
        copy = pltpu.make_async_copy(source, target, local.at[len(loads)])
        copy.start()
        loads.append(copy)
    place.greet_all()
    two.start()
    swaps = []

    def swap(item, source, target):
        for step in range(1, size):
            peer = lax.rem(me + step, size)
            swaps.append(
                remote(
                    source.at[peer],
                    target.at[me],
                    send.at[item, step - 1],
                    recv.at[item, step - 1],
                    axis,
                    peer,
                )
            )
        copy = pltpu.make_async_copy(source.at[me], target.at[me], local.at[len(loads) + item])
        copy.start()
        swaps.append(copy)

    gain_in, gain_attn, gain_pre = gains[0:1], gains[1:2], gains[2:3]
    gain_query, gain_key = gains[4:5, :HEAD], gains[4:5, HEAD : 2 * HEAD]
    here = pl.ds(pl.multiple_of(me * rows, rows), rows)
    cos_here, sin_here = cosine[here], sine[here]
    gain_send[...] = jnp.zeros_like(gain_send)
    gain_send[3:4] = post_grad[...]
    proj_width = width // size
    for index, span in enumerate(two.spans):
        two_grad = two.total(index)
        kept = residual[span]
        inv_two = inverse_rms(kept)
        back = cot[span].astype(f32) + norm_back(kept, inv_two, gain_pre, two_grad)
        res_grad[span] = back
        ahead = projected[span]
        inv_proj = inverse_rms(ahead)
        proj_back = norm_back(ahead, inv_proj, gain_attn, back)
        proj_grad[span] = proj_back.astype(bf16)
        for peer in range(size):
            proj_send[peer, span] = proj_back[:, peer * proj_width : (peer + 1) * proj_width].astype(
                bf16
            )
        gain_send[2:3] += jnp.sum(two_grad * kept * inv_two, axis=0, keepdims=True)
        gain_send[1:2] += jnp.sum(back * ahead * inv_proj, axis=0, keepdims=True)
    swap(0, proj_send, proj_cols)
    loads[0].wait()
    query_grad[...] = matmul_nt(proj_grad[...], out_w[...]).astype(bf16)
    loads[1].wait()
    loads[2].wait()

    def probabilities(head, carry):
        lanes = pl.ds(pl.multiple_of(head * HEAD, HEAD), HEAD)
        level = pl.ds(pl.multiple_of(head * rows, rows), rows)
        query_pos = me * rows + lax.broadcasted_iota(jnp.int32, (rows, total_keys), 0)
        allowed = query_pos >= lax.broadcasted_iota(jnp.int32, (rows, total_keys), 1)
        query = query_rot[:, lanes]
        incoming = query_grad[:, lanes]
        scores = jnp.where(allowed, matmul_nt(query, key_all[...]), NEG_FILL)
        weights = jnp.where(
            allowed, jnp.exp(scores - jnp.max(scores, axis=-1, keepdims=True)), 0.0
        )
        probs = weights / jnp.sum(weights, axis=-1, keepdims=True)
        delta = jnp.sum(
            incoming.astype(f32) * attn_out[:, lanes].astype(f32), axis=-1, keepdims=True
        )
        prob_grad = matmul_nt(incoming, value_all[...])
        stacked_s[level] = (probs * (prob_grad - delta)).astype(bf16)
        stacked_p[level] = probs.astype(bf16)
        stacked_g[level] = incoming
        stacked_q[level] = query
        return carry

    lax.fori_loop(0, HEADS, probabilities, 0)
    values_part = matmul_tn(stacked_p[...], stacked_g[...]).astype(bf16)
    keys_part = matmul_tn(stacked_s[...], stacked_q[...]).astype(bf16)
    for peer in range(size):
        block = slice(peer * rows, (peer + 1) * rows)
        pair_part[peer, :, :HEAD] = keys_part[block]
        pair_part[peer, :, HEAD:] = values_part[block]
    pairs.load()
    pairs.start()
    query_width = HEADS * HEAD // size

    def query_back(head, share):
        lanes = pl.ds(pl.multiple_of(head * HEAD, HEAD), HEAD)
        level = pl.ds(pl.multiple_of(head * rows, rows), rows)
        normed_grad = unrotate(
            matmul(stacked_s[level], key_all[...]) * scaling, cosine[here], sine[here]
        )
        value = queries[:, lanes]
        inverse = inverse_rms(value)
        query_grad[:, lanes] = norm_back(value, inverse, gain_query, normed_grad).astype(bf16)
        return share + jnp.sum(normed_grad * value * inverse, axis=0, keepdims=True)

    gain_share = lax.fori_loop(0, HEADS, query_back, jnp.zeros((1, HEAD), f32))
    for peer in range(size):
        query_send[peer] = query_grad[:, peer * query_width : (peer + 1) * query_width]
    swap(1, query_send, query_cols)
    gain_send[4:5, :HEAD] = gain_share
    loads[3].wait()
    input_grad[...] = matmul_nt(query_grad[...], query_w[...])
    loads[4].wait()
    pair_width = 2 * HEAD // size
    key_share = jnp.zeros((1, HEAD), f32)
    for index, span in enumerate(pairs.spans):
        pair_total = pairs.total(index)
        near = slice(span.start, span.start + span.size)
        normed_grad = unrotate(pair_total[:, :HEAD], cos_here[near], sin_here[near])
        value = keys[span]
        inverse = inverse_rms(value)
        key_share = key_share + jnp.sum(normed_grad * value * inverse, axis=0, keepdims=True)
        both = jnp.concatenate(
            [norm_back(value, inverse, gain_key, normed_grad), pair_total[:, HEAD:]], axis=1
        )
        for peer in range(size):
            pair_send[peer, span] = both[:, peer * pair_width : (peer + 1) * pair_width].astype(bf16)
        one_grad = input_grad[span] + matmul_nt(both.astype(bf16), pair_w[...])
        inputs = tokens[span].astype(f32)
        inv_one = inverse_rms(inputs)
        gain_send[0:1] += jnp.sum(one_grad * inputs * inv_one, axis=0, keepdims=True)
        input_grad[span] = res_grad[span] + norm_back(inputs, inv_one, gain_in, one_grad)
    gain_send[5:6, :HEAD] = key_share
    swap(2, pair_send, pair_cols)
    for step in range(1, size):
        peer = lax.rem(me + step, size)
        swaps.append(
            remote(
                gain_send,
                all_gains.at[me],
                send.at[3, step - 1],
                recv.at[3, step - 1],
                axis,
                peer,
            )
        )
    copy = pltpu.make_async_copy(gain_send, all_gains.at[me], local.at[len(loads) + 3])
    copy.start()
    swaps.append(copy)
    two.finish()
    pairs.finish()
    for copy in swaps:
        copy.wait()


def attn_back(
    part,
    residual,
    cotangent,
    projected,
    tokens,
    gains,
    out_full,
    query_full,
    pair_full,
    attn_out,
    query_rot,
    key_all,
    value_all,
    queries,
    keys,
    cosine,
    sine,
    post_grad,
    axis,
    size,
    ident,
):
    rows, width = residual.shape
    bf16, f32 = jnp.bfloat16, jnp.float32
    whole = pl.BlockSpec(memory_space=pltpu.VMEM)
    away = pl.BlockSpec(memory_space=pl.ANY)
    qwidth, total_keys = query_full.shape[1], key_all.shape[0]
    query_cols = (size, rows, qwidth // size)
    pair_cols = (size, rows, 2 * HEAD // size)
    proj_cols = (size, rows, width // size)
    dma = pltpu.SemaphoreType.DMA
    return pl.pallas_call(
        functools.partial(attn_back_kernel, axis, size),
        out_shape=(
            jax.ShapeDtypeStruct((rows, width), f32),
            jax.ShapeDtypeStruct(query_cols, bf16),
            jax.ShapeDtypeStruct(pair_cols, bf16),
            jax.ShapeDtypeStruct(proj_cols, bf16),
            jax.ShapeDtypeStruct((size, 8, width), f32),
        ),
        in_specs=[away]
        + [whole] * 5
        + [away] * 3
        + [whole] * 2
        + [away] * 2
        + [whole] * 5,
        out_specs=(whole, away, away, away, away),
        scratch_shapes=[
            pltpu.VMEM(out_full.shape, bf16),
            pltpu.VMEM(query_full.shape, bf16),
            pltpu.VMEM(pair_full.shape, bf16),
            pltpu.VMEM(key_all.shape, bf16),
            pltpu.VMEM(value_all.shape, bf16),
            pltpu.VMEM((rows, width), f32),
            pltpu.VMEM((rows, width), bf16),
            pltpu.VMEM((HEADS * rows, total_keys), bf16),
            pltpu.VMEM((HEADS * rows, total_keys), bf16),
            pltpu.VMEM((HEADS * rows, HEAD), bf16),
            pltpu.VMEM((HEADS * rows, HEAD), bf16),
            pltpu.VMEM((size, rows, 2 * HEAD), bf16),
            pltpu.VMEM((rows, qwidth), bf16),
            pltpu.VMEM(query_cols, bf16),
            pltpu.VMEM(pair_cols, bf16),
            pltpu.VMEM(proj_cols, bf16),
            pltpu.VMEM((8, width), f32),
            dma((9,)),
            dma((4, size - 1)),
            dma((4, size - 1)),
        ]
        + scatter_scratch(size, rows, width)
        + scatter_scratch(size, rows, 2 * HEAD),
        compiler_params=pltpu.CompilerParams(collective_id=ident, has_side_effects=True),
        cost_estimate=pl.CostEstimate(
            flops=0, bytes_accessed=30 * part.size * 2, transcendentals=0
        ),
        name=f"attn_back_{ident}",
    )(
        part,
        residual,
        cotangent,
        projected,
        tokens,
        gains,
        out_full,
        query_full,
        pair_full,
        attn_out,
        query_rot,
        key_all,
        value_all,
        queries,
        keys,
        cosine,
        sine,
        post_grad,
    )


def attn_front_kernel(
    dp,
    ctx,
    tokens,
    query_in,
    pair_in,
    out_in,
    gains_in,
    cosine,
    sine,
    residual,
    projected,
    queries,
    keys,
    query_rot,
    attn_out,
    key_all,
    value_all,
    gains,
    normed_hbm,
    query_hbm,
    pair_hbm,
    out_hbm,
    rows_all,
    attn_all,
    tokens_all,
    normed_all,
    query_w,
    pair_w,
    out_w,
    keys_all,
    gains_all,
    normed_two,
    local,
    far_send,
    far_recv,
    near_send,
    near_recv,
    pass_send,
    pass_recv,
    *scratch,
):
    rows, width = tokens.shape
    total_keys = key_all.shape[0]
    bf16, f32 = jnp.bfloat16, jnp.float32
    scaling = 1.0 / math.sqrt(HEAD)
    place = Place("ctx", ctx)
    me, row = place.me, lax.axis_index("dp")
    shard = query_in.shape[0]
    query_width = query_w.shape[1] // ctx
    pair_depth, pair_width = pair_in.shape
    out_shard = out_in.shape[0]
    out_depth = out_shard // ctx

    def query_region(source, base, origin):
        return source.at[
            pl.ds(pl.multiple_of(base * shard, 16), shard),
            pl.ds(pl.multiple_of(origin * query_width, 128), query_width),
        ]

    def pair_region(base, origin):
        start = base * shard + lax.rem(origin, 2) * pair_depth
        return pair_w.at[
            pl.ds(pl.multiple_of(start, 16), pair_depth),
            pl.ds(pl.multiple_of((origin // 2) * pair_width, 128), pair_width),
        ]

    def out_region(source, base, origin):
        start = base * out_shard + origin * out_depth
        return source.at[pl.ds(pl.multiple_of(start, 16), out_depth)]

    regions = (
        pair_region,
        functools.partial(query_region, query_w),
        functools.partial(out_region, out_w),
    )
    sources = (pair_in, query_region(query_in, 0, me), out_region(out_in, 0, me))
    pending = []

    def stay(source, target, index):
        copy = pltpu.make_async_copy(source, target, local.at[index])
        copy.start()
        return copy

    own = [stay(sources[item], regions[item](row, me), item) for item in range(3)]
    own.append(stay(gains_in, gains_all.at[row], 3))
    barrier = pltpu.get_barrier_semaphore()
    for step in range(1, place.half):
        pl.semaphore_signal(
            barrier, inc=1, device_id={"ctx": place.across(step)}, device_id_type=MESH
        )
    pl.semaphore_signal(barrier, inc=1, device_id={"ctx": place.twin}, device_id_type=MESH)
    for step in range(1, dp):
        pl.semaphore_signal(
            barrier, inc=1, device_id={"dp": lax.rem(row + step, dp)}, device_id_type=MESH
        )
    pl.semaphore_wait(barrier, place.half + dp - 1)

    far, near = {}, {}
    for item in (3, 0, 1, 2):
        for step in range(1, dp):
            far[item, step] = remote(
                gains_in if item == 3 else sources[item],
                gains_all.at[row] if item == 3 else regions[item](row, me),
                far_send.at[item, step - 1],
                far_recv.at[item, step - 1],
                "dp",
                lax.rem(row + step, dp),
            )
    token_gather = Gather(place, tokens, tokens_all, scratch[:5])
    row_gather = Gather(place, normed_two, rows_all, scratch[5:10])
    attn_gather = Gather(place, attn_out, attn_all, scratch[10:15])
    for index in range(len(token_gather.spans)):
        token_gather.start(index)

    def spread(item, lag):
        base = lax.rem(row + dp - lag, dp)
        if lag:
            far[item, lag].wait_recv()
        source = regions[item](base, me) if lag else sources[item]
        target = regions[item](base, me)
        for step in range(1, place.half):
            near[item, lag, step] = remote(
                source,
                target,
                near_send.at[item, lag, step],
                near_recv.at[item, lag, step],
                "ctx",
                place.across(step),
            )
        pending.append(
            remote(
                source,
                target,
                pass_send.at[item, lag, 0],
                pass_recv.at[item, lag, 0],
                "ctx",
                place.twin,
            )
        )
        item_passes[item].append(pending[-1])

    def relay(item):
        for lag in range(dp):
            base = lax.rem(row + dp - lag, dp)
            for step in range(1, place.half):
                near[item, lag, step].wait_recv()
                block = regions[item](base, place.behind(step))
                pending.append(
                    remote(
                        block,
                        block,
                        pass_send.at[item, lag, step],
                        pass_recv.at[item, lag, step],
                        "ctx",
                        place.twin,
                    )
                )
                item_passes[item].append(pending[-1])

    def complete(item):
        for copy in item_passes[item]:
            copy.wait_recv()
        own[item].wait()

    item_passes = ([], [], [])
    for item in range(3):
        spread(item, 0)
    token_gather.relay()
    for lag in range(1, dp):
        spread(0, lag)
    for step in range(1, dp):
        far[3, step].wait_recv()
    own[3].wait()
    total = gains_all[0]
    for step in range(1, dp):
        total = total + gains_all[step]
    gains[...] = total
    token_gather.finish()

    def normalize(block, carry):
        value = tokens_all[block].astype(f32)
        normed_all[block] = (value * inverse_rms(value) * gains[0:1]).astype(bf16)
        return carry

    lax.fori_loop(0, ctx, normalize, 0)
    saves = [stay(normed_all, normed_hbm, 4)]
    for lag in range(1, dp):
        spread(1, lag)
    relay(0)
    for lag in range(1, dp):
        spread(2, lag)
    complete(0)
    saves.append(stay(pair_w, pair_hbm, 5))

    def project(block, carry):
        both = matmul(normed_all[block], pair_w[...])
        value = both[:, :HEAD]
        turn = pl.ds(pl.multiple_of(block * rows, rows), rows)
        keys_all[block] = value
        key_all[turn] = rotate(
            value * inverse_rms(value) * gains[4:5, HEAD : 2 * HEAD], cosine[turn], sine[turn]
        ).astype(bf16)
        value_all[turn] = both[:, HEAD:].astype(bf16)
        return carry

    lax.fori_loop(0, ctx, project, 0)
    keys[...] = keys_all[me]
    relay(1)
    complete(1)
    saves.append(stay(query_w, query_hbm, 6))
    queries[...] = matmul(normed_all[me], query_w[...])
    here = pl.ds(pl.multiple_of(me * rows, rows), rows)

    def attend(head, carry):
        lanes = pl.ds(pl.multiple_of(head * HEAD, HEAD), HEAD)
        query_pos = me * rows + lax.broadcasted_iota(jnp.int32, (rows, total_keys), 0)
        allowed = query_pos >= lax.broadcasted_iota(jnp.int32, (rows, total_keys), 1)
        value = queries[:, lanes]
        query = (
            rotate(value * inverse_rms(value) * gains[4:5, :HEAD], cosine[here], sine[here])
            * scaling
        ).astype(bf16)
        query_rot[:, lanes] = query
        scores = jnp.where(allowed, matmul_nt(query, key_all[...]), NEG_FILL)
        weights = jnp.where(
            allowed, jnp.exp(scores - jnp.max(scores, axis=-1, keepdims=True)), 0.0
        )
        attn_out[:, lanes] = (
            matmul(weights.astype(bf16), value_all[...]) / jnp.sum(weights, axis=-1, keepdims=True)
        ).astype(bf16)
        return carry

    lax.fori_loop(0, HEADS, attend, 0)
    relay(2)
    complete(2)
    saves.append(stay(out_w, out_hbm, 7))
    projected[...] = matmul(attn_out[...], out_w[...])
    for index, span in enumerate(row_gather.spans):
        ahead = projected[span]
        kept = tokens[span].astype(f32) + ahead * inverse_rms(ahead) * gains[1:2]
        residual[span] = kept
        normed_two[span] = (kept * inverse_rms(kept) * gains[2:3]).astype(bf16)
        row_gather.start(index)
    for index in range(len(attn_gather.spans)):
        attn_gather.start(index)
    row_gather.relay()
    attn_gather.relay()
    row_gather.finish()
    attn_gather.finish()
    for copy in list(far.values()) + list(near.values()) + pending:
        copy.wait_send()
    for copy in saves:
        copy.wait()


def attn_front(tokens, query_weight, pair, out_weight, gain_rows, cosine, sine, dp, ctx, ident):
    rows, width = tokens.shape
    shard, qwidth = query_weight.shape
    half = ctx // 2
    pair_depth, pair_width = shard // 2, pair.shape[1] // half
    index = lax.axis_index("ctx")
    pair_slice = lax.dynamic_slice(
        pair, (lax.rem(index, 2) * pair_depth, index // 2 * pair_width), (pair_depth, pair_width)
    )
    bf16, f32 = jnp.bfloat16, jnp.float32
    whole = pl.BlockSpec(memory_space=pltpu.VMEM)
    away = pl.BlockSpec(memory_space=pl.ANY)
    dma = pltpu.SemaphoreType.DMA
    vmem, shape = pltpu.VMEM, jax.ShapeDtypeStruct
    query_full, pair_full = (dp * shard, qwidth), (dp * shard, pair.shape[1])
    out_full = (dp * out_weight.shape[0], width)
    return pl.pallas_call(
        functools.partial(attn_front_kernel, dp, ctx),
        out_shape=(
            shape((rows, width), f32),
            shape((rows, width), f32),
            shape((rows, qwidth), f32),
            shape((rows, HEAD), f32),
            shape((rows, qwidth), bf16),
            shape((rows, qwidth), bf16),
            shape((ctx * rows, HEAD), bf16),
            shape((ctx * rows, HEAD), bf16),
            shape((8, width), f32),
            shape((ctx, rows, width), bf16),
            shape(query_full, bf16),
            shape(pair_full, bf16),
            shape(out_full, bf16),
            shape((ctx, rows, width), bf16),
            shape((ctx, rows, qwidth), bf16),
        ),
        in_specs=[whole, away, whole, away, whole, whole, whole],
        out_specs=(whole,) * 9 + (away,) * 6,
        scratch_shapes=[
            vmem((ctx, rows, width), bf16),
            vmem((ctx, rows, width), bf16),
            vmem(query_full, bf16),
            vmem(pair_full, bf16),
            vmem(out_full, bf16),
            vmem((ctx, rows, HEAD), f32),
            vmem((dp, 8, width), f32),
            vmem((rows, width), bf16),
            dma((8,)),
            dma((4, dp - 1)),
            dma((4, dp - 1)),
        ]
        + [dma((3, dp, half))] * 4
        + gather_scratch(ctx, rows) * 3,
        compiler_params=pltpu.CompilerParams(collective_id=ident, has_side_effects=True),
        cost_estimate=pl.CostEstimate(
            flops=0, bytes_accessed=100 * ctx * rows * width, transcendentals=0
        ),
        name=f"attn_front_{ident}",
    )(tokens, query_weight, pair_slice, out_weight, gain_rows, cosine, sine)


def fits_front(shard, qwidth, pair_width, out_shard, ctx):
    return (
        ctx % 2 == 0
        and qwidth % (128 * ctx) == 0
        and pair_width % (64 * ctx) == 0
        and shard % 32 == 0
        and out_shard % (16 * ctx) == 0
    )


def gain_block(gains, width):
    gain_in, gain_query, gain_key, gain_attn, gain_pre, gain_post = gains
    heads = jnp.concatenate([gain_query, gain_key])
    heads = jnp.pad(heads, (0, width - heads.shape[0]))
    stacked = jnp.stack([gain_in, gain_attn, gain_pre, gain_post, heads])
    return jnp.pad(stacked, ((0, 3), (0, 0)))


def spread_gain(gain, dp):
    place = jnp.arange(dp * gain.shape[0], dtype=jnp.int32) // gain.shape[0]
    tiled = jnp.tile(gain.astype(jnp.float32), dp)
    return jnp.where(place == lax.axis_index("dp"), tiled, 0.0)


def by_rows(array):
    return with_layout_constraint(array, Layout(major_to_minor=(0, 1)))


def by_columns(array, parts):
    rows, columns = array.shape
    return jnp.transpose(array.reshape(rows, parts, columns // parts), (1, 0, 2))


def from_columns(array):
    parts, rows, columns = array.shape
    return jnp.transpose(array, (1, 0, 2)).reshape(rows, parts * columns)


def sum_blocks(array):
    return jnp.sum(array.astype(jnp.float32), axis=0)


def plain_front(
    tokens, query_weight, pair, out_weight, raw_gains, cuts, cosine_all, sine_all, dp, ctx
):
    rows, width = tokens.shape
    bf16 = jnp.bfloat16
    scaling = 1.0 / math.sqrt(HEAD)
    ctx_index = lax.axis_index("ctx")
    query_pos = ctx_index * rows + jnp.arange(rows, dtype=jnp.int32)
    cosine = lax.dynamic_slice_in_dim(cosine_all, ctx_index * rows, rows, 0)
    sine = lax.dynamic_slice_in_dim(sine_all, ctx_index * rows, rows, 0)
    kwidth = pair.shape[1] // 2
    query_columns = query_weight.shape[1] // ctx
    pair_rows = pair.shape[0] // ctx
    out_rows = out_weight.shape[0] // ctx
    query_slice = lax.dynamic_slice_in_dim(query_weight, ctx_index * query_columns, query_columns, 1)
    pair_slice = lax.dynamic_slice_in_dim(pair, ctx_index * pair_rows, pair_rows, 0)
    out_slice = lax.dynamic_slice_in_dim(out_weight, ctx_index * out_rows, out_rows, 0)
    packed_gains = jnp.concatenate([gain.astype(jnp.float32) for gain in raw_gains])[None]
    query_dp, pair_dp, out_dp, gains_dp = exchange(
        (query_slice, pair_slice, out_slice, packed_gains), ("gather",) * 4, "dp", dp, 0
    )
    gains_dp = gains_dp[:, 0]
    gain_in, gain_query, gain_key, gain_attn, gain_pre, gain_post = (
        gains_dp[:, low:high].reshape(-1) for low, high in zip(cuts[:-1], cuts[1:])
    )
    query_all, pair_all, out_all, tokens_all = exchange(
        (query_dp.reshape(-1, query_columns), pair_dp, out_dp, tokens),
        ("gather",) * 4,
        "ctx",
        ctx,
        1,
    )
    query_full = from_columns(query_all)
    pair_full = jnp.transpose(pair_all, (1, 0, 2, 3)).reshape(-1, 2 * kwidth)
    key_full = pair_full[:, :kwidth]
    value_full = pair_full[:, kwidth:]
    out_full = jnp.transpose(out_all, (1, 0, 2, 3)).reshape(-1, out_weight.shape[1])

    inputs_f = tokens.astype(jnp.float32)
    inv_one = inverse_rms(inputs_f)
    normed_one = (inputs_f * inv_one * gain_in).astype(bf16)
    all_f = tokens_all.reshape(-1, width).astype(jnp.float32)
    normed_all = (all_f * inverse_rms(all_f) * gain_in).astype(bf16)
    key_pos = jnp.arange(all_f.shape[0], dtype=jnp.int32)
    queries = matmul(normed_one, query_full).reshape(rows, HEADS, HEAD)
    keys = matmul(normed_one, key_full)
    keys_every = matmul(normed_all, key_full)
    value_all = matmul(normed_all, value_full).astype(bf16)
    inv_query = inverse_rms(queries)
    inv_key = inverse_rms(keys)
    query_rot = (
        rotate(queries * inv_query * gain_query, cosine[:, None, :], sine[:, None, :]) * scaling
    ).astype(bf16)
    key_all = rotate(
        keys_every * inverse_rms(keys_every) * gain_key, cosine_all, sine_all
    ).astype(bf16)
    allowed = (query_pos[:, None] >= key_pos[None, :])[None]
    scores = jnp.einsum("qhd,kd->hqk", query_rot, key_all, preferred_element_type=jnp.float32)
    scores = jnp.where(allowed, scores, NEG_FILL)
    row_max = jnp.max(scores, axis=-1, keepdims=True)
    weights = jnp.where(allowed, jnp.exp(scores - row_max), 0.0)
    total = jnp.sum(weights, axis=-1, keepdims=True)
    accum = jnp.einsum(
        "hqk,kd->hqd", weights.astype(bf16), value_all, preferred_element_type=jnp.float32
    )
    attn_heads = jnp.transpose(accum / total, (1, 0, 2)).astype(bf16)
    attn_out = attn_heads.reshape(rows, HEADS * HEAD)
    projected = matmul(attn_out, out_full)
    inv_proj = inverse_rms(projected)
    residual = inputs_f + projected * inv_proj * gain_attn
    inv_two = inverse_rms(residual)
    normed_two = (residual * inv_two * gain_pre).astype(bf16)

    rows_all, attn_all = exchange((normed_two, attn_out), ("gather",) * 2, "ctx", ctx, 2)
    gains = gain_block(
        [gain_in, gain_query, gain_key, gain_attn, gain_pre, gains_dp[:, cuts[-2] :].reshape(-1)], width
    )
    return (
        residual,
        projected,
        queries.reshape(rows, HEADS * HEAD),
        keys,
        query_rot.reshape(rows, HEADS * HEAD),
        attn_out,
        key_all,
        value_all,
        gains,
        normed_all,
        query_full,
        pair_full,
        out_full,
        rows_all,
        attn_all,
    )


def on_device(
    dp,
    ctx,
    tokens,
    in_gain,
    query_weight,
    key_weight,
    value_weight,
    query_gain,
    key_gain,
    out_weight,
    attn_post_gain,
    ffn_pre_gain,
    gate_weight,
    up_weight,
    down_weight,
    ffn_post_gain,
    cotangent,
):
    rows, width = tokens.shape
    bf16 = jnp.bfloat16
    qwidth = query_weight.shape[1]
    kwidth = key_weight.shape[1]
    out_columns = out_weight.shape[1] // ctx
    query_columns = qwidth // ctx
    pair = jnp.concatenate([key_weight, value_weight], axis=1)
    raw_gains = (in_gain, query_gain, key_gain, attn_post_gain, ffn_pre_gain, ffn_post_gain)
    cuts = [0]
    for gain in raw_gains:
        cuts.append(cuts[-1] + gain.shape[0])
    key_pos = jnp.arange(ctx * rows, dtype=jnp.int32)
    cosine_all, sine_all = rope_tables(key_pos.astype(jnp.float32))
    gate_full, up_full, down_full = (
        lax.all_gather(gate_weight, "dp", axis=0, tiled=True),
        lax.all_gather(up_weight, "dp", axis=0, tiled=True),
        lax.all_gather(down_weight, "dp", axis=0, tiled=True),
    )
    if fits_front(query_weight.shape[0], qwidth, 2 * kwidth, out_weight.shape[0], ctx):
        gain_rows = gain_block([spread_gain(gain, dp) for gain in raw_gains], width)
        (
            residual,
            projected,
            queries,
            keys,
            query_rot,
            attn_out,
            key_all,
            value_all,
            gains,
            normed_all,
            query_full,
            pair_full,
            out_full,
            rows_all,
            attn_all,
        ) = attn_front(
            tokens, query_weight, pair, out_weight, gain_rows, cosine_all, sine_all, dp, ctx, 10
        )
    else:
        (
            residual,
            projected,
            queries,
            keys,
            query_rot,
            attn_out,
            key_all,
            value_all,
            gains,
            normed_all,
            query_full,
            pair_full,
            out_full,
            rows_all,
            attn_all,
        ) = plain_front(
            tokens, query_weight, pair, out_weight, raw_gains, cuts, cosine_all, sine_all, dp, ctx
        )
    normed_all = normed_all.reshape(-1, width)
    attn_all = attn_all.reshape(-1, qwidth)
    rows_all = rows_all.reshape(-1, width)
    gate = matmul(rows_all, gate_full)
    upper = matmul(rows_all, up_full)
    gelu_val, gelu_der = gelu_pair(gate)
    hidden = (gelu_val * upper).astype(bf16)
    ffn_part = matmul_nt(hidden, down_full).astype(bf16).reshape(ctx, rows, width)
    block_out, grad_post, grad_all = ffn_turn(
        ffn_part, residual, cotangent, gains[3:4], "ctx", ctx, 3
    )
    grad_all = grad_all.reshape(-1, width)
    down_part, grad_all = lax.optimization_barrier(
        (by_rows(matmul_tn(grad_all, hidden).astype(bf16)), grad_all)
    )
    down_shard = lax.psum_scatter(down_part, "dp", scatter_dimension=0, tiled=True)
    down_shard = down_shard.astype(jnp.float32)
    hidden_grad = matmul(grad_all, down_full)
    gate_grad = (hidden_grad * upper * gelu_der).astype(bf16)
    up_grad = (hidden_grad * gelu_val).astype(bf16)
    gate_part = by_rows(matmul_tn(rows_all, gate_grad).astype(bf16))
    up_part = by_rows(matmul_tn(rows_all, up_grad).astype(bf16))
    gate_shard = lax.psum_scatter(gate_part, "dp", scatter_dimension=0, tiled=True)
    gate_shard = gate_shard.astype(jnp.float32)
    two_part = (matmul_nt(gate_grad, gate_full) + matmul_nt(up_grad, up_full)).astype(bf16)
    two_part, up_part = lax.optimization_barrier((two_part, up_part))
    input_grad, query_cols, pair_cols, proj_cols, all_gains = attn_back(
        two_part.reshape(ctx, rows, width),
        residual,
        cotangent,
        projected,
        tokens,
        gains,
        out_full,
        query_full,
        pair_full,
        attn_out,
        query_rot,
        key_all,
        value_all,
        queries,
        keys,
        cosine_all,
        sine_all,
        grad_post,
        "ctx",
        ctx,
        5,
    )
    gain_sums = jnp.sum(all_gains, axis=0)
    gain_grads = (
        gain_sums[0],
        gain_sums[4, :HEAD],
        gain_sums[5, :HEAD],
        gain_sums[1],
        gain_sums[2],
        gain_sums[3],
    )
    packed = jnp.concatenate([grad.reshape(dp, -1) for grad in gain_grads], axis=1)
    query_w = matmul_tn(normed_all, query_cols.reshape(-1, query_columns)).astype(bf16)
    pair_w = matmul_tn(normed_all, pair_cols.reshape(normed_all.shape[0], -1)).astype(bf16)
    out_w = matmul_tn(attn_all, proj_cols.reshape(-1, out_columns)).astype(bf16)
    query_w, pair_w, out_w, gain_parts = exchange(
        (
            query_w.reshape(dp, -1, query_columns),
            pair_w.reshape(dp, -1, pair_w.shape[1]),
            out_w.reshape(dp, -1, out_columns),
            packed[:, None],
        ),
        ("swap",) * 4,
        "dp",
        dp,
        8,
    )
    up_part, query_w, pair_w, out_w = lax.optimization_barrier((up_part, query_w, pair_w, out_w))
    up_shard = lax.psum_scatter(up_part, "dp", scatter_dimension=0, tiled=True)
    up_shard = up_shard.astype(jnp.float32)
    query_w, pair_w, out_w = exchange(
        (sum_blocks(query_w).astype(bf16), sum_blocks(pair_w).astype(bf16), sum_blocks(out_w).astype(bf16)),
        ("gather",) * 3,
        "ctx",
        ctx,
        9,
    )
    query_w = from_columns(query_w).astype(jnp.float32)
    pair_w = from_columns(pair_w).astype(jnp.float32)
    out_w = from_columns(out_w).astype(jnp.float32)
    gain_done = sum_blocks(gain_parts).reshape(-1)
    share = [gain_done[low:high] for low, high in zip(cuts[:-1], cuts[1:])]
    return (
        block_out,
        input_grad,
        share[0],
        query_w,
        pair_w[:, :kwidth],
        pair_w[:, kwidth:],
        share[1],
        share[2],
        out_w,
        share[3],
        share[4],
        gate_shard,
        up_shard,
        down_shard,
        share[5],
    )


def solution(mesh):
    return jax.shard_map(
        functools.partial(on_device, mesh.shape["dp"], mesh.shape["ctx"]),
        mesh=mesh,
        in_specs=(
            P(("dp", "ctx"), None),
            P("dp"),
            P("dp", None),
            P("dp", None),
            P("dp", None),
            P("dp"),
            P("dp"),
            P("dp", None),
            P("dp"),
            P("dp"),
            P("dp", "ctx"),
            P("dp", "ctx"),
            P("dp", "ctx"),
            P("dp"),
            P(("dp", "ctx"), None),
        ),
        out_specs=(
            P(("dp", "ctx"), None),
            P(("dp", "ctx"), None),
            P("dp"),
            P("dp", None),
            P("dp", None),
            P("dp", None),
            P("dp"),
            P("dp"),
            P("dp", None),
            P("dp"),
            P("dp"),
            P("dp", "ctx"),
            P("dp", "ctx"),
            P("dp", "ctx"),
            P("dp"),
        ),
        check_vma=False,
    )
```
